256 devices in a mesh: frag: 32 (over x, z), basis: 8 (over y, core).
Axes of the slice: x: 4, y: 4, z: 8, core: 2. Of those that a mesh axis runs over, the one named last changes fastest.
Arguments:
- density: bfloat16 [1024, 256, 256], P('frag', 'basis'), as said below
- aux_factor: bfloat16 [1024, 256, 1024], P('frag', None, 'basis')
- pairs: int32 [1024, 2], P(('frag', 'basis')), may hold values from 0 to 1023, as said below
- slot_of: int32 [1024], replicated, may hold values from 0 to 1023, as said below
- costs: int32 [1024], P(('frag', 'basis')), may hold values from 1 to 5
Outputs:
- density_shift: float32 [1024, 256, 256], P('frag', 'basis')
- embedding: float32 [1024, 1024], P('frag', 'basis')
The draws below stay inside these ranges and needn't reach their ends.
Inputs may be any that keep to these rules, and one draw needn't show every extreme that they name: Each density[s] is symmetric. A permutation: slot_of[f] is the storage slot of fragment f, and a slot s lies on index s // 32 of frag. The two fragments of a dimer differ. The rows of pairs on one index of frag hold 64 fragment references; at most 3 of them name fragments stored on any one index of frag, and in every draw some index of frag stores exactly 3 of them.
All inputs are finite; a program needn't handle non-finite values.
Results may differ from the reference program's by a relative error of at most 0.015.
Values may be sent and summed in bfloat16 or wider, within the bound.
No kernel may reach another device: no remote copies, remote signals or barrier semaphores. Data moves between devices by JAX's collectives and lax.ppermute only.
A program may use at most 64 MiB of HBM per device.

```python
import jax
import jax.numpy as jnp
from jax import lax

NB = 256
NAUX = 1024
FRAG_DEV = 32
DIM_DEV = 4
ITERS = 5
FRAGS = 1024
DIMERS = 1024


def pair_layout(key):
    n_frag = FRAGS // FRAG_DEV
    refs_col = 2 * DIMERS // n_frag
    capacity = 3 * DIMERS // (n_frag * n_frag)
    pool_size = n_frag * capacity
    key_perm = jax.random.fold_in(key, 11)
    key_cols = jax.random.fold_in(key, 12)
    slot_of = jax.random.permutation(key_perm, FRAGS).astype(jnp.int32)
    ids_of_slot = jnp.argsort(slot_of).astype(jnp.int32)
    owners_pool = jnp.repeat(jnp.arange(n_frag, dtype=jnp.int32), capacity)

    def column(col_key):
        key_one, key_two, key_three, key_four = jax.random.split(col_key, 4)
        chosen = jax.random.randint(key_one, (), 0, n_frag)
        raw_score = jax.random.randint(key_two, (pool_size,), 0, 65536)
        score = raw_score * pool_size + jnp.arange(pool_size, dtype=jnp.int32)
        score = score + jnp.where(owners_pool == chosen, 268435456, 0)
        picked = jnp.argsort(-score)[:refs_col]
        owners = owners_pool[picked]
        owners = owners[jax.random.permutation(key_three, refs_col)]
        local = jax.random.randint(key_four, (refs_col,), 0, FRAG_DEV).reshape(-1, 2)
        owner_pairs = owners.reshape(-1, 2)
        clash = (owner_pairs[:, 0] == owner_pairs[:, 1]) & (local[:, 0] == local[:, 1])
        second_local = jnp.where(clash, (local[:, 1] + 1) % FRAG_DEV, local[:, 1])
        local = jnp.stack([local[:, 0], second_local], axis=1).reshape(-1)
        return owners * FRAG_DEV + local
    slots = jax.vmap(column)(jax.random.split(key_cols, n_frag))
    fragment_ids = ids_of_slot[slots.reshape(-1)].reshape(DIMERS, 2)
    return (slot_of, fragment_ids.astype(jnp.int32))


def draw_pairs(key, part):
    return pair_layout(key)[1]


def draw_slot_of(key, part):
    return pair_layout(key)[0]


def draw_costs(key, part):
    key_busy = jax.random.fold_in(key, 21)
    key_heavy = jax.random.fold_in(key, 22)
    devices = DIMERS // DIM_DEV
    busy = jax.random.randint(key_busy, (devices, 1), 0, 4) == 0
    heavy = jax.random.randint(key_heavy, (devices, DIM_DEV), ITERS - 1, ITERS + 1)
    light = jnp.ones((devices, DIM_DEV), jnp.int32)
    steps = jnp.where(busy, heavy, light).reshape(-1)
    steps = steps.at[0].set(ITERS)
    return steps.astype(jnp.int32)


def draw_density(key, part):
    shape = (FRAGS, NB, NB)
    raw_values = jax.random.normal(key, shape, jnp.float32)
    symmetric = (raw_values + jnp.swapaxes(raw_values, 1, 2)) * (0.009 * 0.70710678)
    return symmetric.astype(jnp.bfloat16)


def draw_aux_factor(key, part):
    shape = (FRAGS, NB, NAUX)
    spread = 4.0 / jnp.sqrt(jnp.float32(NB))
    raw_values = jax.random.truncated_normal(key, -4.0, 4.0, shape, jnp.float32)
    return (raw_values * spread).astype(jnp.bfloat16)


def setup_inputs(seed: int = 0) -> dict:
    key_list = jax.random.split(jax.random.key(seed), 6)
    return {
        "density": draw_density(jax.random.fold_in(key_list[5], 71), 0),
        "aux_factor": draw_aux_factor(jax.random.fold_in(key_list[5], 71), 0),
        "pairs": draw_pairs(jax.random.fold_in(key_list[5], 71), 0),
        "slot_of": draw_slot_of(jax.random.fold_in(key_list[5], 71), 0),
        "costs": draw_costs(jax.random.fold_in(key_list[5], 71), 0),
    }


COUPLE = 0.015625


def fit_block(block, factor):
    projected = jnp.dot(block, factor, preferred_element_type=jnp.float32)
    return jnp.sum(factor.astype(jnp.float32) * projected, axis=0).astype(jnp.bfloat16)


def purify_step(index, current):
    square = jnp.dot(current, current, preferred_element_type=jnp.float32)
    cube_term = jnp.dot(square.astype(jnp.bfloat16), current, preferred_element_type=jnp.float32)
    return (3.0 * square - 2.0 * cube_term).astype(jnp.bfloat16)


def reference(density, aux_factor, pairs, slot_of, costs):
    fitted = lax.map(lambda item: fit_block(item[0], item[1]), (density, aux_factor))
    slots = slot_of[pairs].astype(jnp.int32)
    whole_eye = jnp.eye(2 * NB, dtype=jnp.float32)
    half_eye = 0.5 * jnp.eye(NB, dtype=jnp.float32)

    def visit(carry, item):
        shift, embed = carry
        pair_slots, steps = item
        first = pair_slots[0]
        second = pair_slots[1]
        rows_first = density[first].astype(jnp.float32)
        rows_second = density[second].astype(jnp.float32)
        stacked = jnp.concatenate([aux_factor[first], aux_factor[second]], axis=0)
        coeff = fitted[first].astype(jnp.float32) + fitted[second].astype(jnp.float32)
        weighted = (stacked.astype(jnp.float32) * coeff[None, :]).astype(jnp.bfloat16)
        coulomb = jnp.dot(weighted, stacked.T, preferred_element_type=jnp.float32)
        zero_block = jnp.zeros((NB, NB), jnp.float32)
        blocks = jnp.block([[rows_first, zero_block], [zero_block, rows_second]])
        start = (0.5 * whole_eye + blocks + COUPLE * coulomb).astype(jnp.bfloat16)
        final = lax.fori_loop(0, steps, purify_step, start).astype(jnp.float32)
        change_first = final[:NB, :NB] - rows_first - half_eye
        change_second = final[NB:, NB:] - rows_second - half_eye
        shift = shift.at[first].add(change_first)
        shift = shift.at[second].add(change_second)
        embed = embed.at[first].add(fitted[second].astype(jnp.float32))
        embed = embed.at[second].add(fitted[first].astype(jnp.float32))
        return (shift, embed), None

    start_carry = (jnp.zeros((FRAGS, NB, NB), jnp.float32), jnp.zeros((FRAGS, NAUX), jnp.float32))
    (shift, embed), unused = lax.scan(visit, start_carry, (slots, costs))
    return shift, embed
```

```python
import functools

import jax
import jax.numpy as jnp
from jax import lax
from jax.experimental import pallas as pl
from jax.experimental.pallas import tpu as pltpu
from jax.sharding import PartitionSpec as P

COUPLE = 0.015625
BIG = 1 << 30
BF16 = jnp.bfloat16
F32 = jnp.float32
LOAD2 = 16

VMEM = pl.BlockSpec(memory_space=pltpu.VMEM)
SMEM = pl.BlockSpec(memory_space=pltpu.SMEM)


def copy_home(out_ref, row, aux_ref, den_ref, slot):
    out_ref[row, 0:256, :] = aux_ref[slot]
    block = den_ref[slot]
    out_ref[row, 256:288, :] = block[:, 0:128]
    out_ref[row, 288:320, :] = block[:, 128:256]


def pack_home(aux, den, index, outs):
    rows = index.shape[0] // outs

    def kernel(index_ref, aux_ref, den_ref, *out_refs):
        for n, out_ref in enumerate(out_refs):
            def step(row, unused, n=n, out_ref=out_ref):
                copy_home(out_ref, row, aux_ref, den_ref, index_ref[n * rows + row])
                return unused
            lax.fori_loop(0, rows, step, 0)

    shape = jax.ShapeDtypeStruct((rows, 320, 128), BF16)
    return pl.pallas_call(
        kernel,
        out_shape=[shape] * outs,
        in_specs=[SMEM, VMEM, VMEM],
        out_specs=[VMEM] * outs,
        name="pack_home",
    )(index, aux, den)


def pack_items(items, index, outs):
    rows = index.shape[0] // outs

    def kernel(index_ref, items_ref, *out_refs):
        for n, out_ref in enumerate(out_refs):
            for row in range(rows):
                out_ref[row] = items_ref[index_ref[n * rows + row]]

    shape = jax.ShapeDtypeStruct((rows,) + items.shape[1:], BF16)
    return pl.pallas_call(
        kernel,
        out_shape=[shape] * outs,
        in_specs=[SMEM, VMEM],
        out_specs=[VMEM] * outs,
        name="pack_items",
    )(index, items)


def pack_mixed(aux, den, items, index, outs):
    rows = index.shape[0] // outs

    def kernel(index_ref, aux_ref, den_ref, items_ref, *out_refs):
        for n, out_ref in enumerate(out_refs):
            def step(row, unused, n=n, out_ref=out_ref):
                at = index_ref[n * rows + row]

                @pl.when(at < 32)
                def _():
                    copy_home(out_ref, row, aux_ref, den_ref, at)

                @pl.when(at >= 32)
                def _():
                    out_ref[row] = items_ref[at - 32]

                return unused
            lax.fori_loop(0, rows, step, 0)

    shape = jax.ShapeDtypeStruct((rows, 320, 128), BF16)
    return pl.pallas_call(
        kernel,
        out_shape=[shape] * outs,
        in_specs=[SMEM, VMEM, VMEM, VMEM],
        out_specs=[VMEM] * outs,
        name="pack_mixed",
    )(index, aux, den, items)


def place_items(parts, target, rows):
    def kernel(target_ref, *refs):
        out_ref = refs[-1]
        for n, part_ref in enumerate(refs[:-1]):
            def step(row, unused, n=n, part_ref=part_ref):
                at = target_ref[n * rows + row]

                @pl.when(at >= 0)
                def _():
                    out_ref[at] = part_ref[row]

                return unused
            lax.fori_loop(0, rows, step, 0)

    return pl.pallas_call(
        kernel,
        out_shape=jax.ShapeDtypeStruct((32, 72, 128), BF16),
        in_specs=[SMEM] + [VMEM] * len(parts),
        out_specs=VMEM,
        name="place_items",
    )(target, *parts)


def dimer_kernel(steps_ref, me_ref, *refs):
    first, second, outs = refs[0:8], refs[8:16], refs[16:24]
    stacked, weighted, dens, current, squares = refs[24:]
    steps = steps_ref[pl.program_id(0)]
    me = me_ref[0]

    @pl.when(steps > 0)
    def _():
        for n in range(8):
            lanes = slice(n * 128, n * 128 + 128)
            at = pl.multiple_of(lax.bitwise_xor(me, n) * 32, 32)
            for half, part in ((0, first[n]), (256, second[n])):
                stacked[half : half + 256, lanes] = part[0, 0:256, :]
                dens[pl.ds(half + at, 32), 0:128] = part[0, 256:288, :]
                dens[pl.ds(half + at, 32), 128:256] = part[0, 288:320, :]
        fits = []
        for half in (0, 256):
            block = dens[half : half + 256, :]
            sums = []
            for n in range(4):
                lanes = slice(n * 256, n * 256 + 256)
                factor = stacked[half : half + 256, lanes]
                projected = jnp.dot(block, factor, preferred_element_type=F32)
                sums.append(jnp.sum(factor.astype(F32) * projected, axis=0, keepdims=True))
            fits.append(jnp.concatenate(sums, axis=1).astype(BF16).astype(F32))
        coeff = fits[0] + fits[1]
        for n in range(8):
            rows = slice(n * 64, n * 64 + 64)
            weighted[rows, :] = (stacked[rows, :].astype(F32) * coeff).astype(BF16)
        for n in range(4):
            rows = slice(n * 128, n * 128 + 128)
            coulomb = lax.dot_general(
                weighted[rows, :], stacked[...], (((1,), (1,)), ((), ())), preferred_element_type=F32
            )
            row_at = lax.broadcasted_iota(jnp.int32, (128, 512), 0) + n * 128
            col_at = lax.broadcasted_iota(jnp.int32, (128, 512), 1)
            own = dens[rows, :].astype(F32)
            blank = jnp.zeros((128, 256), F32)
            wide = jnp.concatenate([own, blank] if n < 2 else [blank, own], axis=1)
            eye = jnp.where(row_at == col_at, 0.5, 0.0)
            current[rows, :] = (eye + wide + COUPLE * coulomb).astype(BF16)

        def purify(index, unused):
            for n in range(4):
                rows = slice(n * 128, n * 128 + 128)
                square = jnp.dot(current[rows, :], current[...], preferred_element_type=F32)
                cube = jnp.dot(square.astype(BF16), current[...], preferred_element_type=F32)
                squares[rows, :] = (3.0 * square - 2.0 * cube).astype(BF16)
            current[...] = squares[...]
            return unused

        lax.fori_loop(0, steps, purify, 0)
        row_at = lax.broadcasted_iota(jnp.int32, (256, 256), 0)
        col_at = lax.broadcasted_iota(jnp.int32, (256, 256), 1)
        eye = jnp.where(row_at == col_at, 0.5, 0.0)
        for half in (0, 256):
            own = slice(half, half + 256)
            change = current[own, own].astype(F32) - dens[own, :].astype(F32) - eye
            dens[own, :] = change.astype(BF16)
        for n in range(8):
            at = pl.multiple_of(lax.bitwise_xor(me, n) * 32, 32)
            lanes = slice(n * 128, n * 128 + 128)
            for r in range(2):
                change = dens[pl.ds(r * 256 + at, 32), :]
                outs[n][r, 0:32, :] = change[:, 0:128]
                outs[n][r, 32:64, :] = change[:, 128:256]
                partner = jnp.broadcast_to(fits[1 - r][:, lanes], (8, 128))
                outs[n][r, 64:72, :] = partner.astype(BF16)


def run_dimers(steps, me, first, second, first_map, second_map):
    count = steps.shape[0]
    shape = jax.ShapeDtypeStruct((2 * count, 72, 128), BF16)
    return pl.pallas_call(
        dimer_kernel,
        out_shape=[shape] * 8,
        grid_spec=pltpu.PrefetchScalarGridSpec(
            num_scalar_prefetch=2,
            grid=(count,),
            in_specs=[pl.BlockSpec((1, 320, 128), first_map)] * 8
            + [pl.BlockSpec((1, 320, 128), second_map)] * 8,
            out_specs=[pl.BlockSpec((2, 72, 128), lambda i, *_: (i, 0, 0))] * 8,
            scratch_shapes=[
                pltpu.VMEM((512, 1024), BF16),
                pltpu.VMEM((512, 1024), BF16),
                pltpu.VMEM((512, 256), BF16),
                pltpu.VMEM((512, 512), BF16),
                pltpu.VMEM((512, 512), BF16),
            ],
        ),
        name="dimers",
        cost_estimate=pl.CostEstimate(
            flops=count * 4_000_000_000, bytes_accessed=count * 1_500_000, transcendentals=0
        ),
    )(steps, me, *first, *second)


def plan_kernel(me_ref, a_ref, b_ref, cost_ref, flag_ref, send_ref, pos_ref, steps_ref, left_ref, taken, load):
    me = me_ref[0]

    def clear(n, unused):
        taken[n] = 0
        load[n] = 0
        send_ref[n] = -1
        pos_ref[n] = 0
        return unused

    def clear_steps(n, unused):
        steps_ref[n] = 0
        return unused

    lax.fori_loop(0, 32, clear, 0)
    lax.fori_loop(0, LOAD2, clear_steps, 0)

    def visit(d, unused):
        left_ref[d] = 0

        @pl.when(flag_ref[d] > 0)
        def _():
            a, b = a_ref[d], b_ref[d]
            oa, ob = lax.shift_right_logical(a, 5), lax.shift_right_logical(b, 5)
            la, lb = a & 31, b & 31
            bit_a, bit_b = lax.shift_left(1, oa), lax.shift_left(1, ob)
            both = bit_a | bit_b
            free_a = ((taken[oa] & bit_b) == 0) & (load[oa] < LOAD2)
            free_b = ((taken[ob] & bit_a) == 0) & (load[ob] < LOAD2)
            inside = oa == ob
            use_a = free_a & (jnp.logical_not(free_b) | (load[oa] <= load[ob]))
            direct = jnp.where(use_a, oa, jnp.where(free_b, ob, -1))
            direct = jnp.where(inside, jnp.where(load[oa] < LOAD2, oa, -1), direct)

            def look(carry):
                n, found = carry
                c = (d + n) & 31
                good = ((taken[c] & both) == 0) & (load[c] < LOAD2) & (c != oa) & (c != ob)
                return n + 1, jnp.where(good, c, -1)

            start = jnp.where((direct >= 0) | inside, 32, 0)
            unused_n, c = lax.while_loop(
                lambda carry: (carry[0] < 32) & (carry[1] < 0), look, (start, direct)
            )

            @pl.when(c < 0)
            def _():
                left_ref[d] = 1

            @pl.when(c >= 0)
            def _():
                away = jnp.where(c == oa, 0, bit_a) | jnp.where(c == ob, 0, bit_b)
                taken[c] = taken[c] | away
                at = load[c]
                load[c] = at + 1

                @pl.when(c == me)
                def _():
                    pos_ref[2 * at] = jnp.where(c == oa, la, 32 + oa)
                    pos_ref[2 * at + 1] = jnp.where(c == ob, lb, 32 + ob)
                    steps_ref[at] = cost_ref[d]

                @pl.when((c != me) & (oa == me))
                def _():
                    send_ref[c] = la

                @pl.when((c != me) & (ob == me))
                def _():
                    send_ref[c] = lb

        return unused

    lax.fori_loop(0, a_ref.shape[0], visit, 0)


def plan_rest(me, a, b, cost, flag):
    s32 = jnp.int32
    return pl.pallas_call(
        plan_kernel,
        out_shape=[
            jax.ShapeDtypeStruct((32,), s32),
            jax.ShapeDtypeStruct((2 * LOAD2,), s32),
            jax.ShapeDtypeStruct((LOAD2,), s32),
            jax.ShapeDtypeStruct(a.shape, s32),
        ],
        in_specs=[SMEM] * 5,
        out_specs=[SMEM] * 4,
        scratch_shapes=[pltpu.SMEM((32,), s32), pltpu.SMEM((32,), s32)],
        name="plan",
        cost_estimate=pl.CostEstimate(flops=1000, bytes_accessed=30_000_000, transcendentals=0),
    )(me, a, b, cost, flag)


def add_up(dens, emb, lists, parts):
    counts = [part.shape[0] for part in parts]

    def kernel(*refs):
        n_parts = len(parts)
        slot_refs, part_refs = refs[:n_parts], refs[n_parts : 2 * n_parts]
        dens_in, emb_in, dens_ref, emb_ref = refs[2 * n_parts :]
        dens_ref[...] = dens_in[...]
        emb_ref[...] = emb_in[...]
        for slot_ref, part_ref, count in zip(slot_refs, part_refs, counts, strict=True):
            def step(row, unused, slot_ref=slot_ref, part_ref=part_ref):
                slot = slot_ref[row]

                @pl.when(slot >= 0)
                def _():
                    dens_ref[slot, :, 0:128] += part_ref[row, 0:32, :].astype(F32)
                    dens_ref[slot, :, 128:256] += part_ref[row, 32:64, :].astype(F32)
                    emb_ref[pl.ds(slot, 1), :] += part_ref[row, 64:72, :].astype(F32)[0:1, :]

                return unused
            lax.fori_loop(0, count, step, 0)

    n = len(parts)
    return pl.pallas_call(
        kernel,
        out_shape=[jax.ShapeDtypeStruct(dens.shape, F32), jax.ShapeDtypeStruct(emb.shape, F32)],
        in_specs=[SMEM] * n + [VMEM] * (n + 2),
        out_specs=[VMEM, VMEM],
        input_output_aliases={2 * n: 0, 2 * n + 1: 1},
        name="add_up",
    )(*lists, *parts, dens, emb)


def exchange(parts):
    got = [parts[0]]
    for k in range(1, 8):
        got.append(lax.ppermute(parts[k], "basis", [(i, i ^ k) for i in range(8)]))
    return got


def shards(density, aux_factor, pairs, slot_of, costs):
    n_frag = lax.axis_size("frag")
    n_basis = lax.axis_size("basis")
    me_frag = lax.axis_index("frag").astype(jnp.int32)
    me_basis = lax.axis_index("basis").astype(jnp.int32)
    dimers = pairs.shape[0] * n_frag * n_basis

    lookup = pairs[:, :, None] == jnp.arange(slot_of.shape[0], dtype=jnp.int32)
    slots = jnp.sum(jnp.where(lookup, slot_of, 0), axis=2)
    mine = jnp.concatenate([slots[:, 0], slots[:, 1], costs, jnp.zeros(116, jnp.int32)])
    column = lax.all_to_all(
        jnp.broadcast_to(mine, (n_basis, 1, 128)), "basis", split_axis=0, concat_axis=0, tiled=True
    )
    column = column[:, 0, 0:12].reshape(n_basis, 3, 4).transpose(1, 0, 2).reshape(96)
    column = jnp.concatenate([column, jnp.zeros(32, jnp.int32)])
    every = lax.all_to_all(
        jnp.broadcast_to(column, (n_frag, 1, 128)), "frag", split_axis=0, concat_axis=0, tiled=True
    )
    a = every[:, 0, 0:32].reshape(dimers)
    b = every[:, 0, 32:64].reshape(dimers)
    cost = every[:, 0, 64:96].reshape(dimers)

    order = jnp.arange(dimers, dtype=jnp.int32)
    columns = jnp.arange(n_frag, dtype=jnp.int32)
    own_a, own_b = a // 32, b // 32
    low, high = jnp.minimum(own_a, own_b), jnp.maximum(own_a, own_b)
    pair_id = low * 32 + high
    inside = own_a == own_b
    mine_a = (own_a == me_frag) & jnp.logical_not(inside)
    mine_b = (own_b == me_frag) & jnp.logical_not(inside)
    other = jnp.where(mine_a, own_b, jnp.where(mine_b, own_a, -1))
    local = jnp.where(mine_a, a, b) & 31
    key = order * 256 + local * 8 + cost
    xor_devices = lax.bitwise_xor(me_basis, jnp.arange(8, dtype=jnp.int32))
    served = (jnp.arange(4, dtype=jnp.int32)[None, :] * 8 + xor_devices[:, None]).reshape(32)
    served_hot = served[:, None] == columns[None, :]
    entries = (jnp.arange(2, dtype=jnp.int32)[None, :] * 8 + xor_devices[:, None]).reshape(16)
    entry_hot = entries[:, None] == jnp.arange(LOAD2, dtype=jnp.int32)[None, :]
    me_f, me_b = me_frag.reshape(1), me_basis.reshape(1)
    keep_first = (me_frag < columns) == ((me_frag + columns) % 2 == 0)

    def pick(hot, table):
        return jnp.sum(jnp.where(hot, table[None, :], 0), axis=1)

    def one_round(carry):
        unused_n, rest, dens, emb = carry
        open_dimer = rest > 0
        match = (other[None, :] == columns[:, None]) & open_dimer[None, :]
        keyed = jnp.where(match, key[None, :], BIG)
        key_0 = jnp.min(keyed, axis=1)
        key_1 = jnp.min(jnp.where(keyed > key_0[:, None], keyed, BIG), axis=1)
        here = jnp.where(keep_first, key_0, key_1)
        there = jnp.where(keep_first, key_1, key_0)
        send_1 = jnp.where(there < BIG, (there >> 3) & 31, -1)
        base_1 = jnp.where(here < BIG, (here >> 3) & 31, -1)
        steps_1 = jnp.where(here < BIG, here & 7, 0)

        (out_1,) = pack_home(aux_factor, density, jnp.maximum(send_1, 0), 1)
        in_1 = lax.all_to_all(out_1, "frag", split_axis=0, concat_axis=0, tiled=True)

        earlier = (pair_id[:, None] == pair_id[None, :]) & (order[None, :] < order[:, None])
        earlier = jnp.sum(jnp.where(earlier & open_dimer[None, :], 1, 0), axis=1)
        flag = jnp.where(open_dimer & ((earlier >= 2) | inside), 1, 0)
        send_2, pos_2, cost_2, left = plan_rest(me_f, a, b, cost, flag)

        base_at = pick(served_hot, base_1)
        home_1 = exchange(pack_home(aux_factor, density, jnp.maximum(base_at, 0), 8))

        (out_2,) = pack_home(aux_factor, density, jnp.maximum(send_2, 0), 1)
        out_2, in_1, home_1 = lax.optimization_barrier((out_2, in_1, home_1))
        in_2 = lax.all_to_all(out_2, "frag", split_axis=0, concat_axis=0, tiled=True)

        away_1 = exchange(pack_items(in_1, served, 8))
        my_steps_1 = jnp.sum(
            jnp.where(me_basis == jnp.arange(8, dtype=jnp.int32), steps_1.reshape(4, 8), 0), axis=1
        )
        same = lambda i, *_: (i, 0, 0)
        done_1 = exchange(run_dimers(my_steps_1, me_b, home_1, away_1, same, same))

        pos_at = jnp.stack([pick(entry_hot, pos_2[0::2]), pick(entry_hot, pos_2[1::2])], axis=1).reshape(32)
        both_2 = exchange(pack_mixed(aux_factor, density, in_2, pos_at, 8))
        my_steps_2 = jnp.sum(
            jnp.where(me_basis == jnp.arange(8, dtype=jnp.int32), cost_2.reshape(2, 8), 0), axis=1
        )
        done_2 = exchange(
            run_dimers(
                my_steps_2, me_b, both_2, both_2, lambda i, *_: (2 * i, 0, 0), lambda i, *_: (2 * i + 1, 0, 0)
            )
        )

        spread = jnp.stack([jnp.full(32, -1, jnp.int32), served], axis=1).reshape(64)
        back_1 = lax.all_to_all(place_items(done_1, spread, 8), "frag", split_axis=0, concat_axis=0, tiled=True)
        live_at = pick(entry_hot, cost_2) > 0
        live_at = jnp.stack([live_at, live_at], axis=1).reshape(32)
        target_2 = jnp.where(live_at & (pos_at >= 32), pos_at - 32, -1)
        back_2 = lax.all_to_all(place_items(done_2, target_2, 4), "frag", split_axis=0, concat_axis=0, tiled=True)

        stay_1 = jnp.stack([base_at, jnp.full(32, -1, jnp.int32)], axis=1).reshape(8, 8)
        stay_2 = jnp.where(live_at & (pos_at < 32), pos_at, -1).reshape(8, 4)
        lists = [stay_1[k] for k in range(8)] + [stay_2[k] for k in range(8)] + [send_1, send_2]
        dens, emb = add_up(dens, emb, lists, list(done_1) + list(done_2) + [back_1, back_2])
        return jnp.sum(left), left, dens, emb

    start = (
        jnp.int32(dimers),
        jnp.ones(dimers, jnp.int32),
        jnp.zeros(density.shape, F32),
        jnp.zeros((density.shape[0], aux_factor.shape[2]), F32),
    )
    unused_n, unused_rest, dens, emb = lax.while_loop(lambda carry: carry[0] > 0, one_round, start)
    return dens, emb


def solution(mesh):
    return jax.shard_map(
        shards,
        mesh=mesh,
        in_specs=(
            P("frag", "basis", None),
            P("frag", None, "basis"),
            P(("frag", "basis"), None),
            P(),
            P(("frag", "basis")),
        ),
        out_specs=(P("frag", "basis", None), P("frag", "basis")),
        check_vma=False,
    )
```

```python
import functools

import jax
import jax.numpy as jnp
from jax import lax
from jax.experimental import pallas as pl
from jax.experimental.pallas import tpu as pltpu
from jax.sharding import PartitionSpec as P

COUPLE = 0.015625
BIG = 1 << 30
BF16 = jnp.bfloat16
F32 = jnp.float32
LOAD2 = 16

VMEM = pl.BlockSpec(memory_space=pltpu.VMEM)
SMEM = pl.BlockSpec(memory_space=pltpu.SMEM)


def copy_home(out_ref, row, aux_ref, den_ref, slot):
    out_ref[row, 0:256, :] = aux_ref[slot]
    block = den_ref[slot]
    out_ref[row, 256:288, :] = block[:, 0:128]
    out_ref[row, 288:320, :] = block[:, 128:256]


def pack_home(aux, den, index, outs):
    rows = index.shape[0] // outs

    def kernel(index_ref, aux_ref, den_ref, *out_refs):
        for n, out_ref in enumerate(out_refs):
            def step(row, unused, n=n, out_ref=out_ref):
                copy_home(out_ref, row, aux_ref, den_ref, index_ref[n * rows + row])
                return unused
            lax.fori_loop(0, rows, step, 0)

    shape = jax.ShapeDtypeStruct((rows, 320, 128), BF16)
    return pl.pallas_call(
        kernel,
        out_shape=[shape] * outs,
        in_specs=[SMEM, VMEM, VMEM],
        out_specs=[VMEM] * outs,
        name="pack_home",
    )(index, aux, den)


def pack_items(items, index, outs):
    rows = index.shape[0] // outs

    def kernel(index_ref, items_ref, *out_refs):
        for n, out_ref in enumerate(out_refs):
            for row in range(rows):
                out_ref[row] = items_ref[index_ref[n * rows + row]]

    shape = jax.ShapeDtypeStruct((rows,) + items.shape[1:], BF16)
    return pl.pallas_call(
        kernel,
        out_shape=[shape] * outs,
        in_specs=[SMEM, VMEM],
        out_specs=[VMEM] * outs,
        name="pack_items",
    )(index, items)


def pack_mixed(aux, den, items, index, outs):
    rows = index.shape[0] // outs

    def kernel(index_ref, aux_ref, den_ref, items_ref, *out_refs):
        for n, out_ref in enumerate(out_refs):
            def step(row, unused, n=n, out_ref=out_ref):
                at = index_ref[n * rows + row]

                @pl.when(at < 32)
                def _():
                    copy_home(out_ref, row, aux_ref, den_ref, at)

                @pl.when(at >= 32)
                def _():
                    out_ref[row] = items_ref[at - 32]

                return unused
            lax.fori_loop(0, rows, step, 0)

    shape = jax.ShapeDtypeStruct((rows, 320, 128), BF16)
    return pl.pallas_call(
        kernel,
        out_shape=[shape] * outs,
        in_specs=[SMEM, VMEM, VMEM, VMEM],
        out_specs=[VMEM] * outs,
        name="pack_mixed",
    )(index, aux, den, items)


def place_items(parts, target, rows):
    def kernel(target_ref, *refs):
        out_ref = refs[-1]
        for n, part_ref in enumerate(refs[:-1]):
            def step(row, unused, n=n, part_ref=part_ref):
                at = target_ref[n * rows + row]

                @pl.when(at >= 0)
                def _():
                    out_ref[at] = part_ref[row]

                return unused
            lax.fori_loop(0, rows, step, 0)

    return pl.pallas_call(
        kernel,
        out_shape=jax.ShapeDtypeStruct((32, 72, 128), BF16),
        in_specs=[SMEM] + [VMEM] * len(parts),
        out_specs=VMEM,
        name="place_items",
    )(target, *parts)


def dimer_kernel(steps_ref, me_ref, *refs):
    first, second, outs = refs[0:8], refs[8:16], refs[16:24]
    stacked, weighted, dens, current, squares = refs[24:]
    steps = steps_ref[pl.program_id(0)]
    me = me_ref[0]

    @pl.when(steps > 0)
    def _():
        for n in range(8):
            lanes = slice(n * 128, n * 128 + 128)
            at = pl.multiple_of(lax.bitwise_xor(me, n) * 32, 32)
            for half, part in ((0, first[n]), (256, second[n])):
                stacked[half : half + 256, lanes] = part[0, 0:256, :]
                dens[pl.ds(half + at, 32), 0:128] = part[0, 256:288, :]
                dens[pl.ds(half + at, 32), 128:256] = part[0, 288:320, :]
        fits = []
        for half in (0, 256):
            block = dens[half : half + 256, :]
            sums = []
            for n in range(4):
                lanes = slice(n * 256, n * 256 + 256)
                factor = stacked[half : half + 256, lanes]
                projected = jnp.dot(block, factor, preferred_element_type=F32)
                sums.append(jnp.sum(factor.astype(F32) * projected, axis=0, keepdims=True))
            fits.append(jnp.concatenate(sums, axis=1).astype(BF16).astype(F32))
        coeff = fits[0] + fits[1]
        for n in range(8):
            rows = slice(n * 64, n * 64 + 64)
            weighted[rows, :] = (stacked[rows, :].astype(F32) * coeff).astype(BF16)
        for n in range(4):
            rows = slice(n * 128, n * 128 + 128)
            coulomb = lax.dot_general(
                weighted[rows, :], stacked[...], (((1,), (1,)), ((), ())), preferred_element_type=F32
            )
            row_at = lax.broadcasted_iota(jnp.int32, (128, 512), 0) + n * 128
            col_at = lax.broadcasted_iota(jnp.int32, (128, 512), 1)
            own = dens[rows, :].astype(F32)
            blank = jnp.zeros((128, 256), F32)
            wide = jnp.concatenate([own, blank] if n < 2 else [blank, own], axis=1)
            eye = jnp.where(row_at == col_at, 0.5, 0.0)
            current[rows, :] = (eye + wide + COUPLE * coulomb).astype(BF16)

        def purify(index, unused):
            for n in range(4):
                rows = slice(n * 128, n * 128 + 128)
                square = jnp.dot(current[rows, :], current[...], preferred_element_type=F32)
                cube = jnp.dot(square.astype(BF16), current[...], preferred_element_type=F32)
                squares[rows, :] = (3.0 * square - 2.0 * cube).astype(BF16)
            current[...] = squares[...]
            return unused

        lax.fori_loop(0, steps, purify, 0)
        row_at = lax.broadcasted_iota(jnp.int32, (256, 256), 0)
        col_at = lax.broadcasted_iota(jnp.int32, (256, 256), 1)
        eye = jnp.where(row_at == col_at, 0.5, 0.0)
        for half in (0, 256):
            own = slice(half, half + 256)
            change = current[own, own].astype(F32) - dens[own, :].astype(F32) - eye
            dens[own, :] = change.astype(BF16)
        for n in range(8):
            at = pl.multiple_of(lax.bitwise_xor(me, n) * 32, 32)
            lanes = slice(n * 128, n * 128 + 128)
            for r in range(2):
                change = dens[pl.ds(r * 256 + at, 32), :]
                outs[n][r, 0:32, :] = change[:, 0:128]
                outs[n][r, 32:64, :] = change[:, 128:256]
                partner = jnp.broadcast_to(fits[1 - r][:, lanes], (8, 128))
                outs[n][r, 64:72, :] = partner.astype(BF16)


def run_dimers(steps, me, first, second, first_map, second_map):
    count = steps.shape[0]
    shape = jax.ShapeDtypeStruct((2 * count, 72, 128), BF16)
    return pl.pallas_call(
        dimer_kernel,
        out_shape=[shape] * 8,
        grid_spec=pltpu.PrefetchScalarGridSpec(
            num_scalar_prefetch=2,
            grid=(count,),
            in_specs=[pl.BlockSpec((1, 320, 128), first_map)] * 8
            + [pl.BlockSpec((1, 320, 128), second_map)] * 8,
            out_specs=[pl.BlockSpec((2, 72, 128), lambda i, *_: (i, 0, 0))] * 8,
            scratch_shapes=[
                pltpu.VMEM((512, 1024), BF16),
                pltpu.VMEM((512, 1024), BF16),
                pltpu.VMEM((512, 256), BF16),
                pltpu.VMEM((512, 512), BF16),
                pltpu.VMEM((512, 512), BF16),
            ],
        ),
        name="dimers",
        cost_estimate=pl.CostEstimate(
            flops=count * 4_000_000_000, bytes_accessed=count * 1_500_000, transcendentals=0
        ),
    )(steps, me, *first, *second)


def plan_kernel(me_ref, a_ref, b_ref, cost_ref, flag_ref, send_ref, pos_ref, steps_ref, left_ref, taken, load):
    me = me_ref[0]

    def clear(n, unused):
        taken[n] = 0
        load[n] = 0
        send_ref[n] = -1
        pos_ref[n] = 0
        return unused

    def clear_steps(n, unused):
        steps_ref[n] = 0
        return unused

    lax.fori_loop(0, 32, clear, 0)
    lax.fori_loop(0, LOAD2, clear_steps, 0)

    def visit(d, unused):
        left_ref[d] = 0

        @pl.when(flag_ref[d] > 0)
        def _():
            a, b = a_ref[d], b_ref[d]
            oa, ob = lax.shift_right_logical(a, 5), lax.shift_right_logical(b, 5)
            la, lb = a & 31, b & 31
            bit_a, bit_b = lax.shift_left(1, oa), lax.shift_left(1, ob)
            both = bit_a | bit_b
            free_a = ((taken[oa] & bit_b) == 0) & (load[oa] < LOAD2)
            free_b = ((taken[ob] & bit_a) == 0) & (load[ob] < LOAD2)
            inside = oa == ob
            use_a = free_a & (jnp.logical_not(free_b) | (load[oa] <= load[ob]))
            direct = jnp.where(use_a, oa, jnp.where(free_b, ob, -1))
            direct = jnp.where(inside, jnp.where(load[oa] < LOAD2, oa, -1), direct)

            def look(carry):
                n, found = carry
                c = (d + n) & 31
                good = ((taken[c] & both) == 0) & (load[c] < LOAD2) & (c != oa) & (c != ob)
                return n + 1, jnp.where(good, c, -1)

            start = jnp.where((direct >= 0) | inside, 32, 0)
            unused_n, c = lax.while_loop(
                lambda carry: (carry[0] < 32) & (carry[1] < 0), look, (start, direct)
            )

            @pl.when(c < 0)
            def _():
                left_ref[d] = 1

            @pl.when(c >= 0)
            def _():
                away = jnp.where(c == oa, 0, bit_a) | jnp.where(c == ob, 0, bit_b)
                taken[c] = taken[c] | away
                at = load[c]
                load[c] = at + 1

                @pl.when(c == me)
                def _():
                    pos_ref[2 * at] = jnp.where(c == oa, la, 32 + oa)
                    pos_ref[2 * at + 1] = jnp.where(c == ob, lb, 32 + ob)
                    steps_ref[at] = cost_ref[d]

                @pl.when((c != me) & (oa == me))
                def _():
                    send_ref[c] = la

                @pl.when((c != me) & (ob == me))
                def _():
                    send_ref[c] = lb

        return unused

    lax.fori_loop(0, a_ref.shape[0], visit, 0)


def plan_rest(me, a, b, cost, flag):
    s32 = jnp.int32
    return pl.pallas_call(
        plan_kernel,
        out_shape=[
            jax.ShapeDtypeStruct((32,), s32),
            jax.ShapeDtypeStruct((2 * LOAD2,), s32),
            jax.ShapeDtypeStruct((LOAD2,), s32),
            jax.ShapeDtypeStruct(a.shape, s32),
        ],
        in_specs=[SMEM] * 5,
        out_specs=[SMEM] * 4,
        scratch_shapes=[pltpu.SMEM((32,), s32), pltpu.SMEM((32,), s32)],
        name="plan",
        cost_estimate=pl.CostEstimate(flops=1000, bytes_accessed=30_000_000, transcendentals=0),
    )(me, a, b, cost, flag)


def add_up(dens, emb, lists, parts):
    counts = [part.shape[0] for part in parts]

    def kernel(*refs):
        n_parts = len(parts)
        slot_refs, part_refs = refs[:n_parts], refs[n_parts : 2 * n_parts]
        dens_in, emb_in, dens_ref, emb_ref = refs[2 * n_parts :]
        dens_ref[...] = dens_in[...]
        emb_ref[...] = emb_in[...]
        for slot_ref, part_ref, count in zip(slot_refs, part_refs, counts, strict=True):
            def step(row, unused, slot_ref=slot_ref, part_ref=part_ref):
                slot = slot_ref[row]

                @pl.when(slot >= 0)
                def _():
                    dens_ref[slot, :, 0:128] += part_ref[row, 0:32, :].astype(F32)
                    dens_ref[slot, :, 128:256] += part_ref[row, 32:64, :].astype(F32)
                    emb_ref[pl.ds(slot, 1), :] += part_ref[row, 64:72, :].astype(F32)[0:1, :]

                return unused
            lax.fori_loop(0, count, step, 0)

    n = len(parts)
    return pl.pallas_call(
        kernel,
        out_shape=[jax.ShapeDtypeStruct(dens.shape, F32), jax.ShapeDtypeStruct(emb.shape, F32)],
        in_specs=[SMEM] * n + [VMEM] * (n + 2),
        out_specs=[VMEM, VMEM],
        input_output_aliases={2 * n: 0, 2 * n + 1: 1},
        name="add_up",
    )(*lists, *parts, dens, emb)


def exchange(parts):
    got = [parts[0]]
    for k in range(1, 8):
        got.append(lax.ppermute(parts[k], "basis", [(i, i ^ k) for i in range(8)]))
    return got


def shards(density, aux_factor, pairs, slot_of, costs):
    n_frag = lax.axis_size("frag")
    n_basis = lax.axis_size("basis")
    me_frag = lax.axis_index("frag").astype(jnp.int32)
    me_basis = lax.axis_index("basis").astype(jnp.int32)
    dimers = pairs.shape[0] * n_frag * n_basis

    lookup = pairs[:, :, None] == jnp.arange(slot_of.shape[0], dtype=jnp.int32)
    slots = jnp.sum(jnp.where(lookup, slot_of, 0), axis=2)
    mine = jnp.concatenate([slots[:, 0], slots[:, 1], costs, jnp.zeros(116, jnp.int32)])
    column = lax.all_to_all(
        jnp.broadcast_to(mine, (n_basis, 1, 128)), "basis", split_axis=0, concat_axis=0, tiled=True
    )
    column = column[:, 0, 0:12].reshape(n_basis, 3, 4).transpose(1, 0, 2).reshape(96)
    column = jnp.concatenate([column, jnp.zeros(32, jnp.int32)])
    every = lax.all_to_all(
        jnp.broadcast_to(column, (n_frag, 1, 128)), "frag", split_axis=0, concat_axis=0, tiled=True
    )
    a = every[:, 0, 0:32].reshape(dimers)
    b = every[:, 0, 32:64].reshape(dimers)
    cost = every[:, 0, 64:96].reshape(dimers)

    order = jnp.arange(dimers, dtype=jnp.int32)
    columns = jnp.arange(n_frag, dtype=jnp.int32)
    own_a, own_b = a // 32, b // 32
    low, high = jnp.minimum(own_a, own_b), jnp.maximum(own_a, own_b)
    pair_id = low * 32 + high
    inside = own_a == own_b
    mine_a = (own_a == me_frag) & jnp.logical_not(inside)
    mine_b = (own_b == me_frag) & jnp.logical_not(inside)
    other = jnp.where(mine_a, own_b, jnp.where(mine_b, own_a, -1))
    local = jnp.where(mine_a, a, b) & 31
    key = order * 256 + local * 8 + cost
    xor_devices = lax.bitwise_xor(me_basis, jnp.arange(8, dtype=jnp.int32))
    served = (jnp.arange(4, dtype=jnp.int32)[None, :] * 8 + xor_devices[:, None]).reshape(32)
    served_hot = served[:, None] == columns[None, :]
    entries = (jnp.arange(2, dtype=jnp.int32)[None, :] * 8 + xor_devices[:, None]).reshape(16)
    entry_hot = entries[:, None] == jnp.arange(LOAD2, dtype=jnp.int32)[None, :]
    me_f, me_b = me_frag.reshape(1), me_basis.reshape(1)
    keep_first = (me_frag < columns) == ((me_frag + columns) % 2 == 0)

    def pick(hot, table):
        return jnp.sum(jnp.where(hot, table[None, :], 0), axis=1)

    def one_round(carry):
        unused_n, rest, dens, emb = carry
        open_dimer = rest > 0
        match = (other[None, :] == columns[:, None]) & open_dimer[None, :]
        keyed = jnp.where(match, key[None, :], BIG)
        key_0 = jnp.min(keyed, axis=1)
        key_1 = jnp.min(jnp.where(keyed > key_0[:, None], keyed, BIG), axis=1)
        here = jnp.where(keep_first, key_0, key_1)
        there = jnp.where(keep_first, key_1, key_0)
        send_1 = jnp.where(there < BIG, (there >> 3) & 31, -1)
        base_1 = jnp.where(here < BIG, (here >> 3) & 31, -1)
        steps_1 = jnp.where(here < BIG, here & 7, 0)

        (out_1,) = pack_home(aux_factor, density, jnp.maximum(send_1, 0), 1)
        in_1 = lax.all_to_all(out_1, "frag", split_axis=0, concat_axis=0, tiled=True)

        earlier = (pair_id[:, None] == pair_id[None, :]) & (order[None, :] < order[:, None])
        earlier = jnp.sum(jnp.where(earlier & open_dimer[None, :], 1, 0), axis=1)
        flag = jnp.where(open_dimer & ((earlier >= 2) | inside), 1, 0)
        send_2, pos_2, cost_2, left = plan_rest(me_f, a, b, cost, flag)

        base_at = pick(served_hot, base_1)
        home_1 = exchange(pack_home(aux_factor, density, jnp.maximum(base_at, 0), 8))

        (out_2,) = pack_home(aux_factor, density, jnp.maximum(send_2, 0), 1)
        out_2, in_1, home_1 = lax.optimization_barrier((out_2, in_1, home_1))
        in_2 = lax.all_to_all(out_2, "frag", split_axis=0, concat_axis=0, tiled=True)

        away_1 = exchange(pack_items(in_1, served, 8))
        my_steps_1 = jnp.sum(
            jnp.where(me_basis == jnp.arange(8, dtype=jnp.int32), steps_1.reshape(4, 8), 0), axis=1
        )
        same = lambda i, *_: (i, 0, 0)
        done_1 = exchange(run_dimers(my_steps_1, me_b, home_1, away_1, same, same))

        in_2, done_1 = lax.optimization_barrier((in_2, done_1))
        pos_at = jnp.stack([pick(entry_hot, pos_2[0::2]), pick(entry_hot, pos_2[1::2])], axis=1).reshape(32)
        both_2 = exchange(pack_mixed(aux_factor, density, in_2, pos_at, 8))
        my_steps_2 = jnp.sum(
            jnp.where(me_basis == jnp.arange(8, dtype=jnp.int32), cost_2.reshape(2, 8), 0), axis=1
        )
        done_2 = exchange(
            run_dimers(
                my_steps_2, me_b, both_2, both_2, lambda i, *_: (2 * i, 0, 0), lambda i, *_: (2 * i + 1, 0, 0)
            )
        )

        spread = jnp.stack([jnp.full(32, -1, jnp.int32), served], axis=1).reshape(64)
        back_1 = lax.all_to_all(place_items(done_1, spread, 8), "frag", split_axis=0, concat_axis=0, tiled=True)
        live_at = pick(entry_hot, cost_2) > 0
        live_at = jnp.stack([live_at, live_at], axis=1).reshape(32)
        target_2 = jnp.where(live_at & (pos_at >= 32), pos_at - 32, -1)
        back_2 = lax.all_to_all(place_items(done_2, target_2, 4), "frag", split_axis=0, concat_axis=0, tiled=True)

        stay_1 = jnp.stack([base_at, jnp.full(32, -1, jnp.int32)], axis=1).reshape(8, 8)
        stay_2 = jnp.where(live_at & (pos_at < 32), pos_at, -1).reshape(8, 4)
        lists = [stay_1[k] for k in range(8)] + [stay_2[k] for k in range(8)] + [send_1, send_2]
        dens, emb = add_up(dens, emb, lists, list(done_1) + list(done_2) + [back_1, back_2])
        return jnp.sum(left), left, dens, emb

    start = (
        jnp.int32(dimers),
        jnp.ones(dimers, jnp.int32),
        jnp.zeros(density.shape, F32),
        jnp.zeros((density.shape[0], aux_factor.shape[2]), F32),
    )
    unused_n, unused_rest, dens, emb = lax.while_loop(lambda carry: carry[0] > 0, one_round, start)
    return dens, emb


def solution(mesh):
    return jax.shard_map(
        shards,
        mesh=mesh,
        in_specs=(
            P("frag", "basis", None),
            P("frag", None, "basis"),
            P(("frag", "basis"), None),
            P(),
            P(("frag", "basis")),
        ),
        out_specs=(P("frag", "basis", None), P("frag", "basis")),
        check_vma=False,
    )
```

```python
import jax
import jax.numpy as jnp
from jax import lax
from jax.experimental import pallas as pl
from jax.experimental.pallas import tpu as pltpu
from jax.sharding import PartitionSpec as P

COUPLE = 0.015625
BIG = 1 << 30
BF16 = jnp.bfloat16
F32 = jnp.float32
KX, KZ = 6, 2
NX, NZ = 3 * KX, 8 * KZ
SENT, RELAY, POS, HOME, LATE, STEPS, MODE, TABLE = 0, 32, 64, 128, 160, 192, 224, 256
OUT, BASE, STEP1, RANKED = 0, 32, 64, 96

VMEM = pl.BlockSpec(memory_space=pltpu.VMEM)
SMEM = pl.BlockSpec(memory_space=pltpu.SMEM)


def loop(count, body):
    def step(n, unused):
        body(n)
        return unused

    lax.fori_loop(0, count, step, 0)


def ranked_at(device, place):
    return place * 8 + jnp.where(place % 2 == 0, device, 7 - device)


def pack(tables, me, find, outs, rows, home, items):
    sizes = ([32] if home else []) + [item.shape[0] for item in items]

    def kernel(*refs):
        table_refs, me_ref, refs = refs[: len(tables)], refs[len(tables)], refs[len(tables) + 1 :]
        sources, out_refs = refs[: len(refs) - outs], refs[len(refs) - outs :]
        for n, out_ref in enumerate(out_refs):

            def body(row, n=n, out_ref=out_ref):
                at = jnp.maximum(find(table_refs, me_ref[0], n, row), 0)
                base, left = 0, list(sources)
                for which, size in enumerate(sizes):
                    here = (at >= base) & (at < base + size)
                    if home and which == 0:
                        aux_ref, den_ref = left.pop(0), left.pop(0)

                        @pl.when(here)
                        def _(aux_ref=aux_ref, den_ref=den_ref):
                            out_ref[row, 0:256, :] = aux_ref[at]
                            block = den_ref[at]
                            out_ref[row, 256:288, :] = block[:, 0:128]
                            out_ref[row, 288:320, :] = block[:, 128:256]
                    else:
                        item_ref = left.pop(0)

                        @pl.when(here)
                        def _(item_ref=item_ref, base=base):
                            out_ref[row] = item_ref[at - base]

                    base += size

            loop(rows, body)

    sources = list(home) + list(items)
    return pl.pallas_call(
        kernel,
        out_shape=[jax.ShapeDtypeStruct((rows, 320, 128), BF16)] * outs,
        in_specs=[SMEM] * (len(tables) + 1) + [VMEM] * len(sources),
        out_specs=[VMEM] * outs,
        name="pack",
    )(*tables, me, *sources)


def place(tables, me, parts, finds, out_rows):
    def kernel(*refs):
        table_refs, me_ref, refs = refs[: len(tables)], refs[len(tables)], refs[len(tables) + 1 :]
        for part_ref, find in zip(refs[: len(parts)], finds, strict=True):

            def body(row, part_ref=part_ref, find=find):
                at = find(table_refs, me_ref[0], row)
                base = 0
                for out_ref, size in zip(refs[len(parts) :], out_rows, strict=True):

                    @pl.when((at >= base) & (at < base + size))
                    def _(out_ref=out_ref, base=base):
                        out_ref[at - base] = part_ref[row]

                    base += size

            loop(part_ref.shape[0], body)

    return pl.pallas_call(
        kernel,
        out_shape=[jax.ShapeDtypeStruct((size, 72, 128), BF16) for size in out_rows],
        in_specs=[SMEM] * (len(tables) + 1) + [VMEM] * len(parts),
        out_specs=[VMEM] * len(out_rows),
        name="place",
    )(*tables, me, *parts)


def add_up(tables, me, parts, finds, dens, emb):
    def kernel(*refs):
        table_refs, me_ref, refs = refs[: len(tables)], refs[len(tables)], refs[len(tables) + 1 :]
        dens_in, emb_in, dens_ref, emb_ref = refs[len(parts) :]
        dens_ref[...] = dens_in[...]
        emb_ref[...] = emb_in[...]
        for part_ref, find in zip(refs[: len(parts)], finds, strict=True):

            def body(row, part_ref=part_ref, find=find):
                slot = find(table_refs, me_ref[0], row)

                @pl.when((slot >= 0) & (slot < 32))
                def _():
                    dens_ref[slot, :, 0:128] += part_ref[row, 0:32, :].astype(F32)
                    dens_ref[slot, :, 128:256] += part_ref[row, 32:64, :].astype(F32)
                    emb_ref[pl.ds(slot, 1), :] += part_ref[row, 64:72, :].astype(F32)[0:1, :]

            loop(part_ref.shape[0], body)

    first = len(tables) + 1 + len(parts)
    return pl.pallas_call(
        kernel,
        out_shape=[jax.ShapeDtypeStruct(dens.shape, F32), jax.ShapeDtypeStruct(emb.shape, F32)],
        in_specs=[SMEM] * (len(tables) + 1) + [VMEM] * (len(parts) + 2),
        out_specs=[VMEM, VMEM],
        input_output_aliases={first: 0, first + 1: 1},
        name="add_up",
    )(*tables, me, *parts, dens, emb)


def take(half, me, parts, row, stacked, dens):
    for n in range(8):
        lanes = slice(n * 128, n * 128 + 128)
        at = pl.multiple_of(lax.bitwise_xor(me, n) * 32, 32)
        stacked[half : half + 256, lanes] = parts[n][row, 0:256, :]
        dens[pl.ds(half + at, 32), 0:128] = parts[n][row, 256:288, :]
        dens[pl.ds(half + at, 32), 128:256] = parts[n][row, 288:320, :]


def one_dimer(steps, me, load, outs, scratch):
    stacked, weighted, dens, current, squares = scratch

    @pl.when(steps > 0)
    def _():
        load()
        fits = []
        for half in (0, 256):
            block = dens[half : half + 256, :]
            sums = []
            for n in range(4):
                lanes = slice(n * 256, n * 256 + 256)
                factor = stacked[half : half + 256, lanes]
                projected = jnp.dot(block, factor, preferred_element_type=F32)
                sums.append(jnp.sum(factor.astype(F32) * projected, axis=0, keepdims=True))
            fits.append(jnp.concatenate(sums, axis=1).astype(BF16).astype(F32))
        coeff = fits[0] + fits[1]
        for n in range(8):
            rows = slice(n * 64, n * 64 + 64)
            weighted[rows, :] = (stacked[rows, :].astype(F32) * coeff).astype(BF16)
        for n in range(4):
            rows = slice(n * 128, n * 128 + 128)
            coulomb = lax.dot_general(
                weighted[rows, :], stacked[...], (((1,), (1,)), ((), ())), preferred_element_type=F32
            )
            row_at = lax.broadcasted_iota(jnp.int32, (128, 512), 0) + n * 128
            col_at = lax.broadcasted_iota(jnp.int32, (128, 512), 1)
            own = dens[rows, :].astype(F32)
            blank = jnp.zeros((128, 256), F32)
            wide = jnp.concatenate([own, blank] if n < 2 else [blank, own], axis=1)
            eye = jnp.where(row_at == col_at, 0.5, 0.0)
            current[rows, :] = (eye + wide + COUPLE * coulomb).astype(BF16)

        def purify(index, unused):
            for n in range(4):
                rows = slice(n * 128, n * 128 + 128)
                square = jnp.dot(current[rows, :], current[...], preferred_element_type=F32)
                cube = jnp.dot(square.astype(BF16), current[...], preferred_element_type=F32)
                squares[rows, :] = (3.0 * square - 2.0 * cube).astype(BF16)
            current[...] = squares[...]
            return unused

        lax.fori_loop(0, steps, purify, 0)
        row_at = lax.broadcasted_iota(jnp.int32, (256, 256), 0)
        col_at = lax.broadcasted_iota(jnp.int32, (256, 256), 1)
        eye = jnp.where(row_at == col_at, 0.5, 0.0)
        for half in (0, 256):
            own = slice(half, half + 256)
            change = current[own, own].astype(F32) - dens[own, :].astype(F32) - eye
            dens[own, :] = change.astype(BF16)
        for n in range(8):
            at = pl.multiple_of(lax.bitwise_xor(me, n) * 32, 32)
            lanes = slice(n * 128, n * 128 + 128)
            for r in range(2):
                change = dens[pl.ds(r * 256 + at, 32), :]
                outs[n][r, 0:32, :] = change[:, 0:128]
                outs[n][r, 32:64, :] = change[:, 128:256]
                partner = jnp.broadcast_to(fits[1 - r][:, lanes], (8, 128))
                outs[n][r, 64:72, :] = partner.astype(BF16)


SCRATCH = [
    pltpu.VMEM((512, 1024), BF16),
    pltpu.VMEM((512, 1024), BF16),
    pltpu.VMEM((512, 256), BF16),
    pltpu.VMEM((512, 512), BF16),
    pltpu.VMEM((512, 512), BF16),
]


def run_dimers(kernel, count, tables, blocks, maps, parts):
    shape = jax.ShapeDtypeStruct((2 * count, 72, 128), BF16)
    specs = []
    for block, index_map in zip(blocks, maps, strict=True):
        specs += [pl.BlockSpec((block, 320, 128), index_map)] * 8
    return pl.pallas_call(
        kernel,
        out_shape=[shape] * 8,
        grid_spec=pltpu.PrefetchScalarGridSpec(
            num_scalar_prefetch=2,
            grid=(count,),
            in_specs=specs,
            out_specs=[pl.BlockSpec((2, 72, 128), lambda i, *_: (i, 0, 0))] * 8,
            scratch_shapes=SCRATCH,
        ),
        name="dimers",
        cost_estimate=pl.CostEstimate(
            flops=count * 4_000_000_000, bytes_accessed=count * 1_500_000, transcendentals=0
        ),
    )(*tables, *parts)


def kernel_1(table_ref, me_ref, *refs):
    me, i = me_ref[0], pl.program_id(0)
    first, second, outs, scratch = refs[0:8], refs[8:16], refs[16:24], refs[24:]
    stacked, dens = scratch[0], scratch[2]

    def load():
        take(0, me, first, 0, stacked, dens)
        take(256, me, second, 0, stacked, dens)

    other = table_ref[RANKED + ranked_at(me, i)]
    one_dimer(table_ref[STEP1 + other], me, load, outs, scratch)


def kernel_2(table_ref, me_ref, *refs):
    me, i = me_ref[0], pl.program_id(0)
    home, late, outs, scratch = refs[0:8], refs[8:16], refs[16:24], refs[24:]
    stacked, dens = scratch[0], scratch[2]
    split = table_ref[MODE + me] > 0

    def load():
        both_late = split & (i == 0)
        both_home = split & (i == 1)

        @pl.when(both_late)
        def _():
            take(0, me, late, 0, stacked, dens)

        @pl.when(jnp.logical_not(both_late))
        def _():
            take(0, me, home, jnp.where(split, 0, i), stacked, dens)

        @pl.when(both_home)
        def _():
            take(256, me, home, 1, stacked, dens)

        @pl.when(jnp.logical_not(both_home))
        def _():
            take(256, me, late, jnp.where(split, 1, i), stacked, dens)

    one_dimer(table_ref[STEPS + 2 * me + i], me, load, outs, scratch)


def plan_kernel(me_ref, inside_ref, a_ref, b_ref, cost_ref, flag_ref, table_ref, left_ref, to_x, to_z, n_direct, n_third, n_self):
    me = me_ref[0]

    def clear(n):
        to_z[n] = 0
        table_ref[n] = jnp.where(n < STEPS, -1, 0)

    def clear_x(n):
        to_x[n] = 0

    def clear_c(n):
        n_direct[n] = 0
        n_third[n] = 0
        n_self[n] = 0

    loop(TABLE, clear)
    loop(128, clear_x)
    loop(32, clear_c)

    def put(at, good, spare, value):
        table_ref[jnp.where(good, at, spare)] = value

    def can(o, c, extra=0):
        xo, zo, xc, zc = o >> 3, o & 7, c >> 3, c & 7
        return ((xo == xc) | (to_x[o * 4 + xc] < KX)) & ((zo == zc) | (to_z[xc * 64 + zo * 8 + zc] + extra < KZ))

    def send(o, slot, c):
        xo, zo, xc, zc = o >> 3, o & 7, c >> 3, c & 7
        at_x, at_z = o * 4 + xc, xc * 64 + zo * 8 + zc
        n_x, n_z = to_x[at_x], to_z[at_z]
        move_x, move_z = xo != xc, zo != zc
        to_x[at_x] = n_x + jnp.where(move_x, 1, 0)
        to_z[at_z] = n_z + jnp.where(move_z, 1, 0)
        in_x = (lax.bitwise_xor(xo, xc) - 1) * KX + n_x
        put(SENT + in_x, move_x & (o == me), SENT + 31, slot)
        put(RELAY + zc * KZ + n_z, move_z & (xc * 8 + zo == me), RELAY + 31, jnp.where(move_x, 32 + in_x, slot))
        return jnp.where(move_z, 32 + NX + zo * KZ + n_z, 32 + in_x)

    def visit(d):
        @pl.when(flag_ref[d] > 0)
        def _():
            a, b, cost = a_ref[d], b_ref[d], cost_ref[d]
            oa, ob, la, lb = a >> 5, b >> 5, a & 31, b & 31
            left_ref[d] = 0

            @pl.when(oa == ob)
            def _():
                q = n_self[oa]

                @pl.when(q < 8)
                def _():
                    n_self[oa] = q + 1

                    @pl.when(oa == me)
                    def _():
                        at = 2 * (7 - q)
                        table_ref[POS + 2 * at + 2] = la
                        table_ref[POS + 2 * at + 3] = lb
                        table_ref[HOME + at] = la
                        table_ref[HOME + at + 1] = lb
                        table_ref[STEPS + at + 1] = cost
                        table_ref[MODE + 7 - q] = 1

                @pl.when(q >= 8)
                def _():
                    left_ref[d] = 1

            @pl.when(oa != ob)
            def _():
                n_a, n_b = n_direct[oa], n_direct[ob]
                fit_a = ((n_a + 2) >> 1) + jnp.maximum(n_third[oa], inside_ref[oa]) <= 8
                fit_b = ((n_b + 2) >> 1) + jnp.maximum(n_third[ob], inside_ref[ob]) <= 8
                can_a, can_b = can(ob, oa) & fit_a, can(oa, ob) & fit_b
                full_a = to_z[(oa >> 3) * 64 + (ob & 7) * 8 + (oa & 7)] * 4 + n_a
                full_b = to_z[(ob >> 3) * 64 + (oa & 7) * 8 + (ob & 7)] * 4 + n_b
                use_a = can_a & (jnp.logical_not(can_b) | (full_a <= full_b))
                direct = can_a | can_b

                @pl.when(direct)
                def _():
                    c, o = jnp.where(use_a, oa, ob), jnp.where(use_a, ob, oa)
                    stay, move = jnp.where(use_a, la, lb), jnp.where(use_a, lb, la)
                    at = jnp.where(use_a, n_a, n_b)
                    n_direct[c] = at + 1
                    late = send(o, move, c)

                    @pl.when(c == me)
                    def _():
                        table_ref[POS + 2 * at] = stay
                        table_ref[POS + 2 * at + 1] = late
                        table_ref[HOME + at] = stay
                        table_ref[LATE + at] = late
                        table_ref[STEPS + at] = cost

                @pl.when(jnp.logical_not(direct))
                def _():
                    same_z = jnp.where((oa & 7) == (ob & 7), 1, 0)

                    def look(carry):
                        n, unused = carry
                        c = (d + n) & 31
                        fit = ((n_direct[c] + 1) >> 1) + jnp.maximum(n_third[c] + 1, inside_ref[c]) <= 8
                        good = fit & can(oa, c, same_z) & can(ob, c, same_z) & (c != oa) & (c != ob)
                        return n + 1, jnp.where(good, c, -1)

                    unused, c = lax.while_loop(
                        lambda carry: (carry[0] < 32) & (carry[1] < 0), look, (jnp.int32(0), jnp.int32(-1))
                    )

                    @pl.when(c < 0)
                    def _():
                        left_ref[d] = 1

                    @pl.when(c >= 0)
                    def _():
                        t = n_third[c]
                        n_third[c] = t + 1
                        late_a = send(oa, la, c)
                        late_b = send(ob, lb, c)

                        @pl.when(c == me)
                        def _():
                            at = 2 * (7 - t)
                            table_ref[POS + 2 * at] = late_a
                            table_ref[POS + 2 * at + 1] = late_b
                            table_ref[LATE + at] = late_a
                            table_ref[LATE + at + 1] = late_b
                            table_ref[STEPS + at] = cost
                            table_ref[MODE + 7 - t] = 1

    loop(a_ref.shape[0], visit)


def plan_rest(me, inside_count, a, b, cost, flag):
    s32 = jnp.int32
    return pl.pallas_call(
        plan_kernel,
        out_shape=[jax.ShapeDtypeStruct((TABLE,), s32), jax.ShapeDtypeStruct(a.shape, s32)],
        in_specs=[SMEM] * 6,
        out_specs=[SMEM] * 2,
        scratch_shapes=[pltpu.SMEM((128,), s32), pltpu.SMEM((256,), s32)] + [pltpu.SMEM((32,), s32)] * 3,
        name="plan",
        cost_estimate=pl.CostEstimate(flops=1000, bytes_accessed=30_000_000, transcendentals=0),
    )(me, inside_count, a, b, cost, flag)


def exchange(parts):
    got = [parts[0]]
    for k in range(1, 8):
        got.append(lax.ppermute(parts[k], "basis", [(i, i ^ k) for i in range(8)]))
    return got


def along_x(parts):
    return [lax.ppermute(parts[k - 1], "frag", [(i, i ^ (8 * k)) for i in range(32)]) for k in (1, 2, 3)]


def along_z(part):
    groups = [[8 * x + z for z in range(8)] for x in range(4)]
    return lax.all_to_all(part, "frag", 0, 0, tiled=True, axis_index_groups=groups)


def across(part):
    return lax.all_to_all(part, "frag", split_axis=0, concat_axis=0, tiled=True)


def after(value, *others):
    return lax.optimization_barrier((value, others))[0]


def shards(density, aux_factor, pairs, slot_of, costs):
    n_frag = lax.axis_size("frag")
    n_basis = lax.axis_size("basis")
    me_frag = lax.axis_index("frag").astype(jnp.int32)
    me_basis = lax.axis_index("basis").astype(jnp.int32)
    dimers = pairs.shape[0] * n_frag * n_basis

    lookup = pairs[:, :, None] == jnp.arange(slot_of.shape[0], dtype=jnp.int32)
    slots = jnp.sum(jnp.where(lookup, slot_of, 0), axis=2)
    mine = jnp.concatenate([slots[:, 0], slots[:, 1], costs, jnp.zeros(116, jnp.int32)])
    column = lax.all_to_all(
        jnp.broadcast_to(mine, (n_basis, 1, 128)), "basis", split_axis=0, concat_axis=0, tiled=True
    )
    column = column[:, 0, 0:12].reshape(n_basis, 3, 4).transpose(1, 0, 2).reshape(96)
    column = jnp.concatenate([column, jnp.zeros(32, jnp.int32)])
    every = across(jnp.broadcast_to(column, (n_frag, 1, 128)))
    a = every[:, 0, 0:32].reshape(dimers)
    b = every[:, 0, 32:64].reshape(dimers)
    cost = every[:, 0, 64:96].reshape(dimers)

    order = jnp.arange(dimers, dtype=jnp.int32)
    columns = jnp.arange(n_frag, dtype=jnp.int32)
    own_a, own_b = a // 32, b // 32
    low, high = jnp.minimum(own_a, own_b), jnp.maximum(own_a, own_b)
    pair_id = low * 32 + high
    inside = own_a == own_b
    mine_a = (own_a == me_frag) & jnp.logical_not(inside)
    mine_b = (own_b == me_frag) & jnp.logical_not(inside)
    other = jnp.where(mine_a, own_b, jnp.where(mine_b, own_a, -1))
    local = jnp.where(mine_a, a, b) & 31
    key = order * 256 + local * 8 + cost
    me_f, me_b = me_frag.reshape(1), me_basis.reshape(1)
    keep_first = (me_frag < columns) == ((me_frag + columns) % 2 == 0)
    home = (aux_factor, density)

    def one_round(carry):
        unused_n, rest, dens, emb = carry
        open_dimer = rest > 0
        match = (other[None, :] == columns[:, None]) & open_dimer[None, :]
        keyed = jnp.where(match, key[None, :], BIG)
        key_0 = jnp.min(keyed, axis=1)
        key_1 = jnp.min(jnp.where(keyed > key_0[:, None], keyed, BIG), axis=1)
        here = jnp.where(keep_first, key_0, key_1)
        there = jnp.where(keep_first, key_1, key_0)
        send_1 = jnp.where(there < BIG, (there >> 3) & 31, -1)
        base_1 = jnp.where(here < BIG, (here >> 3) & 31, -1)
        steps_1 = jnp.where(here < BIG, here & 7, 0)

        (out_1,) = pack((send_1,), me_b, lambda t, me, n, row: t[0][row], 1, 32, home, [])
        in_1 = across(out_1)

        weight = steps_1 * 64 - columns
        rank = jnp.sum((weight[None, :] > weight[:, None]).astype(jnp.int32), axis=1)
        ranked = jnp.sum(jnp.where(rank[None, :] == columns[:, None], columns[None, :], 0), axis=1)
        table_1 = jnp.concatenate([send_1, base_1, steps_1, ranked])

        earlier = (pair_id[:, None] == pair_id[None, :]) & (order[None, :] < order[:, None])
        earlier = jnp.sum(jnp.where(earlier & open_dimer[None, :], 1, 0), axis=1)
        flagged = open_dimer & ((earlier >= 2) | inside)
        flag = jnp.where(flagged, 1, 0)
        inside_here = (own_a[None, :] == columns[:, None]) & (inside & open_dimer)[None, :]
        inside_count = jnp.sum(jnp.where(inside_here, 1, 0), axis=1)
        table_2, left = plan_rest(me_f, inside_count, a, b, cost, flag)
        left = jnp.where(flagged, left, 0)
        tables = (table_1, table_2)

        def served(t, me, n, row):
            return t[0][RANKED + ranked_at(lax.bitwise_xor(me, n), row)]

        home_1 = exchange(
            pack(tables[:1], me_b, lambda t, me, n, row: t[0][BASE + served(t, me, n, row)], 8, 4, home, [])
        )
        in_x = along_x(pack(tables, me_b, lambda t, me, n, row: t[1][SENT + n * KX + row], 3, KX, home, []))
        (out_2,) = pack(tables, me_b, lambda t, me, n, row: t[1][RELAY + row], 1, NZ, home, in_x)
        in_z = along_z(after(out_2, in_1))
        home_2 = exchange(
            pack(
                tables, me_b, lambda t, me, n, row: t[1][HOME + 2 * lax.bitwise_xor(me, n) + row], 8, 2, home, []
            )
        )

        away_1 = exchange(pack(tables, me_b, served, 8, 4, (), [in_1]))
        one = lambda i, *_: (i, 0, 0)
        done_1 = exchange(
            run_dimers(kernel_1, 4, (table_1, me_b), (1, 1), (one, one), [*home_1, *away_1])
        )

        late_2 = exchange(
            pack(
                tables,
                me_b,
                lambda t, me, n, row: t[1][LATE + 2 * lax.bitwise_xor(me, n) + row] - 32,
                8,
                2,
                (),
                [*in_x, after(in_z, away_1)],
            )
        )
        whole = lambda i, *_: (0, 0, 0)
        done_2 = exchange(
            run_dimers(kernel_2, 2, (table_2, me_b), (2, 2), (whole, whole), [*home_2, *late_2])
        )

        def back_to(k):
            return lambda t, me, row: jnp.where(row % 2 == 1, served(t, me, k, row // 2), -1)

        (ret_1,) = place(tables, me_b, done_1, [back_to(k) for k in range(8)], [32])
        back_1 = across(ret_1)

        def place_2(t, me, k, row):
            at = 2 * lax.bitwise_xor(me, k) + row // 2
            return jnp.where(t[1][STEPS + at] > 0, t[1][POS + 2 * at + row % 2], -1)

        def back_z(k):
            return lambda t, me, row: place_2(t, me, k, row) - 32 - NX

        def back_x(k):
            return lambda t, me, row: place_2(t, me, k, row) - 32

        (ret_z,) = place(tables, me_b, done_2, [back_z(k) for k in range(8)], [NZ])
        rest_z = along_z(after(ret_z, back_1))
        ret_x = place(
            tables,
            me_b,
            [*done_2, rest_z],
            [back_x(k) for k in range(8)] + [lambda t, me, row: t[1][RELAY + row] - 32],
            [KX] * 3,
        )
        rest_x = along_x(ret_x)

        def stay_1(k):
            return lambda t, me, row: jnp.where(row % 2 == 0, t[0][BASE + served(t, me, k, row // 2)], -1)

        def stay_2(k):
            return lambda t, me, row: place_2(t, me, k, row)

        def from_x(k):
            return lambda t, me, row: t[1][SENT + k * KX + row]

        finds = (
            [stay_1(k) for k in range(8)]
            + [stay_2(k) for k in range(8)]
            + [lambda t, me, row: t[0][OUT + row], lambda t, me, row: t[1][RELAY + row]]
            + [from_x(k) for k in range(3)]
        )
        dens, emb = add_up(tables, me_b, [*done_1, *done_2, back_1, rest_z, *rest_x], finds, dens, emb)
        return jnp.sum(left), left, dens, emb

    start = (
        jnp.int32(dimers),
        jnp.ones(dimers, jnp.int32),
        jnp.zeros(density.shape, F32),
        jnp.zeros((density.shape[0], aux_factor.shape[2]), F32),
    )
    unused_n, unused_rest, dens, emb = lax.while_loop(lambda carry: carry[0] > 0, one_round, start)
    return dens, emb


def solution(mesh):
    return jax.shard_map(
        shards,
        mesh=mesh,
        in_specs=(
            P("frag", "basis", None),
            P("frag", None, "basis"),
            P(("frag", "basis"), None),
            P(),
            P(("frag", "basis")),
        ),
        out_specs=(P("frag", "basis", None), P("frag", "basis")),
        check_vma=False,
    )
```

```python
import jax
import jax.numpy as jnp
from jax import lax
from jax.experimental import pallas as pl
from jax.experimental.pallas import tpu as pltpu
from jax.sharding import PartitionSpec as P


COUPLE = 0.015625
BIG = 1 << 30
BF16 = jnp.bfloat16
F32 = jnp.float32
KX, KZ = 6, 2
NX, NZ = 3 * KX, 8 * KZ
SENT, RELAY, POS, HOME, LATE, STEPS, MODE, TABLE = 0, 32, 64, 128, 160, 192, 224, 256
OUT, BASE, STEP1, RANKED = 0, 32, 64, 96

VMEM = pl.BlockSpec(memory_space=pltpu.VMEM)
SMEM = pl.BlockSpec(memory_space=pltpu.SMEM)


def loop(count, body):
    def step(n, unused):
        body(n)
        return unused

    lax.fori_loop(0, count, step, 0)


def ranked_at(device, place):
    return place * 8 + jnp.where(place % 2 == 0, device, 7 - device)


def pack(tables, me, find, outs, rows, home, items):
    sizes = ([32] if home else []) + [item.shape[0] for item in items]

    def kernel(*refs):
        table_refs, me_ref, refs = refs[: len(tables)], refs[len(tables)], refs[len(tables) + 1 :]
        sources, out_refs = refs[: len(refs) - outs], refs[len(refs) - outs :]
        for n, out_ref in enumerate(out_refs):

            def body(row, n=n, out_ref=out_ref):
                at = jnp.maximum(find(table_refs, me_ref[0], n, row), 0)
                base, left = 0, list(sources)
                for which, size in enumerate(sizes):
                    here = (at >= base) & (at < base + size)
                    if home and which == 0:
                        aux_ref, den_ref = left.pop(0), left.pop(0)

                        @pl.when(here)
                        def _(aux_ref=aux_ref, den_ref=den_ref):
                            out_ref[row, 0:256, :] = aux_ref[at]
                            block = den_ref[at]
                            out_ref[row, 256:288, :] = block[:, 0:128]
                            out_ref[row, 288:320, :] = block[:, 128:256]
                    else:
                        item_ref = left.pop(0)

                        @pl.when(here)
                        def _(item_ref=item_ref, base=base):
                            out_ref[row] = item_ref[at - base]

                    base += size

            loop(rows, body)

    sources = list(home) + list(items)
    return pl.pallas_call(
        kernel,
        out_shape=[jax.ShapeDtypeStruct((rows, 320, 128), BF16)] * outs,
        in_specs=[SMEM] * (len(tables) + 1) + [VMEM] * len(sources),
        out_specs=[VMEM] * outs,
        name="pack",
    )(*tables, me, *sources)


def place(tables, me, parts, finds, out_rows):
    def kernel(*refs):
        table_refs, me_ref, refs = refs[: len(tables)], refs[len(tables)], refs[len(tables) + 1 :]
        for part_ref, find in zip(refs[: len(parts)], finds, strict=True):

            def body(row, part_ref=part_ref, find=find):
                at = find(table_refs, me_ref[0], row)
                base = 0
                for out_ref, size in zip(refs[len(parts) :], out_rows, strict=True):

                    @pl.when((at >= base) & (at < base + size))
                    def _(out_ref=out_ref, base=base):
                        out_ref[at - base] = part_ref[row]

                    base += size

            loop(part_ref.shape[0], body)

    return pl.pallas_call(
        kernel,
        out_shape=[jax.ShapeDtypeStruct((size, 72, 128), BF16) for size in out_rows],
        in_specs=[SMEM] * (len(tables) + 1) + [VMEM] * len(parts),
        out_specs=[VMEM] * len(out_rows),
        name="place",
    )(*tables, me, *parts)


def add_up(tables, me, parts, finds, dens, emb):
    def kernel(*refs):
        table_refs, me_ref, refs = refs[: len(tables)], refs[len(tables)], refs[len(tables) + 1 :]
        dens_in, emb_in, dens_ref, emb_ref = refs[len(parts) :]
        dens_ref[...] = dens_in[...]
        emb_ref[...] = emb_in[...]
        for part_ref, find in zip(refs[: len(parts)], finds, strict=True):

            def body(row, part_ref=part_ref, find=find):
                slot = find(table_refs, me_ref[0], row)

                @pl.when((slot >= 0) & (slot < 32))
                def _():
                    dens_ref[slot, :, 0:128] += part_ref[row, 0:32, :].astype(F32)
                    dens_ref[slot, :, 128:256] += part_ref[row, 32:64, :].astype(F32)
                    emb_ref[pl.ds(slot, 1), :] += part_ref[row, 64:72, :].astype(F32)[0:1, :]

            loop(part_ref.shape[0], body)

    first = len(tables) + 1 + len(parts)
    return pl.pallas_call(
        kernel,
        out_shape=[jax.ShapeDtypeStruct(dens.shape, F32), jax.ShapeDtypeStruct(emb.shape, F32)],
        in_specs=[SMEM] * (len(tables) + 1) + [VMEM] * (len(parts) + 2),
        out_specs=[VMEM, VMEM],
        input_output_aliases={first: 0, first + 1: 1},
        name="add_up",
    )(*tables, me, *parts, dens, emb)


def take(half, me, parts, row, stacked, dens):
    for n in range(8):
        lanes = slice(n * 128, n * 128 + 128)
        at = pl.multiple_of(lax.bitwise_xor(me, n) * 32, 32)
        stacked[half : half + 256, lanes] = parts[n][row, 0:256, :]
        dens[pl.ds(half + at, 32), 0:128] = parts[n][row, 256:288, :]
        dens[pl.ds(half + at, 32), 128:256] = parts[n][row, 288:320, :]


def one_dimer(steps, me, load, outs, scratch):
    stacked, weighted, dens, current, squares = scratch

    @pl.when(steps > 0)
    def _():
        load()
        fits = []
        for half in (0, 256):
            block = dens[half : half + 256, :]
            sums = []
            for n in range(4):
                lanes = slice(n * 256, n * 256 + 256)
                factor = stacked[half : half + 256, lanes]
                projected = jnp.dot(block, factor, preferred_element_type=F32)
                sums.append(jnp.sum(factor.astype(F32) * projected, axis=0, keepdims=True))
            fits.append(jnp.concatenate(sums, axis=1).astype(BF16).astype(F32))
        coeff = fits[0] + fits[1]

        def weigh(n):
            rows = pl.ds(pl.multiple_of(n * 64, 64), 64)
            weighted[rows, :] = (stacked[rows, :].astype(F32) * coeff).astype(BF16)

        loop(8, weigh)
        for n in range(4):
            rows = slice(n * 128, n * 128 + 128)
            coulomb = lax.dot_general(
                weighted[rows, :], stacked[...], (((1,), (1,)), ((), ())), preferred_element_type=F32
            )
            row_at = lax.broadcasted_iota(jnp.int32, (128, 512), 0) + n * 128
            col_at = lax.broadcasted_iota(jnp.int32, (128, 512), 1)
            own = dens[rows, :].astype(F32)
            blank = jnp.zeros((128, 256), F32)
            wide = jnp.concatenate([own, blank] if n < 2 else [blank, own], axis=1)
            eye = jnp.where(row_at == col_at, 0.5, 0.0)
            current[rows, :] = (eye + wide + COUPLE * coulomb).astype(BF16)

        def purify(index, unused):

            def block(n):
                rows = pl.ds(pl.multiple_of(n * 128, 128), 128)
                square = jnp.dot(current[rows, :], current[...], preferred_element_type=F32)
                cube = jnp.dot(square.astype(BF16), current[...], preferred_element_type=F32)
                squares[rows, :] = (3.0 * square - 2.0 * cube).astype(BF16)

            for n in range(4):
                block(n)
            current[...] = squares[...]
            return unused

        lax.fori_loop(0, steps, purify, 0)
        row_at = lax.broadcasted_iota(jnp.int32, (256, 256), 0)
        col_at = lax.broadcasted_iota(jnp.int32, (256, 256), 1)
        eye = jnp.where(row_at == col_at, 0.5, 0.0)
        for half in (0, 256):
            own = slice(half, half + 256)
            change = current[own, own].astype(F32) - dens[own, :].astype(F32) - eye
            dens[own, :] = change.astype(BF16)
        for n in range(8):
            at = pl.multiple_of(lax.bitwise_xor(me, n) * 32, 32)
            lanes = slice(n * 128, n * 128 + 128)
            for r in range(2):
                change = dens[pl.ds(r * 256 + at, 32), :]
                outs[n][r, 0:32, :] = change[:, 0:128]
                outs[n][r, 32:64, :] = change[:, 128:256]
                partner = jnp.broadcast_to(fits[1 - r][:, lanes], (8, 128))
                outs[n][r, 64:72, :] = partner.astype(BF16)


SCRATCH = [
    pltpu.VMEM((512, 1024), BF16),
    pltpu.VMEM((512, 1024), BF16),
    pltpu.VMEM((512, 256), BF16),
    pltpu.VMEM((512, 512), BF16),
    pltpu.VMEM((512, 512), BF16),
]


def run_dimers(kernel, count, tables, blocks, maps, parts):
    shape = jax.ShapeDtypeStruct((2 * count, 72, 128), BF16)
    specs = []
    for block, index_map in zip(blocks, maps, strict=True):
        specs += [pl.BlockSpec((block, 320, 128), index_map)] * 8
    return pl.pallas_call(
        kernel,
        out_shape=[shape] * 8,
        grid_spec=pltpu.PrefetchScalarGridSpec(
            num_scalar_prefetch=2,
            grid=(count,),
            in_specs=specs,
            out_specs=[pl.BlockSpec((2, 72, 128), lambda i, *_: (i, 0, 0))] * 8,
            scratch_shapes=SCRATCH,
        ),
        name="dimers",
        cost_estimate=pl.CostEstimate(
            flops=count * 4_000_000_000, bytes_accessed=count * 1_500_000, transcendentals=0
        ),
    )(*tables, *parts)


def kernel_1(table_ref, me_ref, *refs):
    me, i = me_ref[0], pl.program_id(0)
    first, second, outs, scratch = refs[0:8], refs[8:16], refs[16:24], refs[24:]
    stacked, dens = scratch[0], scratch[2]

    def load():
        take(0, me, first, 0, stacked, dens)
        take(256, me, second, 0, stacked, dens)

    other = table_ref[RANKED + ranked_at(me, i)]
    one_dimer(table_ref[STEP1 + other], me, load, outs, scratch)


def kernel_2(table_ref, me_ref, *refs):
    me, i = me_ref[0], pl.program_id(0)
    home, late, outs, scratch = refs[0:8], refs[8:16], refs[16:24], refs[24:]
    stacked, dens = scratch[0], scratch[2]
    split = table_ref[MODE + me] > 0

    def load():
        both_late = split & (i == 0)
        both_home = split & (i == 1)

        @pl.when(both_late)
        def _():
            take(0, me, late, 0, stacked, dens)

        @pl.when(jnp.logical_not(both_late))
        def _():
            take(0, me, home, jnp.where(split, 0, i), stacked, dens)

        @pl.when(both_home)
        def _():
            take(256, me, home, 1, stacked, dens)

        @pl.when(jnp.logical_not(both_home))
        def _():
            take(256, me, late, jnp.where(split, 1, i), stacked, dens)

    one_dimer(table_ref[STEPS + 2 * me + i], me, load, outs, scratch)


def plan_kernel(me_ref, inside_ref, count_ref, list_ref, table_ref, left_ref, to_x, to_z, n_direct, n_third, n_self):
    me = me_ref[0]

    def clear(n):
        to_z[n] = 0
        table_ref[n] = jnp.where(n < STEPS, -1, 0)

    def clear_x(n):
        to_x[n] = 0

    def clear_c(n):
        n_direct[n] = 0
        n_third[n] = 0
        n_self[n] = 0

    loop(TABLE, clear)
    loop(128, clear_x)
    loop(32, clear_c)

    def put(at, good, spare, value):
        table_ref[jnp.where(good, at, spare)] = value

    def can(o, c, extra=0):
        xo, zo, xc, zc = o >> 3, o & 7, c >> 3, c & 7
        return ((xo == xc) | (to_x[o * 4 + xc] < KX)) & ((zo == zc) | (to_z[xc * 64 + zo * 8 + zc] + extra < KZ))

    def send(o, slot, c):
        xo, zo, xc, zc = o >> 3, o & 7, c >> 3, c & 7
        at_x, at_z = o * 4 + xc, xc * 64 + zo * 8 + zc
        n_x, n_z = to_x[at_x], to_z[at_z]
        move_x, move_z = xo != xc, zo != zc
        to_x[at_x] = n_x + jnp.where(move_x, 1, 0)
        to_z[at_z] = n_z + jnp.where(move_z, 1, 0)
        in_x = (lax.bitwise_xor(xo, xc) - 1) * KX + n_x
        put(SENT + in_x, move_x & (o == me), SENT + 31, slot)
        put(RELAY + zc * KZ + n_z, move_z & (xc * 8 + zo == me), RELAY + 31, jnp.where(move_x, 32 + in_x, slot))
        return jnp.where(move_z, 32 + NX + zo * KZ + n_z, 32 + in_x)

    def visit(d):
        word = list_ref[d]
        a, b, cost = word & 1023, (word >> 10) & 1023, word >> 20
        oa, ob, la, lb = a >> 5, b >> 5, a & 31, b & 31
        left_ref[d] = 0

        @pl.when(oa == ob)
        def _():
            q = n_self[oa]

            @pl.when(q < 8)
            def _():
                n_self[oa] = q + 1

                @pl.when(oa == me)
                def _():
                    at = 2 * (7 - q)
                    table_ref[POS + 2 * at + 2] = la
                    table_ref[POS + 2 * at + 3] = lb
                    table_ref[HOME + at] = la
                    table_ref[HOME + at + 1] = lb
                    table_ref[STEPS + at + 1] = cost
                    table_ref[MODE + 7 - q] = 1

            @pl.when(q >= 8)
            def _():
                left_ref[d] = 1

        @pl.when(oa != ob)
        def _():
            n_a, n_b = n_direct[oa], n_direct[ob]
            fit_a = ((n_a + 2) >> 1) + jnp.maximum(n_third[oa], inside_ref[oa]) <= 8
            fit_b = ((n_b + 2) >> 1) + jnp.maximum(n_third[ob], inside_ref[ob]) <= 8
            can_a, can_b = can(ob, oa) & fit_a, can(oa, ob) & fit_b
            full_a = to_z[(oa >> 3) * 64 + (ob & 7) * 8 + (oa & 7)] * 4 + n_a
            full_b = to_z[(ob >> 3) * 64 + (oa & 7) * 8 + (ob & 7)] * 4 + n_b
            use_a = can_a & (jnp.logical_not(can_b) | (full_a <= full_b))
            direct = can_a | can_b

            @pl.when(direct)
            def _():
                c, o = jnp.where(use_a, oa, ob), jnp.where(use_a, ob, oa)
                stay, move = jnp.where(use_a, la, lb), jnp.where(use_a, lb, la)
                at = jnp.where(use_a, n_a, n_b)
                n_direct[c] = at + 1
                late = send(o, move, c)

                @pl.when(c == me)
                def _():
                    table_ref[POS + 2 * at] = stay
                    table_ref[POS + 2 * at + 1] = late
                    table_ref[HOME + at] = stay
                    table_ref[LATE + at] = late
                    table_ref[STEPS + at] = cost

            @pl.when(jnp.logical_not(direct))
            def _():
                same_z = jnp.where((oa & 7) == (ob & 7), 1, 0)

                def look(carry):
                    n, _ = carry
                    c = (d + n) & 31
                    fit = ((n_direct[c] + 1) >> 1) + jnp.maximum(n_third[c] + 1, inside_ref[c]) <= 8
                    good = fit & can(oa, c, same_z) & can(ob, c, same_z) & (c != oa) & (c != ob)
                    return n + 1, jnp.where(good, c, -1)

                _, c = lax.while_loop(
                    lambda carry: (carry[0] < 32) & (carry[1] < 0), look, (jnp.int32(0), jnp.int32(-1))
                )

                @pl.when(c < 0)
                def _():
                    left_ref[d] = 1

                @pl.when(c >= 0)
                def _():
                    t = n_third[c]
                    n_third[c] = t + 1
                    late_a = send(oa, la, c)
                    late_b = send(ob, lb, c)

                    @pl.when(c == me)
                    def _():
                        at = 2 * (7 - t)
                        table_ref[POS + 2 * at] = late_a
                        table_ref[POS + 2 * at + 1] = late_b
                        table_ref[LATE + at] = late_a
                        table_ref[LATE + at + 1] = late_b
                        table_ref[STEPS + at] = cost
                        table_ref[MODE + 7 - t] = 1

    loop(count_ref[0], visit)


def plan_rest(me, inside_count, count, words):
    s32 = jnp.int32
    return pl.pallas_call(
        plan_kernel,
        out_shape=[jax.ShapeDtypeStruct((TABLE,), s32), jax.ShapeDtypeStruct(words.shape, s32)],
        in_specs=[SMEM] * 4,
        out_specs=[SMEM] * 2,
        scratch_shapes=[pltpu.SMEM((128,), s32), pltpu.SMEM((256,), s32)] + [pltpu.SMEM((32,), s32)] * 3,
        name="plan",
        cost_estimate=pl.CostEstimate(flops=1000, bytes_accessed=30_000_000, transcendentals=0),
    )(me, inside_count, count, words)


def exchange(parts):
    got = [parts[0]]
    for k in range(1, 8):
        got.append(lax.ppermute(parts[k], "basis", [(i, i ^ k) for i in range(8)]))
    return got


def along_x(parts):
    return [lax.ppermute(parts[k - 1], "frag", [(i, i ^ (8 * k)) for i in range(32)]) for k in (1, 2, 3)]


def along_z(part):
    groups = [[8 * x + z for z in range(8)] for x in range(4)]
    return lax.all_to_all(part, "frag", 0, 0, tiled=True, axis_index_groups=groups)


def across(part):
    return lax.all_to_all(part, "frag", split_axis=0, concat_axis=0, tiled=True)


def after(value, *others):
    return lax.optimization_barrier((value, others))[0]


def shards(density, aux_factor, pairs, slot_of, costs):
    n_frag = lax.axis_size("frag")
    n_basis = lax.axis_size("basis")
    me_frag = lax.axis_index("frag").astype(jnp.int32)
    me_basis = lax.axis_index("basis").astype(jnp.int32)
    dimers = pairs.shape[0] * n_frag * n_basis

    lookup = pairs[:, :, None] == jnp.arange(slot_of.shape[0], dtype=jnp.int32)
    slots = jnp.sum(jnp.where(lookup, slot_of, 0), axis=2)
    mine = jnp.concatenate([slots[:, 0], slots[:, 1], costs, jnp.zeros(116, jnp.int32)])
    column = lax.all_to_all(
        jnp.broadcast_to(mine, (n_basis, 1, 128)), "basis", split_axis=0, concat_axis=0, tiled=True
    )
    column = column[:, 0, 0:12].reshape(n_basis, 3, 4).transpose(1, 0, 2).reshape(96)
    column = jnp.concatenate([column, jnp.zeros(32, jnp.int32)])
    every = across(jnp.broadcast_to(column, (n_frag, 1, 128)))
    a = every[:, 0, 0:32].reshape(dimers)
    b = every[:, 0, 32:64].reshape(dimers)
    cost = every[:, 0, 64:96].reshape(dimers)

    order = jnp.arange(dimers, dtype=jnp.int32)
    columns = jnp.arange(n_frag, dtype=jnp.int32)
    own_a, own_b = a // 32, b // 32
    low, high = jnp.minimum(own_a, own_b), jnp.maximum(own_a, own_b)
    pair_id = low * 32 + high
    inside = own_a == own_b
    mine_a = (own_a == me_frag) & jnp.logical_not(inside)
    mine_b = (own_b == me_frag) & jnp.logical_not(inside)
    other = jnp.where(mine_a, own_b, jnp.where(mine_b, own_a, -1))
    local = jnp.where(mine_a, a, b) & 31
    key = order * 256 + local * 8 + cost
    word = a + b * 1024 + cost * 1048576
    me_f, me_b = me_frag.reshape(1), me_basis.reshape(1)
    keep_first = (me_frag < columns) == ((me_frag + columns) % 2 == 0)
    home = (aux_factor, density)

    def one_round(carry):
        return body_round(carry)

    def body_round(carry):
        _, rest, dens, emb = carry
        open_dimer = rest > 0
        match = (other[None, :] == columns[:, None]) & open_dimer[None, :]
        keyed = jnp.where(match, key[None, :], BIG)
        key_0 = jnp.min(keyed, axis=1)
        key_1 = jnp.min(jnp.where(keyed > key_0[:, None], keyed, BIG), axis=1)
        here = jnp.where(keep_first, key_0, key_1)
        there = jnp.where(keep_first, key_1, key_0)
        send_1 = jnp.where(there < BIG, (there >> 3) & 31, -1)
        base_1 = jnp.where(here < BIG, (here >> 3) & 31, -1)
        steps_1 = jnp.where(here < BIG, here & 7, 0)

        (out_1,) = pack((send_1,), me_b, lambda t, me, n, row: t[0][row], 1, 32, home, [])
        in_1 = across(out_1)

        weight = steps_1 * 64 - columns
        rank = jnp.sum((weight[None, :] > weight[:, None]).astype(jnp.int32), axis=1)
        ranked = jnp.sum(jnp.where(rank[None, :] == columns[:, None], columns[None, :], 0), axis=1)
        table_1 = jnp.concatenate([send_1, base_1, steps_1, ranked])

        earlier = (pair_id[:, None] == pair_id[None, :]) & (order[None, :] < order[:, None])
        earlier = jnp.sum(jnp.where(earlier & open_dimer[None, :], 1, 0), axis=1)
        flagged = open_dimer & ((earlier >= 2) | inside)
        ahead = jnp.sum(jnp.where((order[None, :] < order[:, None]) & flagged[None, :], 1, 0), axis=1)
        ahead = jnp.where(flagged, ahead, -1)
        words = jnp.sum(jnp.where(ahead[None, :] == order[:, None], word[None, :], 0), axis=1)
        count = jnp.sum(jnp.where(flagged, 1, 0)).reshape(1)
        inside_here = (own_a[None, :] == columns[:, None]) & (inside & open_dimer)[None, :]
        inside_count = jnp.sum(jnp.where(inside_here, 1, 0), axis=1)
        table_2, listed = plan_rest(me_f, inside_count, count, words)
        listed = jnp.where(order < count, listed, 0)
        left = jnp.sum(jnp.where(ahead[:, None] == order[None, :], listed[None, :], 0), axis=1)
        tables = (table_1, table_2)

        def served(t, me, n, row):
            return t[0][RANKED + ranked_at(lax.bitwise_xor(me, n), row)]

        home_1 = exchange(
            pack(tables[:1], me_b, lambda t, me, n, row: t[0][BASE + served(t, me, n, row)], 8, 4, home, [])
        )
        in_x = along_x(pack(tables, me_b, lambda t, me, n, row: t[1][SENT + n * KX + row], 3, KX, home, []))
        (out_2,) = pack(tables, me_b, lambda t, me, n, row: t[1][RELAY + row], 1, NZ, home, in_x)
        in_z = along_z(after(out_2, in_1, home_1))
        home_2 = exchange(
            pack(
                tables, me_b, lambda t, me, n, row: t[1][HOME + 2 * lax.bitwise_xor(me, n) + row], 8, 2, home, []
            )
        )

        away_1 = exchange(pack(tables, me_b, served, 8, 4, (), [after(in_1, home_2)]))
        one = lambda i, *_: (i, 0, 0)
        done_1 = exchange(
            run_dimers(kernel_1, 4, (table_1, me_b), (1, 1), (one, one), [*home_1, *away_1])
        )

        late_parts = pack(
            tables,
            me_b,
            lambda t, me, n, row: t[1][LATE + 2 * lax.bitwise_xor(me, n) + row] - 32,
            8,
            2,
            (),
            [*in_x, after(in_z, away_1)],
        )
        late_2 = exchange(late_parts)
        done_1 = after(done_1, late_parts)
        whole = lambda i, *_: (0, 0, 0)
        done_2 = exchange(
            run_dimers(kernel_2, 2, (table_2, me_b), (2, 2), (whole, whole), [*home_2, *late_2])
        )

        def back_to(k):
            return lambda t, me, row: jnp.where(row % 2 == 1, served(t, me, k, row // 2), -1)

        (ret_1,) = place(tables, me_b, done_1, [back_to(k) for k in range(8)], [32])
        back_1 = across(ret_1)

        def place_2(t, me, k, row):
            at = 2 * lax.bitwise_xor(me, k) + row // 2
            return jnp.where(t[1][STEPS + at] > 0, t[1][POS + 2 * at + row % 2], -1)

        def back_z(k):
            return lambda t, me, row: place_2(t, me, k, row) - 32 - NX

        def back_x(k):
            return lambda t, me, row: place_2(t, me, k, row) - 32

        (ret_z,) = place(tables, me_b, done_2, [back_z(k) for k in range(8)], [NZ])
        rest_z = along_z(after(ret_z, back_1))
        ret_x = place(
            tables,
            me_b,
            [*done_2, rest_z],
            [back_x(k) for k in range(8)] + [lambda t, me, row: t[1][RELAY + row] - 32],
            [KX] * 3,
        )
        rest_x = along_x(ret_x)

        def stay_1(k):
            return lambda t, me, row: jnp.where(row % 2 == 0, t[0][BASE + served(t, me, k, row // 2)], -1)

        def stay_2(k):
            return lambda t, me, row: place_2(t, me, k, row)

        def from_x(k):
            return lambda t, me, row: t[1][SENT + k * KX + row]

        finds = (
            [stay_1(k) for k in range(8)]
            + [stay_2(k) for k in range(8)]
            + [lambda t, me, row: t[0][OUT + row]]
        )
        dens, emb = add_up(tables, me_b, [*done_1, *done_2, back_1], finds, dens, emb)
        finds = [lambda t, me, row: t[1][RELAY + row]] + [from_x(k) for k in range(3)]
        dens, emb = add_up(tables, me_b, [rest_z, *rest_x], finds, dens, emb)
        return jnp.sum(left), left, dens, emb

    start = (
        jnp.int32(dimers),
        jnp.ones(dimers, jnp.int32),
        jnp.zeros(density.shape, F32),
        jnp.zeros((density.shape[0], aux_factor.shape[2]), F32),
    )
    _, _, dens, emb = lax.while_loop(lambda carry: carry[0] > 0, one_round, start)
    return dens, emb


def solution(mesh):
    return jax.shard_map(
        shards,
        mesh=mesh,
        in_specs=(
            P("frag", "basis", None),
            P("frag", None, "basis"),
            P(("frag", "basis"), None),
            P(),
            P(("frag", "basis")),
        ),
        out_specs=(P("frag", "basis", None), P("frag", "basis")),
        check_vma=False,
    )
```

```python
import jax
import jax.numpy as jnp
from jax import lax
from jax.experimental import pallas as pl
from jax.experimental.pallas import tpu as pltpu
from jax.sharding import PartitionSpec as P


COUPLE = 0.015625
BIG = 1 << 30
BF16 = jnp.bfloat16
F32 = jnp.float32
KX, KZ = 6, 2
NX, NZ = 3 * KX, 8 * KZ
SENT, RELAY, POS, HOME, LATE, STEPS, MODE, TABLE = 0, 32, 64, 128, 160, 192, 224, 256
OUT, BASE, STEP1, RANKED = 0, 32, 64, 96

VMEM = pl.BlockSpec(memory_space=pltpu.VMEM)
SMEM = pl.BlockSpec(memory_space=pltpu.SMEM)


def loop(count, body):
    def step(n, unused):
        body(n)
        return unused

    lax.fori_loop(0, count, step, 0)


def ranked_at(device, place):
    return place * 8 + jnp.where(place % 2 == 0, device, 7 - device)


def pack(tables, me, find, outs, rows, home, items):
    sizes = ([32] if home else []) + [item.shape[0] for item in items]

    def kernel(*refs):
        table_refs, me_ref, refs = refs[: len(tables)], refs[len(tables)], refs[len(tables) + 1 :]
        sources, out_refs = refs[: len(refs) - outs], refs[len(refs) - outs :]
        for n, out_ref in enumerate(out_refs):

            def body(row, n=n, out_ref=out_ref):
                at = jnp.maximum(find(table_refs, me_ref[0], n, row), 0)
                base, left = 0, list(sources)
                for which, size in enumerate(sizes):
                    here = (at >= base) & (at < base + size)
                    if home and which == 0:
                        aux_ref, den_ref = left.pop(0), left.pop(0)

                        @pl.when(here)
                        def _(aux_ref=aux_ref, den_ref=den_ref):
                            out_ref[row, 0:256, :] = aux_ref[at]
                            block = den_ref[at]
                            out_ref[row, 256:288, :] = block[:, 0:128]
                            out_ref[row, 288:320, :] = block[:, 128:256]
                    else:
                        item_ref = left.pop(0)

                        @pl.when(here)
                        def _(item_ref=item_ref, base=base):
                            out_ref[row] = item_ref[at - base]

                    base += size

            loop(rows, body)

    sources = list(home) + list(items)
    return pl.pallas_call(
        kernel,
        out_shape=[jax.ShapeDtypeStruct((rows, 320, 128), BF16)] * outs,
        in_specs=[SMEM] * (len(tables) + 1) + [VMEM] * len(sources),
        out_specs=[VMEM] * outs,
        name="pack",
    )(*tables, me, *sources)


def place(tables, me, parts, finds, out_rows):
    def kernel(*refs):
        table_refs, me_ref, refs = refs[: len(tables)], refs[len(tables)], refs[len(tables) + 1 :]
        for part_ref, find in zip(refs[: len(parts)], finds, strict=True):

            def body(row, part_ref=part_ref, find=find):
                at = find(table_refs, me_ref[0], row)
                base = 0
                for out_ref, size in zip(refs[len(parts) :], out_rows, strict=True):

                    @pl.when((at >= base) & (at < base + size))
                    def _(out_ref=out_ref, base=base):
                        out_ref[at - base] = part_ref[row]

                    base += size

            loop(part_ref.shape[0], body)

    return pl.pallas_call(
        kernel,
        out_shape=[jax.ShapeDtypeStruct((size, 72, 128), BF16) for size in out_rows],
        in_specs=[SMEM] * (len(tables) + 1) + [VMEM] * len(parts),
        out_specs=[VMEM] * len(out_rows),
        name="place",
    )(*tables, me, *parts)


def add_up(tables, me, parts, finds, dens, emb):
    def kernel(*refs):
        table_refs, me_ref, refs = refs[: len(tables)], refs[len(tables)], refs[len(tables) + 1 :]
        dens_in, emb_in, dens_ref, emb_ref = refs[len(parts) :]
        dens_ref[...] = dens_in[...]
        emb_ref[...] = emb_in[...]
        for part_ref, find in zip(refs[: len(parts)], finds, strict=True):

            def body(row, part_ref=part_ref, find=find):
                slot = find(table_refs, me_ref[0], row)

                @pl.when((slot >= 0) & (slot < 32))
                def _():
                    dens_ref[slot, :, 0:128] += part_ref[row, 0:32, :].astype(F32)
                    dens_ref[slot, :, 128:256] += part_ref[row, 32:64, :].astype(F32)
                    emb_ref[pl.ds(slot, 1), :] += part_ref[row, 64:72, :].astype(F32)[0:1, :]

            loop(part_ref.shape[0], body)

    first = len(tables) + 1 + len(parts)
    return pl.pallas_call(
        kernel,
        out_shape=[jax.ShapeDtypeStruct(dens.shape, F32), jax.ShapeDtypeStruct(emb.shape, F32)],
        in_specs=[SMEM] * (len(tables) + 1) + [VMEM] * (len(parts) + 2),
        out_specs=[VMEM, VMEM],
        input_output_aliases={first: 0, first + 1: 1},
        name="add_up",
    )(*tables, me, *parts, dens, emb)


def take(half, me, parts, row, stacked, dens):
    for n in range(8):
        lanes = slice(n * 128, n * 128 + 128)
        at = pl.multiple_of(lax.bitwise_xor(me, n) * 32, 32)
        stacked[half : half + 256, lanes] = parts[n][row, 0:256, :]
        dens[pl.ds(half + at, 32), 0:128] = parts[n][row, 256:288, :]
        dens[pl.ds(half + at, 32), 128:256] = parts[n][row, 288:320, :]


def one_dimer(steps, me, load, outs, scratch):
    stacked, weighted, dens, current, squares = scratch

    @pl.when(steps > 0)
    def _():
        load()
        fits = []
        for half in (0, 256):
            block = dens[half : half + 256, :]
            sums = []
            for n in range(4):
                lanes = slice(n * 256, n * 256 + 256)
                factor = stacked[half : half + 256, lanes]
                projected = jnp.dot(block, factor, preferred_element_type=F32)
                sums.append(jnp.sum(factor.astype(F32) * projected, axis=0, keepdims=True))
            fits.append(jnp.concatenate(sums, axis=1).astype(BF16).astype(F32))
        coeff = fits[0] + fits[1]

        def weigh(n):
            rows = pl.ds(pl.multiple_of(n * 64, 64), 64)
            weighted[rows, :] = (stacked[rows, :].astype(F32) * coeff).astype(BF16)

        loop(8, weigh)
        for n in range(4):
            rows = slice(n * 128, n * 128 + 128)
            coulomb = lax.dot_general(
                weighted[rows, :], stacked[...], (((1,), (1,)), ((), ())), preferred_element_type=F32
            )
            row_at = lax.broadcasted_iota(jnp.int32, (128, 512), 0) + n * 128
            col_at = lax.broadcasted_iota(jnp.int32, (128, 512), 1)
            own = dens[rows, :].astype(F32)
            blank = jnp.zeros((128, 256), F32)
            wide = jnp.concatenate([own, blank] if n < 2 else [blank, own], axis=1)
            eye = jnp.where(row_at == col_at, 0.5, 0.0)
            current[rows, :] = (eye + wide + COUPLE * coulomb).astype(BF16)

        def purify(index, unused):

            def block(n):
                rows = pl.ds(pl.multiple_of(n * 128, 128), 128)
                square = jnp.dot(current[rows, :], current[...], preferred_element_type=F32)
                cube = jnp.dot(square.astype(BF16), current[...], preferred_element_type=F32)
                squares[rows, :] = (3.0 * square - 2.0 * cube).astype(BF16)

            for n in range(4):
                block(n)
            current[...] = squares[...]
            return unused

        lax.fori_loop(0, steps, purify, 0)
        row_at = lax.broadcasted_iota(jnp.int32, (256, 256), 0)
        col_at = lax.broadcasted_iota(jnp.int32, (256, 256), 1)
        eye = jnp.where(row_at == col_at, 0.5, 0.0)
        for half in (0, 256):
            own = slice(half, half + 256)
            change = current[own, own].astype(F32) - dens[own, :].astype(F32) - eye
            dens[own, :] = change.astype(BF16)
        for n in range(8):
            at = pl.multiple_of(lax.bitwise_xor(me, n) * 32, 32)
            lanes = slice(n * 128, n * 128 + 128)
            for r in range(2):
                change = dens[pl.ds(r * 256 + at, 32), :]
                outs[n][r, 0:32, :] = change[:, 0:128]
                outs[n][r, 32:64, :] = change[:, 128:256]
                partner = jnp.broadcast_to(fits[1 - r][:, lanes], (8, 128))
                outs[n][r, 64:72, :] = partner.astype(BF16)


SCRATCH = [
    pltpu.VMEM((512, 1024), BF16),
    pltpu.VMEM((512, 1024), BF16),
    pltpu.VMEM((512, 256), BF16),
    pltpu.VMEM((512, 512), BF16),
    pltpu.VMEM((512, 512), BF16),
]


def run_dimers(kernel, count, tables, blocks, maps, parts):
    shape = jax.ShapeDtypeStruct((2 * count, 72, 128), BF16)
    specs = []
    for block, index_map in zip(blocks, maps, strict=True):
        specs += [pl.BlockSpec((block, 320, 128), index_map)] * 8
    return pl.pallas_call(
        kernel,
        out_shape=[shape] * 8,
        grid_spec=pltpu.PrefetchScalarGridSpec(
            num_scalar_prefetch=2,
            grid=(count,),
            in_specs=specs,
            out_specs=[pl.BlockSpec((2, 72, 128), lambda i, *_: (i, 0, 0))] * 8,
            scratch_shapes=SCRATCH,
        ),
        name="dimers",
        cost_estimate=pl.CostEstimate(
            flops=count * 4_000_000_000, bytes_accessed=count * 1_500_000, transcendentals=0
        ),
    )(*tables, *parts)


def kernel_1(table_ref, me_ref, *refs):
    me, i = me_ref[0], pl.program_id(0)
    first, second, outs, scratch = refs[0:8], refs[8:16], refs[16:24], refs[24:]
    stacked, dens = scratch[0], scratch[2]

    def load():
        take(0, me, first, 0, stacked, dens)
        take(256, me, second, 0, stacked, dens)

    other = table_ref[RANKED + ranked_at(me, i)]
    one_dimer(table_ref[STEP1 + other], me, load, outs, scratch)


def kernel_2(table_ref, me_ref, *refs):
    me, i = me_ref[0], pl.program_id(0)
    home, late, outs, scratch = refs[0:8], refs[8:16], refs[16:24], refs[24:]
    stacked, dens = scratch[0], scratch[2]
    split = table_ref[MODE + me] > 0

    def load():
        both_late = split & (i == 0)
        both_home = split & (i == 1)

        @pl.when(both_late)
        def _():
            take(0, me, late, 0, stacked, dens)

        @pl.when(jnp.logical_not(both_late))
        def _():
            take(0, me, home, jnp.where(split, 0, i), stacked, dens)

        @pl.when(both_home)
        def _():
            take(256, me, home, 1, stacked, dens)

        @pl.when(jnp.logical_not(both_home))
        def _():
            take(256, me, late, jnp.where(split, 1, i), stacked, dens)

    one_dimer(table_ref[STEPS + 2 * me + i], me, load, outs, scratch)


def plan_kernel(me_ref, inside_ref, count_ref, list_ref, table_ref, left_ref, to_x, to_z, n_direct, n_third, n_self, n_split, room):
    me = me_ref[0]
    me_x, me_z = me >> 3, me & 7

    def clear(n):
        for i in range(8):
            to_z[n * 8 + i] = 0
            table_ref[n * 8 + i] = jnp.where(n < STEPS // 8, -1, 0)

    def clear_x(n):
        for i in range(8):
            to_x[n * 8 + i] = 0

    def clear_c(n):
        n_direct[n] = 0
        n_third[n] = 0
        n_self[n] = 0
        n_split[n] = inside_ref[n]
        room[n] = 1 + inside_ref[n]

    loop(TABLE // 8, clear)
    loop(16, clear_x)
    loop(32, clear_c)

    def put(at, good, spare, value):
        table_ref[jnp.where(good, at, spare)] = value

    def can(o, c, extra):
        zo, xc, zc = o & 7, c >> 3, c & 7
        return (to_x[o * 4 + xc] < KX) & ((zo == zc) | (to_z[xc * 64 + zo * 8 + zc] + extra < KZ))

    def send(o, slot, c, at_x, at_z, n_x, n_z):
        xo, zo, xc, zc = o >> 3, o & 7, c >> 3, c & 7
        move_x, move_z = xo != xc, zo != zc
        to_x[at_x] = n_x + jnp.where(move_x, 1, 0)
        to_z[at_z] = n_z + jnp.where(move_z, 1, 0)
        in_x = (lax.bitwise_xor(xo, xc) - 1) * KX + n_x

        @pl.when(zo == me_z)
        def _():
            put(SENT + in_x, move_x & (o == me), SENT + 31, slot)
            put(RELAY + zc * KZ + n_z, move_z & (xc == me_x), RELAY + 31, jnp.where(move_x, 32 + in_x, slot))

        return jnp.where(move_z, 32 + NX + zo * KZ + n_z, 32 + in_x)

    def visit(d):
        word = list_ref[d]
        cost = word >> 20
        la, oa, lb, ob = word & 31, (word >> 5) & 31, (word >> 10) & 31, (word >> 15) & 31
        left_ref[d] = 0
        za, xa, zb, xb = oa & 7, oa >> 3, ob & 7, ob >> 3
        x_at_a, z_at_a = ob * 4 + xa, xa * 64 + zb * 8 + za
        x_at_b, z_at_b = oa * 4 + xb, xb * 64 + za * 8 + zb
        x_a, z_a, x_b, z_b = to_x[x_at_a], to_z[z_at_a], to_x[x_at_b], to_z[z_at_b]
        room_a, room_b = room[oa], room[ob]
        can_a = (x_a < KX) & (z_a < KZ) & (room_a <= 8)
        can_b = (x_b < KX) & (z_b < KZ) & (room_b <= 8)
        use_a = can_a & (jnp.logical_not(can_b) | (z_a * 4 + room_a <= z_b * 4 + room_b))
        apart = oa != ob
        direct = apart & (can_a | can_b)

        @pl.when(direct)
        def _():
            c, o = jnp.where(use_a, oa, ob), jnp.where(use_a, ob, oa)
            stay, move = jnp.where(use_a, la, lb), jnp.where(use_a, lb, la)
            at = n_direct[c]
            n_direct[c] = at + 1
            room[c] = ((at + 3) >> 1) + n_split[c]
            late = send(
                o,
                move,
                c,
                jnp.where(use_a, x_at_a, x_at_b),
                jnp.where(use_a, z_at_a, z_at_b),
                jnp.where(use_a, x_a, x_b),
                jnp.where(use_a, z_a, z_b),
            )

            @pl.when(c == me)
            def _():
                table_ref[POS + 2 * at] = stay
                table_ref[POS + 2 * at + 1] = late
                table_ref[HOME + at] = stay
                table_ref[LATE + at] = late
                table_ref[STEPS + at] = cost

        @pl.when(jnp.logical_not(direct))
        def _():
            @pl.when(jnp.logical_not(apart))
            def _():
                q = n_self[oa]

                @pl.when(q < 8)
                def _():
                    n_self[oa] = q + 1

                    @pl.when(oa == me)
                    def _():
                        at = 2 * (7 - q)
                        table_ref[POS + 2 * at + 2] = la
                        table_ref[POS + 2 * at + 3] = lb
                        table_ref[HOME + at] = la
                        table_ref[HOME + at + 1] = lb
                        table_ref[STEPS + at + 1] = cost
                        table_ref[MODE + 7 - q] = 1

                @pl.when(q >= 8)
                def _():
                    left_ref[d] = 1

            @pl.when(apart)
            def _():
                same_z = jnp.where(za == zb, 1, 0)

                def look(carry):
                    n, _ = carry
                    c = (d + n) & 31
                    fit = ((n_direct[c] + 1) >> 1) + jnp.maximum(n_third[c] + 1, inside_ref[c]) <= 8
                    good = fit & can(oa, c, same_z) & can(ob, c, same_z) & (c != oa) & (c != ob)
                    return n + 1, jnp.where(good, c, -1)

                _, c = lax.while_loop(
                    lambda carry: (carry[0] < 32) & (carry[1] < 0), look, (jnp.int32(0), jnp.int32(-1))
                )

                @pl.when(c < 0)
                def _():
                    left_ref[d] = 1

                @pl.when(c >= 0)
                def _():
                    t = n_third[c]
                    n_third[c] = t + 1
                    split = jnp.maximum(t + 1, inside_ref[c])
                    n_split[c] = split
                    room[c] = ((n_direct[c] + 2) >> 1) + split
                    xc, zc = c >> 3, c & 7
                    x_at, z_at = oa * 4 + xc, xc * 64 + za * 8 + zc
                    late_a = send(oa, la, c, x_at, z_at, to_x[x_at], to_z[z_at])
                    x_at, z_at = ob * 4 + xc, xc * 64 + zb * 8 + zc
                    late_b = send(ob, lb, c, x_at, z_at, to_x[x_at], to_z[z_at])

                    @pl.when(c == me)
                    def _():
                        at = 2 * (7 - t)
                        table_ref[POS + 2 * at] = late_a
                        table_ref[POS + 2 * at + 1] = late_b
                        table_ref[LATE + at] = late_a
                        table_ref[LATE + at + 1] = late_b
                        table_ref[STEPS + at] = cost
                        table_ref[MODE + 7 - t] = 1

    loop(count_ref[0], visit)


def plan_rest(me, inside_count, count, words):
    s32 = jnp.int32
    return pl.pallas_call(
        plan_kernel,
        out_shape=[jax.ShapeDtypeStruct((TABLE,), s32), jax.ShapeDtypeStruct(words.shape, s32)],
        in_specs=[SMEM] * 4,
        out_specs=[SMEM] * 2,
        scratch_shapes=[pltpu.SMEM((128,), s32), pltpu.SMEM((256,), s32)] + [pltpu.SMEM((32,), s32)] * 5,
        name="plan",
        cost_estimate=pl.CostEstimate(flops=1000, bytes_accessed=30_000_000, transcendentals=0),
    )(me, inside_count, count, words)


def exchange(parts):
    got = [parts[0]]
    for k in range(1, 8):
        got.append(lax.ppermute(parts[k], "basis", [(i, i ^ k) for i in range(8)]))
    return got


def along_x(parts):
    return [lax.ppermute(parts[k - 1], "frag", [(i, i ^ (8 * k)) for i in range(32)]) for k in (1, 2, 3)]


def along_z(part):
    groups = [[8 * x + z for z in range(8)] for x in range(4)]
    return lax.all_to_all(part, "frag", 0, 0, tiled=True, axis_index_groups=groups)


def across(part):
    return lax.all_to_all(part, "frag", split_axis=0, concat_axis=0, tiled=True)


def after(value, *others):
    return lax.optimization_barrier((value, others))[0]


def shards(density, aux_factor, pairs, slot_of, costs):
    n_frag = lax.axis_size("frag")
    n_basis = lax.axis_size("basis")
    me_frag = lax.axis_index("frag").astype(jnp.int32)
    me_basis = lax.axis_index("basis").astype(jnp.int32)
    dimers = pairs.shape[0] * n_frag * n_basis

    lookup = pairs[:, :, None] == jnp.arange(slot_of.shape[0], dtype=jnp.int32)
    slots = jnp.sum(jnp.where(lookup, slot_of, 0), axis=2)
    mine = jnp.concatenate([slots[:, 0], slots[:, 1], costs, jnp.zeros(116, jnp.int32)])
    column = lax.all_to_all(
        jnp.broadcast_to(mine, (n_basis, 1, 128)), "basis", split_axis=0, concat_axis=0, tiled=True
    )
    column = column[:, 0, 0:12].reshape(n_basis, 3, 4).transpose(1, 0, 2).reshape(96)
    column = jnp.concatenate([column, jnp.zeros(32, jnp.int32)])
    every = across(jnp.broadcast_to(column, (n_frag, 1, 128)))
    a = every[:, 0, 0:32].reshape(dimers)
    b = every[:, 0, 32:64].reshape(dimers)
    cost = every[:, 0, 64:96].reshape(dimers)

    order = jnp.arange(dimers, dtype=jnp.int32)
    columns = jnp.arange(n_frag, dtype=jnp.int32)
    own_a, own_b = a // 32, b // 32
    low, high = jnp.minimum(own_a, own_b), jnp.maximum(own_a, own_b)
    pair_id = low * 32 + high
    inside = own_a == own_b
    mine_a = (own_a == me_frag) & jnp.logical_not(inside)
    mine_b = (own_b == me_frag) & jnp.logical_not(inside)
    other = jnp.where(mine_a, own_b, jnp.where(mine_b, own_a, -1))
    local = jnp.where(mine_a, a, b) & 31
    key = order * 256 + local * 8 + cost
    word = a + b * 1024 + cost * 1048576
    me_f, me_b = me_frag.reshape(1), me_basis.reshape(1)
    keep_first = (me_frag < columns) == ((me_frag + columns) % 2 == 0)
    home = (aux_factor, density)

    def one_round(carry):
        return body_round(carry)

    def body_round(carry):
        _, rest, dens, emb = carry
        open_dimer = rest > 0
        match = (other[None, :] == columns[:, None]) & open_dimer[None, :]
        keyed = jnp.where(match, key[None, :], BIG)
        key_0 = jnp.min(keyed, axis=1)
        key_1 = jnp.min(jnp.where(keyed > key_0[:, None], keyed, BIG), axis=1)
        here = jnp.where(keep_first, key_0, key_1)
        there = jnp.where(keep_first, key_1, key_0)
        send_1 = jnp.where(there < BIG, (there >> 3) & 31, -1)
        base_1 = jnp.where(here < BIG, (here >> 3) & 31, -1)
        steps_1 = jnp.where(here < BIG, here & 7, 0)

        (out_1,) = pack((send_1,), me_b, lambda t, me, n, row: t[0][row], 1, 32, home, [])
        in_1 = across(out_1)

        weight = steps_1 * 64 - columns
        rank = jnp.sum((weight[None, :] > weight[:, None]).astype(jnp.int32), axis=1)
        ranked = jnp.sum(jnp.where(rank[None, :] == columns[:, None], columns[None, :], 0), axis=1)
        table_1 = jnp.concatenate([send_1, base_1, steps_1, ranked])

        earlier = (pair_id[:, None] == pair_id[None, :]) & (order[None, :] < order[:, None])
        earlier = jnp.sum(jnp.where(earlier & open_dimer[None, :], 1, 0), axis=1)
        flagged = open_dimer & ((earlier >= 2) | inside)
        ahead = jnp.sum(jnp.where((order[None, :] < order[:, None]) & flagged[None, :], 1, 0), axis=1)
        ahead = jnp.where(flagged, ahead, -1)
        words = jnp.sum(jnp.where(ahead[None, :] == order[:, None], word[None, :], 0), axis=1)
        count = jnp.sum(jnp.where(flagged, 1, 0)).reshape(1)
        inside_here = (own_a[None, :] == columns[:, None]) & (inside & open_dimer)[None, :]
        inside_count = jnp.sum(jnp.where(inside_here, 1, 0), axis=1)
        table_2, listed = plan_rest(me_f, inside_count, count, words)
        listed = jnp.where(order < count, listed, 0)
        left = jnp.sum(jnp.where(ahead[:, None] == order[None, :], listed[None, :], 0), axis=1)
        tables = (table_1, table_2)

        def served(t, me, n, row):
            return t[0][RANKED + ranked_at(lax.bitwise_xor(me, n), row)]

        home_1 = exchange(
            pack(tables[:1], me_b, lambda t, me, n, row: t[0][BASE + served(t, me, n, row)], 8, 4, home, [])
        )
        in_x = along_x(pack(tables, me_b, lambda t, me, n, row: t[1][SENT + n * KX + row], 3, KX, home, []))
        parts_1 = pack(tables, me_b, served, 8, 4, (), [in_1])
        away_1 = exchange(parts_1)
        (out_2,) = pack(
            tables, me_b, lambda t, me, n, row: t[1][RELAY + row], 1, NZ, home, after(in_x, parts_1)
        )
        in_z = along_z(out_2)

        def home_at(t, me, n, row):
            return t[1][HOME + 2 * lax.bitwise_xor(me, n) + row]

        home_parts = pack(tuple(after(tables, away_1)), me_b, home_at, 8, 2, home, [])
        home_2 = exchange(home_parts)
        one = lambda i, *_: (i, 0, 0)
        ready_1 = run_dimers(kernel_1, 4, (table_1, me_b), (1, 1), (one, one), [*home_1, *away_1])
        done_1 = exchange(ready_1)

        late_parts = pack(
            tables,
            me_b,
            lambda t, me, n, row: t[1][LATE + 2 * lax.bitwise_xor(me, n) + row] - 32,
            8,
            2,
            (),
            [*in_x, after(in_z, away_1)],
        )
        late_2 = exchange(late_parts)
        done_1 = after(done_1, late_parts)
        whole = lambda i, *_: (0, 0, 0)
        done_2 = exchange(
            run_dimers(kernel_2, 2, (table_2, me_b), (2, 2), (whole, whole), [*home_2, *late_2])
        )

        def back_to(k):
            return lambda t, me, row: jnp.where(row % 2 == 1, served(t, me, k, row // 2), -1)

        (ret_1,) = place(tables, me_b, done_1, [back_to(k) for k in range(8)], [32])
        back_1 = across(ret_1)

        def place_2(t, me, k, row):
            at = 2 * lax.bitwise_xor(me, k) + row // 2
            return jnp.where(t[1][STEPS + at] > 0, t[1][POS + 2 * at + row % 2], -1)

        def back_z(k):
            return lambda t, me, row: place_2(t, me, k, row) - 32 - NX

        def back_x(k):
            return lambda t, me, row: place_2(t, me, k, row) - 32

        (ret_z,) = place(tables, me_b, done_2, [back_z(k) for k in range(8)], [NZ])
        rest_z = along_z(after(ret_z, back_1))
        ret_x = place(
            tables,
            me_b,
            [*done_2, rest_z],
            [back_x(k) for k in range(8)] + [lambda t, me, row: t[1][RELAY + row] - 32],
            [KX] * 3,
        )
        rest_x = along_x(ret_x)

        def stay_1(k):
            return lambda t, me, row: jnp.where(row % 2 == 0, t[0][BASE + served(t, me, k, row // 2)], -1)

        def stay_2(k):
            return lambda t, me, row: place_2(t, me, k, row)

        def from_x(k):
            return lambda t, me, row: t[1][SENT + k * KX + row]

        finds = (
            [stay_1(k) for k in range(8)]
            + [stay_2(k) for k in range(8)]
        )
        finds += [lambda t, me, row: t[0][OUT + row]]
        dens, emb = add_up(tables, me_b, [*done_1, *done_2, back_1], finds, dens, emb)
        finds = [lambda t, me, row: t[1][RELAY + row]] + [from_x(k) for k in range(3)]
        dens, emb = add_up(tables, me_b, [rest_z, *rest_x], finds, dens, emb)
        return jnp.sum(left), left, dens, emb

    start = (
        jnp.int32(dimers),
        jnp.ones(dimers, jnp.int32),
        jnp.zeros(density.shape, F32),
        jnp.zeros((density.shape[0], aux_factor.shape[2]), F32),
    )
    _, _, dens, emb = lax.while_loop(lambda carry: carry[0] > 0, one_round, start)
    return dens, emb


def solution(mesh):
    return jax.shard_map(
        shards,
        mesh=mesh,
        in_specs=(
            P("frag", "basis", None),
            P("frag", None, "basis"),
            P(("frag", "basis"), None),
            P(),
            P(("frag", "basis")),
        ),
        out_specs=(P("frag", "basis", None), P("frag", "basis")),
        check_vma=False,
    )
```

```python
import jax
import jax.numpy as jnp
from jax import lax
from jax.experimental import pallas as pl
from jax.experimental.pallas import tpu as pltpu
from jax.sharding import PartitionSpec as P


COUPLE = 0.015625
BIG = 1 << 30
BF16 = jnp.bfloat16
F32 = jnp.float32
KX, KZ = 6, 2
NX, NZ = 3 * KX, 8 * KZ
SENT, RELAY, POS, BACK, HOME, LATE, STEPS, MODE, TABLE = 0, 32, 64, 96, 128, 160, 192, 224, 256
OUT, BASE, STEP1, RANKED = 0, 32, 64, 96

VMEM = pl.BlockSpec(memory_space=pltpu.VMEM)
SMEM = pl.BlockSpec(memory_space=pltpu.SMEM)


def loop(count, body):
    def step(n, unused):
        body(n)
        return unused

    lax.fori_loop(0, count, step, 0)


def ranked_at(device, place):
    return place * 8 + jnp.where(place % 2 == 0, device, 7 - device)


def pack(tables, me, find, outs, rows, home, items):
    sizes = ([32] if home else []) + [item.shape[0] for item in items]

    def kernel(*refs):
        table_refs, me_ref, refs = refs[: len(tables)], refs[len(tables)], refs[len(tables) + 1 :]
        sources, out_refs = refs[: len(refs) - outs], refs[len(refs) - outs :]
        for n, out_ref in enumerate(out_refs):

            def body(row, n=n, out_ref=out_ref):
                at = jnp.maximum(find(table_refs, me_ref[0], n, row), 0)
                base, left = 0, list(sources)
                for which, size in enumerate(sizes):
                    here = (at >= base) & (at < base + size)
                    if home and which == 0:
                        aux_ref, den_ref = left.pop(0), left.pop(0)

                        @pl.when(here)
                        def _(aux_ref=aux_ref, den_ref=den_ref):
                            out_ref[row, 0:256, :] = aux_ref[at]
                            block = den_ref[at]
                            out_ref[row, 256:288, :] = block[:, 0:128]
                            out_ref[row, 288:320, :] = block[:, 128:256]
                    else:
                        item_ref = left.pop(0)

                        @pl.when(here)
                        def _(item_ref=item_ref, base=base):
                            out_ref[row] = item_ref[at - base]

                    base += size

            loop(rows, body)

    sources = list(home) + list(items)
    return pl.pallas_call(
        kernel,
        out_shape=[jax.ShapeDtypeStruct((rows, 320, 128), BF16)] * outs,
        in_specs=[SMEM] * (len(tables) + 1) + [VMEM] * len(sources),
        out_specs=[VMEM] * outs,
        name="pack",
    )(*tables, me, *sources)


def place(tables, me, parts, finds, out_rows):
    def kernel(*refs):
        table_refs, me_ref, refs = refs[: len(tables)], refs[len(tables)], refs[len(tables) + 1 :]
        for part_ref, find in zip(refs[: len(parts)], finds, strict=True):

            def body(row, part_ref=part_ref, find=find):
                at = find(table_refs, me_ref[0], row)
                base = 0
                for out_ref, size in zip(refs[len(parts) :], out_rows, strict=True):

                    @pl.when((at >= base) & (at < base + size))
                    def _(out_ref=out_ref, base=base):
                        out_ref[at - base] = part_ref[row]

                    base += size

            loop(part_ref.shape[0], body)

    return pl.pallas_call(
        kernel,
        out_shape=[jax.ShapeDtypeStruct((size, 72, 128), BF16) for size in out_rows],
        in_specs=[SMEM] * (len(tables) + 1) + [VMEM] * len(parts),
        out_specs=[VMEM] * len(out_rows),
        name="place",
    )(*tables, me, *parts)


def add_up(tables, me, parts, finds, dens, emb):
    def kernel(*refs):
        table_refs, me_ref, refs = refs[: len(tables)], refs[len(tables)], refs[len(tables) + 1 :]
        dens_in, emb_in, dens_ref, emb_ref = refs[len(parts) :]
        dens_ref[...] = dens_in[...]
        emb_ref[...] = emb_in[...]
        for part_ref, find in zip(refs[: len(parts)], finds, strict=True):

            def body(row, part_ref=part_ref, find=find):
                slot = find(table_refs, me_ref[0], row)

                @pl.when((slot >= 0) & (slot < 32))
                def _():
                    dens_ref[slot, :, 0:128] += part_ref[row, 0:32, :].astype(F32)
                    dens_ref[slot, :, 128:256] += part_ref[row, 32:64, :].astype(F32)
                    emb_ref[pl.ds(slot, 1), :] += part_ref[row, 64:72, :].astype(F32)[0:1, :]

            loop(part_ref.shape[0], body)

    first = len(tables) + 1 + len(parts)
    return pl.pallas_call(
        kernel,
        out_shape=[jax.ShapeDtypeStruct(dens.shape, F32), jax.ShapeDtypeStruct(emb.shape, F32)],
        in_specs=[SMEM] * (len(tables) + 1) + [VMEM] * (len(parts) + 2),
        out_specs=[VMEM, VMEM],
        input_output_aliases={first: 0, first + 1: 1},
        name="add_up",
    )(*tables, me, *parts, dens, emb)


def take(half, me, parts, row, stacked, dens):
    for n in range(8):
        lanes = slice(n * 128, n * 128 + 128)
        at = pl.multiple_of(lax.bitwise_xor(me, n) * 32, 32)
        stacked[half : half + 256, lanes] = parts[n][row, 0:256, :]
        dens[pl.ds(half + at, 32), 0:128] = parts[n][row, 256:288, :]
        dens[pl.ds(half + at, 32), 128:256] = parts[n][row, 288:320, :]


def one_dimer(steps, me, load, out, scratch):
    stacked, weighted, dens, current, squares = scratch

    @pl.when(steps > 0)
    def _():
        load()
        fits = []
        for half in (0, 256):
            block = dens[half : half + 256, :]
            sums = []
            for n in range(4):
                lanes = slice(n * 256, n * 256 + 256)
                factor = stacked[half : half + 256, lanes]
                projected = jnp.dot(block, factor, preferred_element_type=F32)
                sums.append(jnp.sum(factor.astype(F32) * projected, axis=0, keepdims=True))
            fits.append(jnp.concatenate(sums, axis=1).astype(BF16).astype(F32))
        coeff = fits[0] + fits[1]

        def weigh(n):
            rows = pl.ds(pl.multiple_of(n * 64, 64), 64)
            weighted[rows, :] = (stacked[rows, :].astype(F32) * coeff).astype(BF16)

        loop(8, weigh)
        for n in range(4):
            rows = slice(n * 128, n * 128 + 128)
            coulomb = lax.dot_general(
                weighted[rows, :], stacked[...], (((1,), (1,)), ((), ())), preferred_element_type=F32
            )
            row_at = lax.broadcasted_iota(jnp.int32, (128, 512), 0) + n * 128
            col_at = lax.broadcasted_iota(jnp.int32, (128, 512), 1)
            own = dens[rows, :].astype(F32)
            blank = jnp.zeros((128, 256), F32)
            wide = jnp.concatenate([own, blank] if n < 2 else [blank, own], axis=1)
            eye = jnp.where(row_at == col_at, 0.5, 0.0)
            current[rows, :] = (eye + wide + COUPLE * coulomb).astype(BF16)

        def purify(index, unused):

            def block(n):
                rows = pl.ds(pl.multiple_of(n * 128, 128), 128)
                square = jnp.dot(current[rows, :], current[...], preferred_element_type=F32)
                cube = jnp.dot(square.astype(BF16), current[...], preferred_element_type=F32)
                squares[rows, :] = (3.0 * square - 2.0 * cube).astype(BF16)

            for n in range(4):
                block(n)
            current[...] = squares[...]
            return unused

        lax.fori_loop(0, steps, purify, 0)
        row_at = lax.broadcasted_iota(jnp.int32, (256, 256), 0)
        col_at = lax.broadcasted_iota(jnp.int32, (256, 256), 1)
        eye = jnp.where(row_at == col_at, 0.5, 0.0)
        for half in (0, 256):
            own = slice(half, half + 256)
            change = current[own, own].astype(F32) - dens[own, :].astype(F32) - eye
            dens[own, :] = change.astype(BF16)
        for n in range(8):
            to = lax.bitwise_xor(me, n)
            at = pl.multiple_of(to * 32, 32)
            lanes = slice(n * 128, n * 128 + 128)
            for r in range(2):
                change = dens[pl.ds(r * 256 + at, 32), :]
                out[to, r, 0:32, :] = change[:, 0:128]
                out[to, r, 32:64, :] = change[:, 128:256]
                partner = jnp.broadcast_to(fits[1 - r][:, lanes], (8, 128))
                out[to, r, 64:72, :] = partner.astype(BF16)


SCRATCH = [
    pltpu.VMEM((512, 1024), BF16),
    pltpu.VMEM((512, 1024), BF16),
    pltpu.VMEM((512, 256), BF16),
    pltpu.VMEM((512, 512), BF16),
    pltpu.VMEM((512, 512), BF16),
]


def run_dimers(kernel, count, tables, blocks, maps, parts):
    specs = []
    for block, index_map in zip(blocks, maps, strict=True):
        specs += [pl.BlockSpec((block, 320, 128), index_map)] * 8
    return pl.pallas_call(
        kernel,
        out_shape=jax.ShapeDtypeStruct((8, 2 * count, 72, 128), BF16),
        grid_spec=pltpu.PrefetchScalarGridSpec(
            num_scalar_prefetch=2,
            grid=(count,),
            in_specs=specs,
            out_specs=pl.BlockSpec((8, 2, 72, 128), lambda i, *_: (0, i, 0, 0)),
            scratch_shapes=SCRATCH,
        ),
        name="dimers",
        cost_estimate=pl.CostEstimate(
            flops=count * 4_000_000_000, bytes_accessed=count * 1_500_000, transcendentals=0
        ),
    )(*tables, *parts)


def kernel_1(table_ref, me_ref, *refs):
    me, i = me_ref[0], pl.program_id(0)
    first, second, out, scratch = refs[0:8], refs[8:16], refs[16], refs[17:]
    stacked, dens = scratch[0], scratch[2]

    def load():
        take(0, me, first, 0, stacked, dens)
        take(256, me, second, 0, stacked, dens)

    other = table_ref[RANKED + ranked_at(me, i)]
    one_dimer(table_ref[STEP1 + other], me, load, out, scratch)


def kernel_2(table_ref, me_ref, *refs):
    me, i = me_ref[0], pl.program_id(0)
    home, late, out, scratch = refs[0:8], refs[8:16], refs[16], refs[17:]
    stacked, dens = scratch[0], scratch[2]
    split = table_ref[MODE + me] > 0

    def load():
        both_late = split & (i == 0)
        both_home = split & (i == 1)

        @pl.when(both_late)
        def _():
            take(0, me, late, 0, stacked, dens)

        @pl.when(jnp.logical_not(both_late))
        def _():
            take(0, me, home, jnp.where(split, 0, i), stacked, dens)

        @pl.when(both_home)
        def _():
            take(256, me, home, 1, stacked, dens)

        @pl.when(jnp.logical_not(both_home))
        def _():
            take(256, me, late, jnp.where(split, 1, i), stacked, dens)

    one_dimer(table_ref[STEPS + 2 * me + i], me, load, out, scratch)


def plan_kernel(me_ref, inside_ref, count_ref, list_ref, table_ref, left_ref, to_x, to_z, n_direct, n_third, n_self, n_split, room, taken):
    me = me_ref[0]
    me_x, me_z = me >> 3, me & 7

    def clear(n):
        for i in range(8):
            to_z[n * 8 + i] = 0
            table_ref[n * 8 + i] = jnp.where(n < STEPS // 8, -1, 0)

    def clear_x(n):
        for i in range(8):
            to_x[n * 8 + i] = 0

    def clear_c(n):
        n_direct[n] = 0
        n_third[n] = 0
        n_self[n] = 0
        n_split[n] = inside_ref[n]
        room[n] = 1 + inside_ref[n]
        taken[n] = 0

    loop(TABLE // 8, clear)
    loop(16, clear_x)
    loop(32, clear_c)

    def put(at, good, spare, value):
        table_ref[jnp.where(good, at, spare)] = value

    def can(o, c, extra):
        zo, xc, zc = o & 7, c >> 3, c & 7
        free = ((taken[c] >> o) & 1) == 0
        return free & (to_x[o * 4 + xc] < KX) & ((zo == zc) | (to_z[xc * 64 + zo * 8 + zc] + extra < KZ))

    def send(o, slot, c, at_x, at_z, n_x, n_z):
        xo, zo, xc, zc = o >> 3, o & 7, c >> 3, c & 7
        move_x, move_z = xo != xc, zo != zc
        taken[c] = taken[c] | lax.shift_left(jnp.int32(1), o)
        to_x[at_x] = n_x + jnp.where(move_x, 1, 0)
        to_z[at_z] = n_z + jnp.where(move_z, 1, 0)
        in_x = (lax.bitwise_xor(xo, xc) - 1) * KX + n_x

        @pl.when(zo == me_z)
        def _():
            put(SENT + in_x, move_x & (o == me), SENT + 31, slot)
            put(BACK + c, o == me, SENT + 31, slot)
            put(RELAY + zc * KZ + n_z, move_z & (xc == me_x), RELAY + 31, jnp.where(move_x, 32 + in_x, slot))

        return jnp.where(move_z, 32 + NX + zo * KZ + n_z, 32 + in_x)

    def visit(d):
        word = list_ref[d]
        cost = word >> 20
        la, oa, lb, ob = word & 31, (word >> 5) & 31, (word >> 10) & 31, (word >> 15) & 31
        left_ref[d] = 0
        za, xa, zb, xb = oa & 7, oa >> 3, ob & 7, ob >> 3
        x_at_a, z_at_a = ob * 4 + xa, xa * 64 + zb * 8 + za
        x_at_b, z_at_b = oa * 4 + xb, xb * 64 + za * 8 + zb
        x_a, z_a, x_b, z_b = to_x[x_at_a], to_z[z_at_a], to_x[x_at_b], to_z[z_at_b]
        room_a, room_b = room[oa], room[ob]
        free_a, free_b = ((taken[oa] >> ob) & 1) == 0, ((taken[ob] >> oa) & 1) == 0
        can_a = free_a & (x_a < KX) & (z_a < KZ) & (room_a <= 8)
        can_b = free_b & (x_b < KX) & (z_b < KZ) & (room_b <= 8)
        use_a = can_a & (jnp.logical_not(can_b) | (z_a * 4 + room_a <= z_b * 4 + room_b))
        apart = oa != ob
        direct = apart & (can_a | can_b)

        @pl.when(direct)
        def _():
            c, o = jnp.where(use_a, oa, ob), jnp.where(use_a, ob, oa)
            stay, move = jnp.where(use_a, la, lb), jnp.where(use_a, lb, la)
            at = n_direct[c]
            n_direct[c] = at + 1
            room[c] = ((at + 3) >> 1) + n_split[c]
            late = send(
                o,
                move,
                c,
                jnp.where(use_a, x_at_a, x_at_b),
                jnp.where(use_a, z_at_a, z_at_b),
                jnp.where(use_a, x_a, x_b),
                jnp.where(use_a, z_a, z_b),
            )

            @pl.when(c == me)
            def _():
                table_ref[POS + 2 * at] = stay
                table_ref[POS + 2 * at + 1] = 32 + o
                table_ref[HOME + at] = stay
                table_ref[LATE + at] = late
                table_ref[STEPS + at] = cost

        @pl.when(jnp.logical_not(direct))
        def _():
            @pl.when(jnp.logical_not(apart))
            def _():
                q = n_self[oa]

                @pl.when(q < 8)
                def _():
                    n_self[oa] = q + 1

                    @pl.when(oa == me)
                    def _():
                        at = 2 * (7 - q)
                        table_ref[POS + 2 * at + 2] = la
                        table_ref[POS + 2 * at + 3] = lb
                        table_ref[HOME + at] = la
                        table_ref[HOME + at + 1] = lb
                        table_ref[STEPS + at + 1] = cost
                        table_ref[MODE + 7 - q] = 1

                @pl.when(q >= 8)
                def _():
                    left_ref[d] = 1

            @pl.when(apart)
            def _():
                same_z = jnp.where(za == zb, 1, 0)

                def look(carry):
                    n, _ = carry
                    c = (d + n) & 31
                    fit = ((n_direct[c] + 1) >> 1) + jnp.maximum(n_third[c] + 1, inside_ref[c]) <= 8
                    good = fit & can(oa, c, same_z) & can(ob, c, same_z) & (c != oa) & (c != ob)
                    return n + 1, jnp.where(good, c, -1)

                _, c = lax.while_loop(
                    lambda carry: (carry[0] < 32) & (carry[1] < 0), look, (jnp.int32(0), jnp.int32(-1))
                )

                @pl.when(c < 0)
                def _():
                    left_ref[d] = 1

                @pl.when(c >= 0)
                def _():
                    t = n_third[c]
                    n_third[c] = t + 1
                    split = jnp.maximum(t + 1, inside_ref[c])
                    n_split[c] = split
                    room[c] = ((n_direct[c] + 2) >> 1) + split
                    xc, zc = c >> 3, c & 7
                    x_at, z_at = oa * 4 + xc, xc * 64 + za * 8 + zc
                    late_a = send(oa, la, c, x_at, z_at, to_x[x_at], to_z[z_at])
                    x_at, z_at = ob * 4 + xc, xc * 64 + zb * 8 + zc
                    late_b = send(ob, lb, c, x_at, z_at, to_x[x_at], to_z[z_at])

                    @pl.when(c == me)
                    def _():
                        at = 2 * (7 - t)
                        table_ref[POS + 2 * at] = 32 + oa
                        table_ref[POS + 2 * at + 1] = 32 + ob
                        table_ref[LATE + at] = late_a
                        table_ref[LATE + at + 1] = late_b
                        table_ref[STEPS + at] = cost
                        table_ref[MODE + 7 - t] = 1

    loop(count_ref[0], visit)


def plan_rest(me, inside_count, count, words):
    s32 = jnp.int32
    return pl.pallas_call(
        plan_kernel,
        out_shape=[jax.ShapeDtypeStruct((TABLE,), s32), jax.ShapeDtypeStruct(words.shape, s32)],
        in_specs=[SMEM] * 4,
        out_specs=[SMEM] * 2,
        scratch_shapes=[pltpu.SMEM((128,), s32), pltpu.SMEM((256,), s32)] + [pltpu.SMEM((32,), s32)] * 6,
        name="plan",
        cost_estimate=pl.CostEstimate(flops=1000, bytes_accessed=30_000_000, transcendentals=0),
    )(me, inside_count, count, words)


def exchange(parts):
    got = [parts[0]]
    for k in range(1, 8):
        got.append(lax.ppermute(parts[k], "basis", [(i, i ^ k) for i in range(8)]))
    return got


def give_back(done):
    return lax.all_to_all(done, "basis", split_axis=0, concat_axis=0, tiled=True).reshape(-1, 72, 128)


def along_x(parts):
    return [lax.ppermute(parts[k - 1], "frag", [(i, i ^ (8 * k)) for i in range(32)]) for k in (1, 2, 3)]


def along_z(part):
    groups = [[8 * x + z for z in range(8)] for x in range(4)]
    return lax.all_to_all(part, "frag", 0, 0, tiled=True, axis_index_groups=groups)


def across(part):
    return lax.all_to_all(part, "frag", split_axis=0, concat_axis=0, tiled=True)


def after(value, *others):
    return lax.optimization_barrier((value, others))[0]


def shards(density, aux_factor, pairs, slot_of, costs):
    n_frag = lax.axis_size("frag")
    n_basis = lax.axis_size("basis")
    me_frag = lax.axis_index("frag").astype(jnp.int32)
    me_basis = lax.axis_index("basis").astype(jnp.int32)
    dimers = pairs.shape[0] * n_frag * n_basis

    lookup = pairs[:, :, None] == jnp.arange(slot_of.shape[0], dtype=jnp.int32)
    slots = jnp.sum(jnp.where(lookup, slot_of, 0), axis=2)
    mine = jnp.concatenate([slots[:, 0], slots[:, 1], costs, jnp.zeros(116, jnp.int32)])
    column = lax.all_to_all(
        jnp.broadcast_to(mine, (n_basis, 1, 128)), "basis", split_axis=0, concat_axis=0, tiled=True
    )
    column = column[:, 0, 0:12].reshape(n_basis, 3, 4).transpose(1, 0, 2).reshape(96)
    column = jnp.concatenate([column, jnp.zeros(32, jnp.int32)])
    every = across(jnp.broadcast_to(column, (n_frag, 1, 128)))
    a = every[:, 0, 0:32].reshape(dimers)
    b = every[:, 0, 32:64].reshape(dimers)
    cost = every[:, 0, 64:96].reshape(dimers)

    order = jnp.arange(dimers, dtype=jnp.int32)
    columns = jnp.arange(n_frag, dtype=jnp.int32)
    own_a, own_b = a // 32, b // 32
    low, high = jnp.minimum(own_a, own_b), jnp.maximum(own_a, own_b)
    pair_id = low * 32 + high
    inside = own_a == own_b
    mine_a = (own_a == me_frag) & jnp.logical_not(inside)
    mine_b = (own_b == me_frag) & jnp.logical_not(inside)
    other = jnp.where(mine_a, own_b, jnp.where(mine_b, own_a, -1))
    local = jnp.where(mine_a, a, b) & 31
    key = order * 256 + local * 8 + cost
    word = a + b * 1024 + cost * 1048576
    me_f, me_b = me_frag.reshape(1), me_basis.reshape(1)
    keep_first = (me_frag < columns) == ((me_frag + columns) % 2 == 0)
    home = (aux_factor, density)

    def one_round(carry):
        return body_round(carry)

    def body_round(carry):
        _, rest, dens, emb = carry
        open_dimer = rest > 0
        match = (other[None, :] == columns[:, None]) & open_dimer[None, :]
        keyed = jnp.where(match, key[None, :], BIG)
        key_0 = jnp.min(keyed, axis=1)
        key_1 = jnp.min(jnp.where(keyed > key_0[:, None], keyed, BIG), axis=1)
        here = jnp.where(keep_first, key_0, key_1)
        there = jnp.where(keep_first, key_1, key_0)
        send_1 = jnp.where(there < BIG, (there >> 3) & 31, -1)
        base_1 = jnp.where(here < BIG, (here >> 3) & 31, -1)
        steps_1 = jnp.where(here < BIG, here & 7, 0)

        (out_1,) = pack((send_1,), me_b, lambda t, me, n, row: t[0][row], 1, 32, home, [])
        in_1 = across(out_1)

        weight = steps_1 * 64 - columns
        rank = jnp.sum((weight[None, :] > weight[:, None]).astype(jnp.int32), axis=1)
        ranked = jnp.sum(jnp.where(rank[None, :] == columns[:, None], columns[None, :], 0), axis=1)
        table_1 = jnp.concatenate([send_1, base_1, steps_1, ranked])

        earlier = (pair_id[:, None] == pair_id[None, :]) & (order[None, :] < order[:, None])
        earlier = jnp.sum(jnp.where(earlier & open_dimer[None, :], 1, 0), axis=1)
        flagged = open_dimer & ((earlier >= 2) | inside)
        ahead = jnp.sum(jnp.where((order[None, :] < order[:, None]) & flagged[None, :], 1, 0), axis=1)
        ahead = jnp.where(flagged, ahead, -1)
        words = jnp.sum(jnp.where(ahead[None, :] == order[:, None], word[None, :], 0), axis=1)
        count = jnp.sum(jnp.where(flagged, 1, 0)).reshape(1)
        inside_here = (own_a[None, :] == columns[:, None]) & (inside & open_dimer)[None, :]
        inside_count = jnp.sum(jnp.where(inside_here, 1, 0), axis=1)
        table_2, listed = plan_rest(me_f, inside_count, count, words)
        listed = jnp.where(order < count, listed, 0)
        left = jnp.sum(jnp.where(ahead[:, None] == order[None, :], listed[None, :], 0), axis=1)
        tables = (table_1, table_2)

        def served(t, me, n, row):
            return t[0][RANKED + ranked_at(lax.bitwise_xor(me, n), row)]

        home_1 = exchange(
            pack(tables[:1], me_b, lambda t, me, n, row: t[0][BASE + served(t, me, n, row)], 8, 4, home, [])
        )
        in_x = along_x(pack(tables, me_b, lambda t, me, n, row: t[1][SENT + n * KX + row], 3, KX, home, []))

        def home_at(t, me, n, row):
            return t[1][HOME + 2 * lax.bitwise_xor(me, n) + row]

        home_2 = exchange(pack(tables, me_b, home_at, 8, 2, home, []))
        parts_1 = pack(tables, me_b, served, 8, 4, (), [in_1])
        away_1 = exchange(parts_1)
        (out_2,) = pack(
            tables, me_b, lambda t, me, n, row: t[1][RELAY + row], 1, NZ, home, after(in_x, parts_1)
        )
        in_z = along_z(out_2)

        one = lambda i, *_: (i, 0, 0)
        ready_1 = run_dimers(kernel_1, 4, (table_1, me_b), (1, 1), (one, one), [*home_1, *away_1])
        done_1 = give_back(ready_1)

        def late_at(t, me, n, row):
            return t[1][LATE + 2 * lax.bitwise_xor(me, n) + row] - 32

        late_parts = pack(tables, me_b, late_at, 8, 2, (), [*in_x, after(in_z, away_1)])
        late_2 = exchange(late_parts)
        whole = lambda i, *_: (0, 0, 0)
        ready_2 = run_dimers(kernel_2, 2, (table_2, me_b), (2, 2), (whole, whole), [*home_2, *late_2])

        def place_1(t, row):
            return t[0][RANKED + ranked_at(row // 8, row % 8 // 2)]

        def place_2(t, row):
            at = row // 2
            return jnp.where(t[1][STEPS + at] > 0, t[1][POS + row], -1)

        (ret_1,) = place(
            tables, me_b, [done_1], [lambda t, me, row: jnp.where(row % 2 == 1, place_1(t, row), -1)], [32]
        )
        back_1 = across(ret_1)
        done_2 = give_back(after(ready_2, back_1))
        (ret_2,) = place(tables, me_b, [done_2], [lambda t, me, row: place_2(t, row) - 32], [32])
        back_2 = across(ret_2)
        finds = [
            lambda t, me, row: jnp.where(row % 2 == 0, t[0][BASE + place_1(t, row)], -1),
            lambda t, me, row: place_2(t, row),
            lambda t, me, row: t[0][OUT + row],
        ]
        dens, emb = add_up(tables, me_b, [done_1, done_2, back_1], finds, dens, emb)
        dens, emb = add_up(tables, me_b, [back_2], [lambda t, me, row: t[1][BACK + row]], dens, emb)
        return jnp.sum(left), left, dens, emb

    start = (
        jnp.int32(dimers),
        jnp.ones(dimers, jnp.int32),
        jnp.zeros(density.shape, F32),
        jnp.zeros((density.shape[0], aux_factor.shape[2]), F32),
    )
    _, _, dens, emb = lax.while_loop(lambda carry: carry[0] > 0, one_round, start)
    return dens, emb


def solution(mesh):
    return jax.shard_map(
        shards,
        mesh=mesh,
        in_specs=(
            P("frag", "basis", None),
            P("frag", None, "basis"),
            P(("frag", "basis"), None),
            P(),
            P(("frag", "basis")),
        ),
        out_specs=(P("frag", "basis", None), P("frag", "basis")),
        check_vma=False,
    )
```

```python
import jax
import jax.numpy as jnp
from jax import lax
from jax.experimental import pallas as pl
from jax.experimental.pallas import tpu as pltpu
from jax.sharding import PartitionSpec as P


COUPLE = 0.015625
BIG = 1 << 30
BF16 = jnp.bfloat16
F32 = jnp.float32
KX, KZ = 6, 2
NX, NZ = 3 * KX, 8 * KZ
SENT, RELAY, POS, BACK, HOME, LATE, STEPS, MODE, TABLE = 0, 32, 64, 96, 128, 160, 192, 224, 256
OUT, BASE, STEP1, RANKED = 0, 32, 64, 96

VMEM = pl.BlockSpec(memory_space=pltpu.VMEM)
SMEM = pl.BlockSpec(memory_space=pltpu.SMEM)


def loop(count, body):
    def step(n, unused):
        body(n)
        return unused

    lax.fori_loop(0, count, step, 0)


def ranked_at(device, place):
    return place * 8 + jnp.where(place % 2 == 0, device, 7 - device)


def pack(tables, me, find, outs, rows, home, items):
    sizes = ([32] if home else []) + [item.shape[0] for item in items]

    def kernel(*refs):
        table_refs, me_ref, refs = refs[: len(tables)], refs[len(tables)], refs[len(tables) + 1 :]
        sources, out_refs = refs[: len(refs) - outs], refs[len(refs) - outs :]
        for n, out_ref in enumerate(out_refs):

            def body(row, n=n, out_ref=out_ref):
                at = jnp.maximum(find(table_refs, me_ref[0], n, row), 0)
                base, left = 0, list(sources)
                for which, size in enumerate(sizes):
                    here = (at >= base) & (at < base + size)
                    if home and which == 0:
                        aux_ref, den_ref = left.pop(0), left.pop(0)

                        @pl.when(here)
                        def _(aux_ref=aux_ref, den_ref=den_ref):
                            out_ref[row, 0:256, :] = aux_ref[at]
                            block = den_ref[at]
                            out_ref[row, 256:288, :] = block[:, 0:128]
                            out_ref[row, 288:320, :] = block[:, 128:256]
                    else:
                        item_ref = left.pop(0)

                        @pl.when(here)
                        def _(item_ref=item_ref, base=base):
                            out_ref[row] = item_ref[at - base]

                    base += size

            loop(rows, body)

    sources = list(home) + list(items)
    return pl.pallas_call(
        kernel,
        out_shape=[jax.ShapeDtypeStruct((rows, 320, 128), BF16)] * outs,
        in_specs=[SMEM] * (len(tables) + 1) + [VMEM] * len(sources),
        out_specs=[VMEM] * outs,
        name="pack",
    )(*tables, me, *sources)


def place(tables, me, parts, finds, out_rows):
    def kernel(*refs):
        table_refs, me_ref, refs = refs[: len(tables)], refs[len(tables)], refs[len(tables) + 1 :]
        for part_ref, find in zip(refs[: len(parts)], finds, strict=True):

            def body(row, part_ref=part_ref, find=find):
                at = find(table_refs, me_ref[0], row)
                base = 0
                for out_ref, size in zip(refs[len(parts) :], out_rows, strict=True):

                    @pl.when((at >= base) & (at < base + size))
                    def _(out_ref=out_ref, base=base):
                        out_ref[at - base] = part_ref[row]

                    base += size

            loop(part_ref.shape[0], body)

    return pl.pallas_call(
        kernel,
        out_shape=[jax.ShapeDtypeStruct((size, 72, 128), BF16) for size in out_rows],
        in_specs=[SMEM] * (len(tables) + 1) + [VMEM] * len(parts),
        out_specs=[VMEM] * len(out_rows),
        name="place",
    )(*tables, me, *parts)


def add_up(tables, me, parts, finds, dens, emb):
    def kernel(*refs):
        table_refs, me_ref, refs = refs[: len(tables)], refs[len(tables)], refs[len(tables) + 1 :]
        dens_in, emb_in, dens_ref, emb_ref = refs[len(parts) :]
        dens_ref[...] = dens_in[...]
        emb_ref[...] = emb_in[...]
        for part_ref, find in zip(refs[: len(parts)], finds, strict=True):

            def body(row, part_ref=part_ref, find=find):
                slot = find(table_refs, me_ref[0], row)

                @pl.when((slot >= 0) & (slot < 32))
                def _():
                    dens_ref[slot, :, 0:128] += part_ref[row, 0:32, :].astype(F32)
                    dens_ref[slot, :, 128:256] += part_ref[row, 32:64, :].astype(F32)
                    emb_ref[pl.ds(slot, 1), :] += part_ref[row, 64:72, :].astype(F32)[0:1, :]

            loop(part_ref.shape[0], body)

    first = len(tables) + 1 + len(parts)
    return pl.pallas_call(
        kernel,
        out_shape=[jax.ShapeDtypeStruct(dens.shape, F32), jax.ShapeDtypeStruct(emb.shape, F32)],
        in_specs=[SMEM] * (len(tables) + 1) + [VMEM] * (len(parts) + 2),
        out_specs=[VMEM, VMEM],
        input_output_aliases={first: 0, first + 1: 1},
        name="add_up",
    )(*tables, me, *parts, dens, emb)


def take(half, me, parts, row, stacked, dens):
    for n in range(8):
        lanes = slice(n * 128, n * 128 + 128)
        at = pl.multiple_of(lax.bitwise_xor(me, n) * 32, 32)
        stacked[half : half + 256, lanes] = parts[n][row, 0:256, :]
        dens[pl.ds(half + at, 32), 0:128] = parts[n][row, 256:288, :]
        dens[pl.ds(half + at, 32), 128:256] = parts[n][row, 288:320, :]


def one_dimer(steps, me, load, out, scratch):
    stacked, weighted, dens, current = scratch

    @pl.when(steps > 0)
    def _():
        load()
        fits = []
        for half in (0, 256):
            block = dens[half : half + 256, :]
            sums = []
            for n in range(4):
                lanes = slice(n * 256, n * 256 + 256)
                factor = stacked[half : half + 256, lanes]
                projected = jnp.dot(block, factor, preferred_element_type=F32)
                sums.append(jnp.sum(factor.astype(F32) * projected, axis=0, keepdims=True))
            fits.append(jnp.concatenate(sums, axis=1).astype(BF16).astype(F32))
        coeff = fits[0] + fits[1]

        def weigh(n):
            rows = pl.ds(pl.multiple_of(n * 64, 64), 64)
            weighted[rows, :] = (stacked[rows, :].astype(F32) * coeff).astype(BF16)

        loop(8, weigh)
        coulomb = lax.dot_general(
            weighted[...], stacked[...], (((1,), (1,)), ((), ())), preferred_element_type=F32
        )
        row_at = lax.broadcasted_iota(jnp.int32, (256, 512), 0)
        col_at = lax.broadcasted_iota(jnp.int32, (256, 512), 1)
        blank = jnp.zeros((256, 256), F32)
        for half in (0, 256):
            own = dens[half : half + 256, :].astype(F32)
            wide = jnp.concatenate([own, blank] if half == 0 else [blank, own], axis=1)
            eye = jnp.where(row_at + half == col_at, 0.5, 0.0)
            current[half : half + 256, :] = (eye + wide + COUPLE * coulomb[half : half + 256, :]).astype(BF16)

        def purify(index, unused):
            whole = current[...]
            square = jnp.dot(whole, whole, preferred_element_type=F32)
            cube = jnp.dot(square.astype(BF16), whole, preferred_element_type=F32)
            current[...] = (3.0 * square - 2.0 * cube).astype(BF16)
            return unused

        lax.fori_loop(0, steps, purify, 0)
        row_at = lax.broadcasted_iota(jnp.int32, (256, 256), 0)
        col_at = lax.broadcasted_iota(jnp.int32, (256, 256), 1)
        eye = jnp.where(row_at == col_at, 0.5, 0.0)
        for half in (0, 256):
            own = slice(half, half + 256)
            change = current[own, own].astype(F32) - dens[own, :].astype(F32) - eye
            dens[own, :] = change.astype(BF16)
        for n in range(8):
            to = lax.bitwise_xor(me, n)
            at = pl.multiple_of(to * 32, 32)
            lanes = slice(n * 128, n * 128 + 128)
            for r in range(2):
                change = dens[pl.ds(r * 256 + at, 32), :]
                out[to, r, 0:32, :] = change[:, 0:128]
                out[to, r, 32:64, :] = change[:, 128:256]
                partner = jnp.broadcast_to(fits[1 - r][:, lanes], (8, 128))
                out[to, r, 64:72, :] = partner.astype(BF16)


SCRATCH = [
    pltpu.VMEM((512, 1024), BF16),
    pltpu.VMEM((512, 1024), BF16),
    pltpu.VMEM((512, 256), BF16),
    pltpu.VMEM((512, 512), BF16),
]


def run_dimers(kernel, count, tables, blocks, maps, parts):
    specs = []
    for block, index_map in zip(blocks, maps, strict=True):
        specs += [pl.BlockSpec((block, 320, 128), index_map)] * 8
    return pl.pallas_call(
        kernel,
        out_shape=jax.ShapeDtypeStruct((8, 2 * count, 72, 128), BF16),
        grid_spec=pltpu.PrefetchScalarGridSpec(
            num_scalar_prefetch=2,
            grid=(count,),
            in_specs=specs,
            out_specs=pl.BlockSpec((8, 2, 72, 128), lambda i, *_: (0, i, 0, 0)),
            scratch_shapes=SCRATCH,
        ),
        name="dimers",
        cost_estimate=pl.CostEstimate(
            flops=count * 4_000_000_000, bytes_accessed=count * 1_500_000, transcendentals=0
        ),
    )(*tables, *parts)


def kernel_1(table_ref, me_ref, *refs):
    me, i = me_ref[0], pl.program_id(0)
    first, second, out, scratch = refs[0:8], refs[8:16], refs[16], refs[17:]
    stacked, dens = scratch[0], scratch[2]

    def load():
        take(0, me, first, 0, stacked, dens)
        take(256, me, second, 0, stacked, dens)

    other = table_ref[RANKED + ranked_at(me, i)]
    one_dimer(table_ref[STEP1 + other], me, load, out, scratch)


def kernel_2(table_ref, me_ref, *refs):
    me, i = me_ref[0], pl.program_id(0)
    home, late, out, scratch = refs[0:8], refs[8:16], refs[16], refs[17:]
    stacked, dens = scratch[0], scratch[2]
    split = table_ref[MODE + me] > 0

    def load():
        both_late = split & (i == 0)
        both_home = split & (i == 1)

        @pl.when(both_late)
        def _():
            take(0, me, late, 0, stacked, dens)

        @pl.when(jnp.logical_not(both_late))
        def _():
            take(0, me, home, jnp.where(split, 0, i), stacked, dens)

        @pl.when(both_home)
        def _():
            take(256, me, home, 1, stacked, dens)

        @pl.when(jnp.logical_not(both_home))
        def _():
            take(256, me, late, jnp.where(split, 1, i), stacked, dens)

    one_dimer(table_ref[STEPS + 2 * me + i], me, load, out, scratch)


def plan_kernel(me_ref, inside_ref, count_ref, list_ref, table_ref, left_ref, to_x, to_z, n_direct, n_third, n_self, n_split, room, taken):
    me = me_ref[0]
    me_x, me_z = me >> 3, me & 7

    def clear(n):
        for i in range(8):
            to_z[n * 8 + i] = 0
            table_ref[n * 8 + i] = jnp.where(n < STEPS // 8, -1, 0)

    def clear_x(n):
        for i in range(8):
            to_x[n * 8 + i] = 0

    def clear_c(n):
        n_direct[n] = 0
        n_third[n] = 0
        n_self[n] = 0
        n_split[n] = inside_ref[n]
        room[n] = 1 + inside_ref[n]
        taken[n] = 0

    loop(TABLE // 8, clear)
    loop(16, clear_x)
    loop(32, clear_c)

    def put(at, good, spare, value):
        table_ref[jnp.where(good, at, spare)] = value

    def can(o, c, extra):
        zo, xc, zc = o & 7, c >> 3, c & 7
        free = ((taken[c] >> o) & 1) == 0
        return free & (to_x[o * 4 + xc] < KX) & ((zo == zc) | (to_z[xc * 64 + zo * 8 + zc] + extra < KZ))

    def send(o, slot, c, at_x, at_z, n_x, n_z):
        xo, zo, xc, zc = o >> 3, o & 7, c >> 3, c & 7
        move_x, move_z = xo != xc, zo != zc
        taken[c] = taken[c] | lax.shift_left(jnp.int32(1), o)
        to_x[at_x] = n_x + jnp.where(move_x, 1, 0)
        to_z[at_z] = n_z + jnp.where(move_z, 1, 0)
        in_x = (lax.bitwise_xor(xo, xc) - 1) * KX + n_x

        @pl.when(zo == me_z)
        def _():
            put(SENT + in_x, move_x & (o == me), SENT + 31, slot)
            put(BACK + c, o == me, SENT + 31, slot)
            put(RELAY + zc * KZ + n_z, move_z & (xc == me_x), RELAY + 31, jnp.where(move_x, 32 + in_x, slot))

        return jnp.where(move_z, 32 + NX + zo * KZ + n_z, 32 + in_x)

    def visit(d):
        word = list_ref[d]
        cost = word >> 20
        la, oa, lb, ob = word & 31, (word >> 5) & 31, (word >> 10) & 31, (word >> 15) & 31
        left_ref[d] = 0
        za, xa, zb, xb = oa & 7, oa >> 3, ob & 7, ob >> 3
        x_at_a, z_at_a = ob * 4 + xa, xa * 64 + zb * 8 + za
        x_at_b, z_at_b = oa * 4 + xb, xb * 64 + za * 8 + zb
        x_a, z_a, x_b, z_b = to_x[x_at_a], to_z[z_at_a], to_x[x_at_b], to_z[z_at_b]
        room_a, room_b = room[oa], room[ob]
        free_a, free_b = ((taken[oa] >> ob) & 1) == 0, ((taken[ob] >> oa) & 1) == 0
        can_a = free_a & (x_a < KX) & (z_a < KZ) & (room_a <= 8)
        can_b = free_b & (x_b < KX) & (z_b < KZ) & (room_b <= 8)
        use_a = can_a & (jnp.logical_not(can_b) | (z_a * 4 + room_a <= z_b * 4 + room_b))
        apart = oa != ob
        direct = apart & (can_a | can_b)

        @pl.when(direct)
        def _():
            c, o = jnp.where(use_a, oa, ob), jnp.where(use_a, ob, oa)
            stay, move = jnp.where(use_a, la, lb), jnp.where(use_a, lb, la)
            at = n_direct[c]
            n_direct[c] = at + 1
            room[c] = ((at + 3) >> 1) + n_split[c]
            late = send(
                o,
                move,
                c,
                jnp.where(use_a, x_at_a, x_at_b),
                jnp.where(use_a, z_at_a, z_at_b),
                jnp.where(use_a, x_a, x_b),
                jnp.where(use_a, z_a, z_b),
            )

            @pl.when(c == me)
            def _():
                table_ref[POS + 2 * at] = stay
                table_ref[POS + 2 * at + 1] = 32 + o
                table_ref[HOME + at] = stay
                table_ref[LATE + at] = late
                table_ref[STEPS + at] = cost

        @pl.when(jnp.logical_not(direct))
        def _():
            @pl.when(jnp.logical_not(apart))
            def _():
                q = n_self[oa]

                @pl.when(q < 8)
                def _():
                    n_self[oa] = q + 1

                    @pl.when(oa == me)
                    def _():
                        at = 2 * (7 - q)
                        table_ref[POS + 2 * at + 2] = la
                        table_ref[POS + 2 * at + 3] = lb
                        table_ref[HOME + at] = la
                        table_ref[HOME + at + 1] = lb
                        table_ref[STEPS + at + 1] = cost
                        table_ref[MODE + 7 - q] = 1

                @pl.when(q >= 8)
                def _():
                    left_ref[d] = 1

            @pl.when(apart)
            def _():
                same_z = jnp.where(za == zb, 1, 0)

                def look(carry):
                    n, _ = carry
                    turn = ((d + n) & 3) * 8
                    c = jnp.where(n < 4, turn + za, jnp.where(n < 8, turn + zb, (d + n) & 31))
                    fit = ((n_direct[c] + 1) >> 1) + jnp.maximum(n_third[c] + 1, inside_ref[c]) <= 8
                    good = fit & can(oa, c, same_z) & can(ob, c, same_z) & (c != oa) & (c != ob)
                    return n + 1, jnp.where(good, c, -1)

                _, c = lax.while_loop(
                    lambda carry: (carry[0] < 40) & (carry[1] < 0), look, (jnp.int32(0), jnp.int32(-1))
                )

                @pl.when(c < 0)
                def _():
                    left_ref[d] = 1

                @pl.when(c >= 0)
                def _():
                    t = n_third[c]
                    n_third[c] = t + 1
                    split = jnp.maximum(t + 1, inside_ref[c])
                    n_split[c] = split
                    room[c] = ((n_direct[c] + 2) >> 1) + split
                    xc, zc = c >> 3, c & 7
                    x_at, z_at = oa * 4 + xc, xc * 64 + za * 8 + zc
                    late_a = send(oa, la, c, x_at, z_at, to_x[x_at], to_z[z_at])
                    x_at, z_at = ob * 4 + xc, xc * 64 + zb * 8 + zc
                    late_b = send(ob, lb, c, x_at, z_at, to_x[x_at], to_z[z_at])

                    @pl.when(c == me)
                    def _():
                        at = 2 * (7 - t)
                        table_ref[POS + 2 * at] = 32 + oa
                        table_ref[POS + 2 * at + 1] = 32 + ob
                        table_ref[LATE + at] = late_a
                        table_ref[LATE + at + 1] = late_b
                        table_ref[STEPS + at] = cost
                        table_ref[MODE + 7 - t] = 1

    loop(count_ref[0], visit)


def plan_rest(me, inside_count, count, words):
    s32 = jnp.int32
    return pl.pallas_call(
        plan_kernel,
        out_shape=[jax.ShapeDtypeStruct((TABLE,), s32), jax.ShapeDtypeStruct(words.shape, s32)],
        in_specs=[SMEM] * 4,
        out_specs=[SMEM] * 2,
        scratch_shapes=[pltpu.SMEM((128,), s32), pltpu.SMEM((256,), s32)] + [pltpu.SMEM((32,), s32)] * 6,
        name="plan",
        cost_estimate=pl.CostEstimate(flops=1000, bytes_accessed=30_000_000, transcendentals=0),
    )(me, inside_count, count, words)


def exchange(parts):
    got = [parts[0]]
    for k in range(1, 8):
        got.append(lax.ppermute(parts[k], "basis", [(i, i ^ k) for i in range(8)]))
    return got


def give_back(done):
    return lax.all_to_all(done, "basis", split_axis=0, concat_axis=0, tiled=True).reshape(-1, 72, 128)


def along_x(parts):
    return [lax.ppermute(parts[k - 1], "frag", [(i, i ^ (8 * k)) for i in range(32)]) for k in (1, 2, 3)]


def along_z(part):
    groups = [[8 * x + z for z in range(8)] for x in range(4)]
    return lax.all_to_all(part, "frag", 0, 0, tiled=True, axis_index_groups=groups)


def across(part):
    return lax.all_to_all(part, "frag", split_axis=0, concat_axis=0, tiled=True)


def after(value, *others):
    return lax.optimization_barrier((value, others))[0]


def shards(density, aux_factor, pairs, slot_of, costs):
    n_frag = lax.axis_size("frag")
    n_basis = lax.axis_size("basis")
    me_frag = lax.axis_index("frag").astype(jnp.int32)
    me_basis = lax.axis_index("basis").astype(jnp.int32)
    dimers = pairs.shape[0] * n_frag * n_basis

    lookup = pairs[:, :, None] == jnp.arange(slot_of.shape[0], dtype=jnp.int32)
    slots = jnp.sum(jnp.where(lookup, slot_of, 0), axis=2)
    mine = jnp.concatenate([slots[:, 0], slots[:, 1], costs, jnp.zeros(116, jnp.int32)])
    column = lax.all_to_all(
        jnp.broadcast_to(mine, (n_basis, 1, 128)), "basis", split_axis=0, concat_axis=0, tiled=True
    )
    column = column[:, 0, 0:12].reshape(n_basis, 3, 4).transpose(1, 0, 2).reshape(96)
    column = jnp.concatenate([column, jnp.zeros(32, jnp.int32)])
    every = across(jnp.broadcast_to(column, (n_frag, 1, 128)))
    a = every[:, 0, 0:32].reshape(dimers)
    b = every[:, 0, 32:64].reshape(dimers)
    cost = every[:, 0, 64:96].reshape(dimers)

    order = jnp.arange(dimers, dtype=jnp.int32)
    columns = jnp.arange(n_frag, dtype=jnp.int32)
    own_a, own_b = a // 32, b // 32
    low, high = jnp.minimum(own_a, own_b), jnp.maximum(own_a, own_b)
    pair_id = low * 32 + high
    inside = own_a == own_b
    mine_a = (own_a == me_frag) & jnp.logical_not(inside)
    mine_b = (own_b == me_frag) & jnp.logical_not(inside)
    other = jnp.where(mine_a, own_b, jnp.where(mine_b, own_a, -1))
    local = jnp.where(mine_a, a, b) & 31
    key = order * 256 + local * 8 + cost
    word = a + b * 1024 + cost * 1048576
    me_f, me_b = me_frag.reshape(1), me_basis.reshape(1)
    keep_first = (me_frag < columns) == ((me_frag + columns) % 2 == 0)
    home = (aux_factor, density)

    def one_round(carry):
        return body_round(carry)

    def body_round(carry):
        _, rest, dens, emb = carry
        open_dimer = rest > 0
        match = (other[None, :] == columns[:, None]) & open_dimer[None, :]
        keyed = jnp.where(match, key[None, :], BIG)
        key_0 = jnp.min(keyed, axis=1)
        key_1 = jnp.min(jnp.where(keyed > key_0[:, None], keyed, BIG), axis=1)
        here = jnp.where(keep_first, key_0, key_1)
        there = jnp.where(keep_first, key_1, key_0)
        send_1 = jnp.where(there < BIG, (there >> 3) & 31, -1)
        base_1 = jnp.where(here < BIG, (here >> 3) & 31, -1)
        steps_1 = jnp.where(here < BIG, here & 7, 0)

        (out_1,) = pack((send_1,), me_b, lambda t, me, n, row: t[0][row], 1, 32, home, [])
        in_1 = across(out_1)

        weight = steps_1 * 64 - columns
        rank = jnp.sum((weight[None, :] > weight[:, None]).astype(jnp.int32), axis=1)
        ranked = jnp.sum(jnp.where(rank[None, :] == columns[:, None], columns[None, :], 0), axis=1)
        table_1 = jnp.concatenate([send_1, base_1, steps_1, ranked])

        earlier = (pair_id[:, None] == pair_id[None, :]) & (order[None, :] < order[:, None])
        earlier = jnp.sum(jnp.where(earlier & open_dimer[None, :], 1, 0), axis=1)
        flagged = open_dimer & ((earlier >= 2) | inside)
        ahead = jnp.sum(jnp.where((order[None, :] < order[:, None]) & flagged[None, :], 1, 0), axis=1)
        ahead = jnp.where(flagged, ahead, -1)
        words = jnp.sum(jnp.where(ahead[None, :] == order[:, None], word[None, :], 0), axis=1)
        count = jnp.sum(jnp.where(flagged, 1, 0)).reshape(1)
        inside_here = (own_a[None, :] == columns[:, None]) & (inside & open_dimer)[None, :]
        inside_count = jnp.sum(jnp.where(inside_here, 1, 0), axis=1)
        table_2, listed = plan_rest(me_f, inside_count, count, words)
        listed = jnp.where(order < count, listed, 0)
        left = jnp.sum(jnp.where(ahead[:, None] == order[None, :], listed[None, :], 0), axis=1)
        tables = (table_1, table_2)

        def served(t, me, n, row):
            return t[0][RANKED + ranked_at(lax.bitwise_xor(me, n), row)]

        home_1 = exchange(
            pack(tables[:1], me_b, lambda t, me, n, row: t[0][BASE + served(t, me, n, row)], 8, 4, home, [])
        )
        in_x = along_x(pack(tables, me_b, lambda t, me, n, row: t[1][SENT + n * KX + row], 3, KX, home, []))

        def home_at(t, me, n, row):
            return t[1][HOME + 2 * lax.bitwise_xor(me, n) + row]

        home_2 = exchange(pack(tables, me_b, home_at, 8, 2, home, []))
        parts_1 = pack(tables, me_b, served, 8, 4, (), [in_1])
        away_1 = exchange(parts_1)
        (out_2,) = pack(
            tables, me_b, lambda t, me, n, row: t[1][RELAY + row], 1, NZ, home, after(in_x, parts_1)
        )
        in_z = along_z(out_2)

        one = lambda i, *_: (i, 0, 0)
        ready_1 = run_dimers(kernel_1, 4, (table_1, me_b), (1, 1), (one, one), [*home_1, *away_1])
        done_1 = give_back(ready_1)

        def late_at(t, me, n, row):
            return t[1][LATE + 2 * lax.bitwise_xor(me, n) + row] - 32

        late_parts = pack(tables, me_b, late_at, 8, 2, (), [*in_x, after(in_z, away_1)])
        late_2 = exchange(late_parts)
        whole = lambda i, *_: (0, 0, 0)
        ready_2 = run_dimers(kernel_2, 2, (table_2, me_b), (2, 2), (whole, whole), [*home_2, *late_2])

        def place_1(t, row):
            return t[0][RANKED + ranked_at(row // 8, row % 8 // 2)]

        def place_2(t, row):
            at = row // 2
            return jnp.where(t[1][STEPS + at] > 0, t[1][POS + row], -1)

        (ret_1,) = place(
            tables, me_b, [done_1], [lambda t, me, row: jnp.where(row % 2 == 1, place_1(t, row), -1)], [32]
        )
        back_1 = across(ret_1)
        done_2 = give_back(after(ready_2, back_1))
        (ret_2,) = place(tables, me_b, [done_2], [lambda t, me, row: place_2(t, row) - 32], [32])
        back_2 = across(ret_2)
        finds = [
            lambda t, me, row: jnp.where(row % 2 == 0, t[0][BASE + place_1(t, row)], -1),
            lambda t, me, row: place_2(t, row),
            lambda t, me, row: t[0][OUT + row],
        ]
        dens, emb = add_up(tables, me_b, [done_1, done_2, back_1], finds, dens, emb)
        dens, emb = add_up(tables, me_b, [back_2], [lambda t, me, row: t[1][BACK + row]], dens, emb)
        return jnp.sum(left), left, dens, emb

    start = (
        jnp.int32(dimers),
        jnp.ones(dimers, jnp.int32),
        jnp.zeros(density.shape, F32),
        jnp.zeros((density.shape[0], aux_factor.shape[2]), F32),
    )
    _, _, dens, emb = lax.while_loop(lambda carry: carry[0] > 0, one_round, start)
    return dens, emb


def solution(mesh):
    return jax.shard_map(
        shards,
        mesh=mesh,
        in_specs=(
            P("frag", "basis", None),
            P("frag", None, "basis"),
            P(("frag", "basis"), None),
            P(),
            P(("frag", "basis")),
        ),
        out_specs=(P("frag", "basis", None), P("frag", "basis")),
        check_vma=False,
    )
```

```python
import jax
import jax.numpy as jnp
from jax import lax
from jax.experimental import pallas as pl
from jax.experimental.pallas import tpu as pltpu
from jax.sharding import PartitionSpec as P


COUPLE = 0.015625
BIG = 1 << 30
BF16 = jnp.bfloat16
F32 = jnp.float32
KX, KZ = 6, 2
NX, NZ = 3 * KX, 8 * KZ
SENT, RELAY, POS, BACK, HOME, LATE, STEPS, MODE, TABLE = 0, 32, 64, 96, 128, 160, 192, 224, 256
OUT, BASE, STEP1, RANKED = 0, 32, 64, 96

VMEM = pl.BlockSpec(memory_space=pltpu.VMEM)
SMEM = pl.BlockSpec(memory_space=pltpu.SMEM)


def loop(count, body):
    def step(n, unused):
        body(n)
        return unused

    lax.fori_loop(0, count, step, 0)


def ranked_at(device, place):
    return place * 8 + jnp.where(place % 2 == 0, device, 7 - device)


def pack(tables, me, find, outs, rows, home, items):
    sizes = ([32] if home else []) + [item.shape[0] for item in items]

    def kernel(*refs):
        table_refs, me_ref, refs = refs[: len(tables)], refs[len(tables)], refs[len(tables) + 1 :]
        sources, out_refs = refs[: len(refs) - outs], refs[len(refs) - outs :]
        for n, out_ref in enumerate(out_refs):

            def body(row, n=n, out_ref=out_ref):
                at = jnp.maximum(find(table_refs, me_ref[0], n, row), 0)
                base, left = 0, list(sources)
                for which, size in enumerate(sizes):
                    here = (at >= base) & (at < base + size)
                    if home and which == 0:
                        aux_ref, den_ref = left.pop(0), left.pop(0)

                        @pl.when(here)
                        def _(aux_ref=aux_ref, den_ref=den_ref):
                            out_ref[row, 0:256, :] = aux_ref[at]
                            block = den_ref[at]
                            out_ref[row, 256:288, :] = block[:, 0:128]
                            out_ref[row, 288:320, :] = block[:, 128:256]
                    else:
                        item_ref = left.pop(0)

                        @pl.when(here)
                        def _(item_ref=item_ref, base=base):
                            out_ref[row] = item_ref[at - base]

                    base += size

            loop(rows, body)

    sources = list(home) + list(items)
    return pl.pallas_call(
        kernel,
        out_shape=[jax.ShapeDtypeStruct((rows, 320, 128), BF16)] * outs,
        in_specs=[SMEM] * (len(tables) + 1) + [VMEM] * len(sources),
        out_specs=[VMEM] * outs,
        name="pack",
    )(*tables, me, *sources)


def place(tables, me, parts, finds, out_rows):
    def kernel(*refs):
        table_refs, me_ref, refs = refs[: len(tables)], refs[len(tables)], refs[len(tables) + 1 :]
        for part_ref, find in zip(refs[: len(parts)], finds, strict=True):

            def body(row, part_ref=part_ref, find=find):
                at = find(table_refs, me_ref[0], row)
                base = 0
                for out_ref, size in zip(refs[len(parts) :], out_rows, strict=True):

                    @pl.when((at >= base) & (at < base + size))
                    def _(out_ref=out_ref, base=base):
                        out_ref[at - base] = part_ref[row]

                    base += size

            loop(part_ref.shape[0], body)

    return pl.pallas_call(
        kernel,
        out_shape=[jax.ShapeDtypeStruct((size, 72, 128), BF16) for size in out_rows],
        in_specs=[SMEM] * (len(tables) + 1) + [VMEM] * len(parts),
        out_specs=[VMEM] * len(out_rows),
        name="place",
    )(*tables, me, *parts)


def add_up(tables, me, parts, finds, dens, emb):
    def kernel(*refs):
        table_refs, me_ref, refs = refs[: len(tables)], refs[len(tables)], refs[len(tables) + 1 :]
        dens_in, emb_in, dens_ref, emb_ref = refs[len(parts) :]
        dens_ref[...] = dens_in[...]
        emb_ref[...] = emb_in[...]
        for part_ref, find in zip(refs[: len(parts)], finds, strict=True):

            def body(row, part_ref=part_ref, find=find):
                slot = find(table_refs, me_ref[0], row)

                @pl.when((slot >= 0) & (slot < 32))
                def _():
                    dens_ref[slot, :, 0:128] += part_ref[row, 0:32, :].astype(F32)
                    dens_ref[slot, :, 128:256] += part_ref[row, 32:64, :].astype(F32)
                    emb_ref[pl.ds(slot, 1), :] += part_ref[row, 64:72, :].astype(F32)[0:1, :]

            loop(part_ref.shape[0], body)

    first = len(tables) + 1 + len(parts)
    return pl.pallas_call(
        kernel,
        out_shape=[jax.ShapeDtypeStruct(dens.shape, F32), jax.ShapeDtypeStruct(emb.shape, F32)],
        in_specs=[SMEM] * (len(tables) + 1) + [VMEM] * (len(parts) + 2),
        out_specs=[VMEM, VMEM],
        input_output_aliases={first: 0, first + 1: 1},
        name="add_up",
    )(*tables, me, *parts, dens, emb)


def take(half, me, parts, row, stacked, dens):
    for n in range(8):
        lanes = slice(n * 128, n * 128 + 128)
        at = pl.multiple_of(lax.bitwise_xor(me, n) * 32, 32)
        stacked[half : half + 256, lanes] = parts[n][row, 0:256, :]
        dens[pl.ds(half + at, 32), 0:128] = parts[n][row, 256:288, :]
        dens[pl.ds(half + at, 32), 128:256] = parts[n][row, 288:320, :]


def one_dimer(steps, me, load, out, scratch):
    stacked, weighted, dens, current = scratch

    @pl.when(steps > 0)
    def _():
        load()
        fits = []
        for half in (0, 256):
            block = dens[half : half + 256, :]
            sums = []
            for n in range(4):
                lanes = slice(n * 256, n * 256 + 256)
                factor = stacked[half : half + 256, lanes]
                projected = jnp.dot(block, factor, preferred_element_type=F32)
                sums.append(jnp.sum(factor.astype(F32) * projected, axis=0, keepdims=True))
            fits.append(jnp.concatenate(sums, axis=1).astype(BF16).astype(F32))
        coeff = fits[0] + fits[1]

        def weigh(n):
            rows = pl.ds(pl.multiple_of(n * 64, 64), 64)
            weighted[rows, :] = (stacked[rows, :].astype(F32) * coeff).astype(BF16)

        loop(8, weigh)
        coulomb = lax.dot_general(
            weighted[...], stacked[...], (((1,), (1,)), ((), ())), preferred_element_type=F32
        )
        row_at = lax.broadcasted_iota(jnp.int32, (256, 512), 0)
        col_at = lax.broadcasted_iota(jnp.int32, (256, 512), 1)
        blank = jnp.zeros((256, 256), F32)
        for half in (0, 256):
            own = dens[half : half + 256, :].astype(F32)
            wide = jnp.concatenate([own, blank] if half == 0 else [blank, own], axis=1)
            eye = jnp.where(row_at + half == col_at, 0.5, 0.0)
            current[half : half + 256, :] = (eye + wide + COUPLE * coulomb[half : half + 256, :]).astype(BF16)

        def purify(index, unused):
            whole = current[...]
            square = jnp.dot(whole, whole, preferred_element_type=F32)
            cube = jnp.dot(square.astype(BF16), whole, preferred_element_type=F32)
            current[...] = (3.0 * square - 2.0 * cube).astype(BF16)
            return unused

        lax.fori_loop(0, steps, purify, 0)
        row_at = lax.broadcasted_iota(jnp.int32, (256, 256), 0)
        col_at = lax.broadcasted_iota(jnp.int32, (256, 256), 1)
        eye = jnp.where(row_at == col_at, 0.5, 0.0)
        for half in (0, 256):
            own = slice(half, half + 256)
            change = current[own, own].astype(F32) - dens[own, :].astype(F32) - eye
            dens[own, :] = change.astype(BF16)
        for n in range(8):
            to = lax.bitwise_xor(me, n)
            at = pl.multiple_of(to * 32, 32)
            lanes = slice(n * 128, n * 128 + 128)
            for r in range(2):
                change = dens[pl.ds(r * 256 + at, 32), :]
                out[to, r, 0:32, :] = change[:, 0:128]
                out[to, r, 32:64, :] = change[:, 128:256]
                partner = jnp.broadcast_to(fits[1 - r][:, lanes], (8, 128))
                out[to, r, 64:72, :] = partner.astype(BF16)


SCRATCH = [
    pltpu.VMEM((512, 1024), BF16),
    pltpu.VMEM((512, 1024), BF16),
    pltpu.VMEM((512, 256), BF16),
    pltpu.VMEM((512, 512), BF16),
]


def run_dimers(kernel, count, tables, blocks, maps, parts):
    specs = []
    for block, index_map in zip(blocks, maps, strict=True):
        specs += [pl.BlockSpec((block, 320, 128), index_map)] * 8
    return pl.pallas_call(
        kernel,
        out_shape=jax.ShapeDtypeStruct((8, 2 * count, 72, 128), BF16),
        grid_spec=pltpu.PrefetchScalarGridSpec(
            num_scalar_prefetch=2,
            grid=(count,),
            in_specs=specs,
            out_specs=pl.BlockSpec((8, 2, 72, 128), lambda i, *_: (0, i, 0, 0)),
            scratch_shapes=SCRATCH,
        ),
        name="dimers",
        cost_estimate=pl.CostEstimate(
            flops=count * 4_000_000_000, bytes_accessed=count * 1_500_000, transcendentals=0
        ),
    )(*tables, *parts)


def kernel_1(table_ref, me_ref, *refs):
    me, i = me_ref[0], pl.program_id(0)
    first, second, out, scratch = refs[0:8], refs[8:16], refs[16], refs[17:]
    stacked, dens = scratch[0], scratch[2]

    def load():
        take(0, me, first, 0, stacked, dens)
        take(256, me, second, 0, stacked, dens)

    other = table_ref[RANKED + ranked_at(me, i)]
    one_dimer(table_ref[STEP1 + other], me, load, out, scratch)


def kernel_2(table_ref, me_ref, *refs):
    me, i = me_ref[0], pl.program_id(0)
    home, late, out, scratch = refs[0:8], refs[8:16], refs[16], refs[17:]
    stacked, dens = scratch[0], scratch[2]
    split = table_ref[MODE + me] > 0

    def load():
        both_late = split & (i == 0)
        both_home = split & (i == 1)

        @pl.when(both_late)
        def _():
            take(0, me, late, 0, stacked, dens)

        @pl.when(jnp.logical_not(both_late))
        def _():
            take(0, me, home, jnp.where(split, 0, i), stacked, dens)

        @pl.when(both_home)
        def _():
            take(256, me, home, 1, stacked, dens)

        @pl.when(jnp.logical_not(both_home))
        def _():
            take(256, me, late, jnp.where(split, 1, i), stacked, dens)

    one_dimer(table_ref[STEPS + 2 * me + i], me, load, out, scratch)


def plan_kernel(me_ref, inside_ref, count_ref, list_ref, table_ref, left_ref, to_x, to_z, n_direct, n_third, n_self, n_split, room, taken, mine):
    me = me_ref[0]
    me_x, me_z = me >> 3, me & 7

    def clear(n):
        for i in range(8):
            to_z[n * 8 + i] = 0
            table_ref[n * 8 + i] = jnp.where(n < STEPS // 8, -1, 0)

    def clear_x(n):
        for i in range(8):
            to_x[n * 8 + i] = 0

    def clear_c(n):
        n_direct[n] = 0
        n_third[n] = 0
        n_self[n] = 0
        n_split[n] = inside_ref[n]
        room[n] = 1 + inside_ref[n]
        taken[n] = 0

    loop(TABLE // 8, clear)
    loop(16, clear_x)
    loop(32, clear_c)

    def put(at, good, spare, value):
        table_ref[jnp.where(good, at, spare)] = value

    def can(o, c, extra):
        zo, xc, zc = o & 7, c >> 3, c & 7
        free = ((taken[c] >> o) & 1) == 0
        return free & (to_x[o * 4 + xc] < KX) & ((zo == zc) | (to_z[xc * 64 + zo * 8 + zc] + extra < KZ))

    def send(o, slot, c, at_x, at_z, n_x, n_z):
        xo, zo, xc, zc = o >> 3, o & 7, c >> 3, c & 7
        move_x, move_z = xo != xc, zo != zc
        taken[c] = taken[c] | lax.shift_left(jnp.int32(1), o)
        to_x[at_x] = n_x + jnp.where(move_x, 1, 0)
        to_z[at_z] = n_z + jnp.where(move_z, 1, 0)
        in_x = (lax.bitwise_xor(xo, xc) - 1) * KX + n_x

        @pl.when(zo == me_z)
        def _():
            put(SENT + in_x, move_x & (o == me), SENT + 31, slot)
            put(BACK + c, o == me, SENT + 31, slot)
            put(RELAY + zc * KZ + n_z, move_z & (xc == me_x), RELAY + 31, jnp.where(move_x, 32 + in_x, slot))

        return jnp.where(move_z, 32 + NX + zo * KZ + n_z, 32 + in_x)

    def visit(d):
        word = list_ref[d]
        cost = word >> 20
        la, oa, lb, ob = word & 31, (word >> 5) & 31, (word >> 10) & 31, (word >> 15) & 31
        left_ref[d] = 0
        za, xa, zb, xb = oa & 7, oa >> 3, ob & 7, ob >> 3
        x_at_a, z_at_a = ob * 4 + xa, xa * 64 + zb * 8 + za
        x_at_b, z_at_b = oa * 4 + xb, xb * 64 + za * 8 + zb
        x_a, z_a, x_b, z_b = to_x[x_at_a], to_z[z_at_a], to_x[x_at_b], to_z[z_at_b]
        room_a, room_b = room[oa], room[ob]
        free_a, free_b = ((taken[oa] >> ob) & 1) == 0, ((taken[ob] >> oa) & 1) == 0
        can_a = free_a & (x_a < KX) & (z_a < KZ) & (room_a <= 8)
        can_b = free_b & (x_b < KX) & (z_b < KZ) & (room_b <= 8)
        use_a = can_a & (jnp.logical_not(can_b) | (z_a * 4 + room_a <= z_b * 4 + room_b))
        apart = oa != ob
        direct = apart & (can_a | can_b)

        @pl.when(direct)
        def _():
            c, o = jnp.where(use_a, oa, ob), jnp.where(use_a, ob, oa)
            stay, move = jnp.where(use_a, la, lb), jnp.where(use_a, lb, la)
            at = n_direct[c]
            n_direct[c] = at + 1
            room[c] = ((at + 3) >> 1) + n_split[c]
            late = send(
                o,
                move,
                c,
                jnp.where(use_a, x_at_a, x_at_b),
                jnp.where(use_a, z_at_a, z_at_b),
                jnp.where(use_a, x_a, x_b),
                jnp.where(use_a, z_a, z_b),
            )

            @pl.when(c == me)
            def _():
                mine[at * 4] = stay
                mine[at * 4 + 1] = 32 + o
                mine[at * 4 + 2] = late
                mine[at * 4 + 3] = cost

        @pl.when(jnp.logical_not(direct))
        def _():
            @pl.when(jnp.logical_not(apart))
            def _():
                q = n_self[oa]

                @pl.when(q < 8)
                def _():
                    n_self[oa] = q + 1

                    @pl.when(oa == me)
                    def _():
                        at = 2 * (7 - q)
                        table_ref[POS + 2 * at + 2] = la
                        table_ref[POS + 2 * at + 3] = lb
                        table_ref[HOME + at] = la
                        table_ref[HOME + at + 1] = lb
                        table_ref[STEPS + at + 1] = cost
                        table_ref[MODE + 7 - q] = 1

                @pl.when(q >= 8)
                def _():
                    left_ref[d] = 1

            @pl.when(apart)
            def _():
                same_z = jnp.where(za == zb, 1, 0)

                def look(carry):
                    n, _ = carry
                    turn = ((d + n) & 3) * 8
                    c = jnp.where(n < 4, turn + za, jnp.where(n < 8, turn + zb, (d + n) & 31))
                    fit = ((n_direct[c] + 1) >> 1) + jnp.maximum(n_third[c] + 1, inside_ref[c]) <= 8
                    good = fit & can(oa, c, same_z) & can(ob, c, same_z) & (c != oa) & (c != ob)
                    return n + 1, jnp.where(good, c, -1)

                _, c = lax.while_loop(
                    lambda carry: (carry[0] < 40) & (carry[1] < 0), look, (jnp.int32(0), jnp.int32(-1))
                )

                @pl.when(c < 0)
                def _():
                    left_ref[d] = 1

                @pl.when(c >= 0)
                def _():
                    t = n_third[c]
                    n_third[c] = t + 1
                    split = jnp.maximum(t + 1, inside_ref[c])
                    n_split[c] = split
                    room[c] = ((n_direct[c] + 2) >> 1) + split
                    xc, zc = c >> 3, c & 7
                    x_at, z_at = oa * 4 + xc, xc * 64 + za * 8 + zc
                    late_a = send(oa, la, c, x_at, z_at, to_x[x_at], to_z[z_at])
                    x_at, z_at = ob * 4 + xc, xc * 64 + zb * 8 + zc
                    late_b = send(ob, lb, c, x_at, z_at, to_x[x_at], to_z[z_at])

                    @pl.when(c == me)
                    def _():
                        at = 2 * (7 - t)
                        table_ref[POS + 2 * at] = 32 + oa
                        table_ref[POS + 2 * at + 1] = 32 + ob
                        table_ref[LATE + at] = late_a
                        table_ref[LATE + at + 1] = late_b
                        table_ref[STEPS + at] = cost
                        table_ref[MODE + 7 - t] = 1

    loop(count_ref[0], visit)
    devices = 8 - jnp.maximum(n_third[me], n_self[me])

    def settle(n):
        second = n >= devices
        at = 2 * jnp.where(second, n - devices, n) + jnp.where(second, 1, 0)
        table_ref[POS + 2 * at] = mine[n * 4]
        table_ref[POS + 2 * at + 1] = mine[n * 4 + 1]
        table_ref[HOME + at] = mine[n * 4]
        table_ref[LATE + at] = mine[n * 4 + 2]
        table_ref[STEPS + at] = mine[n * 4 + 3]

    loop(n_direct[me], settle)


def plan_rest(me, inside_count, count, words):
    s32 = jnp.int32
    return pl.pallas_call(
        plan_kernel,
        out_shape=[jax.ShapeDtypeStruct((TABLE,), s32), jax.ShapeDtypeStruct(words.shape, s32)],
        in_specs=[SMEM] * 4,
        out_specs=[SMEM] * 2,
        scratch_shapes=[pltpu.SMEM((128,), s32), pltpu.SMEM((256,), s32)] + [pltpu.SMEM((32,), s32)] * 6 + [pltpu.SMEM((64,), s32)],
        name="plan",
        cost_estimate=pl.CostEstimate(flops=1000, bytes_accessed=30_000_000, transcendentals=0),
    )(me, inside_count, count, words)


def exchange(parts):
    got = [parts[0]]
    for k in range(1, 8):
        got.append(lax.ppermute(parts[k], "basis", [(i, i ^ k) for i in range(8)]))
    return got


def give_back(done):
    return lax.all_to_all(done, "basis", split_axis=0, concat_axis=0, tiled=True).reshape(-1, 72, 128)


def along_x(parts):
    return [lax.ppermute(parts[k - 1], "frag", [(i, i ^ (8 * k)) for i in range(32)]) for k in (1, 2, 3)]


def along_z(part):
    groups = [[8 * x + z for z in range(8)] for x in range(4)]
    return lax.all_to_all(part, "frag", 0, 0, tiled=True, axis_index_groups=groups)


def across(part):
    return lax.all_to_all(part, "frag", split_axis=0, concat_axis=0, tiled=True)


def after(value, *others):
    return lax.optimization_barrier((value, others))[0]


def shards(density, aux_factor, pairs, slot_of, costs):
    n_frag = lax.axis_size("frag")
    n_basis = lax.axis_size("basis")
    me_frag = lax.axis_index("frag").astype(jnp.int32)
    me_basis = lax.axis_index("basis").astype(jnp.int32)
    dimers = pairs.shape[0] * n_frag * n_basis

    lookup = pairs[:, :, None] == jnp.arange(slot_of.shape[0], dtype=jnp.int32)
    slots = jnp.sum(jnp.where(lookup, slot_of, 0), axis=2)
    mine = jnp.concatenate([slots[:, 0], slots[:, 1], costs, jnp.zeros(116, jnp.int32)])
    column = lax.all_to_all(
        jnp.broadcast_to(mine, (n_basis, 1, 128)), "basis", split_axis=0, concat_axis=0, tiled=True
    )
    column = column[:, 0, 0:12].reshape(n_basis, 3, 4).transpose(1, 0, 2).reshape(96)
    column = jnp.concatenate([column, jnp.zeros(32, jnp.int32)])
    every = across(jnp.broadcast_to(column, (n_frag, 1, 128)))
    a = every[:, 0, 0:32].reshape(dimers)
    b = every[:, 0, 32:64].reshape(dimers)
    cost = every[:, 0, 64:96].reshape(dimers)

    order = jnp.arange(dimers, dtype=jnp.int32)
    columns = jnp.arange(n_frag, dtype=jnp.int32)
    own_a, own_b = a // 32, b // 32
    low, high = jnp.minimum(own_a, own_b), jnp.maximum(own_a, own_b)
    pair_id = low * 32 + high
    inside = own_a == own_b
    mine_a = (own_a == me_frag) & jnp.logical_not(inside)
    mine_b = (own_b == me_frag) & jnp.logical_not(inside)
    other = jnp.where(mine_a, own_b, jnp.where(mine_b, own_a, -1))
    local = jnp.where(mine_a, a, b) & 31
    key = order * 256 + local * 8 + cost
    word = a + b * 1024 + cost * 1048576
    me_f, me_b = me_frag.reshape(1), me_basis.reshape(1)
    keep_first = (me_frag < columns) == ((me_frag + columns) % 2 == 0)
    home = (aux_factor, density)

    def one_round(carry):
        return body_round(carry)

    def body_round(carry):
        _, rest, dens, emb = carry
        open_dimer = rest > 0
        match = (other[None, :] == columns[:, None]) & open_dimer[None, :]
        keyed = jnp.where(match, key[None, :], BIG)
        key_0 = jnp.min(keyed, axis=1)
        key_1 = jnp.min(jnp.where(keyed > key_0[:, None], keyed, BIG), axis=1)
        here = jnp.where(keep_first, key_0, key_1)
        there = jnp.where(keep_first, key_1, key_0)
        send_1 = jnp.where(there < BIG, (there >> 3) & 31, -1)
        base_1 = jnp.where(here < BIG, (here >> 3) & 31, -1)
        steps_1 = jnp.where(here < BIG, here & 7, 0)

        (out_1,) = pack((send_1,), me_b, lambda t, me, n, row: t[0][row], 1, 32, home, [])
        in_1 = across(out_1)

        weight = steps_1 * 64 - columns
        rank = jnp.sum((weight[None, :] > weight[:, None]).astype(jnp.int32), axis=1)
        ranked = jnp.sum(jnp.where(rank[None, :] == columns[:, None], columns[None, :], 0), axis=1)
        table_1 = jnp.concatenate([send_1, base_1, steps_1, ranked])

        earlier = (pair_id[:, None] == pair_id[None, :]) & (order[None, :] < order[:, None])
        earlier = jnp.sum(jnp.where(earlier & open_dimer[None, :], 1, 0), axis=1)
        flagged = open_dimer & ((earlier >= 2) | inside)
        turn = order + jnp.where(inside, 2 * dimers, dimers * (2 - jnp.clip(earlier - 2, 0, 2)))
        ahead = jnp.sum(jnp.where((turn[None, :] < turn[:, None]) & flagged[None, :], 1, 0), axis=1)
        ahead = jnp.where(flagged, ahead, -1)
        words = jnp.sum(jnp.where(ahead[None, :] == order[:, None], word[None, :], 0), axis=1)
        count = jnp.sum(jnp.where(flagged, 1, 0)).reshape(1)
        inside_here = (own_a[None, :] == columns[:, None]) & (inside & open_dimer)[None, :]
        inside_count = jnp.sum(jnp.where(inside_here, 1, 0), axis=1)
        table_2, listed = plan_rest(me_f, inside_count, count, words)
        listed = jnp.where(order < count, listed, 0)
        left = jnp.sum(jnp.where(ahead[:, None] == order[None, :], listed[None, :], 0), axis=1)
        tables = (table_1, table_2)

        def served(t, me, n, row):
            return t[0][RANKED + ranked_at(lax.bitwise_xor(me, n), row)]

        home_1 = exchange(
            pack(tables[:1], me_b, lambda t, me, n, row: t[0][BASE + served(t, me, n, row)], 8, 4, home, [])
        )
        in_x = along_x(pack(tables, me_b, lambda t, me, n, row: t[1][SENT + n * KX + row], 3, KX, home, []))

        def home_at(t, me, n, row):
            return t[1][HOME + 2 * lax.bitwise_xor(me, n) + row]

        home_2 = exchange(pack(tables, me_b, home_at, 8, 2, home, []))
        parts_1 = pack(tables, me_b, served, 8, 4, (), [in_1])
        away_1 = exchange(parts_1)
        (out_2,) = pack(
            tables, me_b, lambda t, me, n, row: t[1][RELAY + row], 1, NZ, home, after(in_x, parts_1)
        )
        in_z = along_z(out_2)

        one = lambda i, *_: (i, 0, 0)
        ready_1 = run_dimers(kernel_1, 4, (table_1, me_b), (1, 1), (one, one), [*home_1, *away_1])
        done_1 = give_back(after(ready_1, in_z))

        def place_1(t, row):
            return t[0][RANKED + ranked_at(row // 8, row % 8 // 2)]

        def place_2(t, row):
            at = row // 2
            return jnp.where(t[1][STEPS + at] > 0, t[1][POS + row], -1)

        (ret_1,) = place(
            tables, me_b, [done_1], [lambda t, me, row: jnp.where(row % 2 == 1, place_1(t, row), -1)], [32]
        )
        back_1 = across(ret_1)

        def late_at(t, me, n, row):
            return t[1][LATE + 2 * lax.bitwise_xor(me, n) + row] - 32

        late_parts = pack(tables, me_b, late_at, 8, 2, (), [*in_x, after(in_z, ret_1)])
        late_2 = exchange(late_parts)
        whole = lambda i, *_: (0, 0, 0)
        ready_2 = run_dimers(kernel_2, 2, (table_2, me_b), (2, 2), (whole, whole), [*home_2, *late_2])
        done_2 = give_back(after(ready_2, back_1))
        (ret_2,) = place(tables, me_b, [done_2], [lambda t, me, row: place_2(t, row) - 32], [32])
        back_2 = across(ret_2)
        finds = [
            lambda t, me, row: jnp.where(row % 2 == 0, t[0][BASE + place_1(t, row)], -1),
            lambda t, me, row: place_2(t, row),
            lambda t, me, row: t[0][OUT + row],
        ]
        dens, emb = add_up(tables, me_b, [done_1, done_2, back_1], finds, dens, emb)
        dens, emb = add_up(tables, me_b, [back_2], [lambda t, me, row: t[1][BACK + row]], dens, emb)
        return jnp.sum(left), left, dens, emb

    start = (
        jnp.int32(dimers),
        jnp.ones(dimers, jnp.int32),
        jnp.zeros(density.shape, F32),
        jnp.zeros((density.shape[0], aux_factor.shape[2]), F32),
    )
    _, _, dens, emb = lax.while_loop(lambda carry: carry[0] > 0, one_round, start)
    return dens, emb


def solution(mesh):
    return jax.shard_map(
        shards,
        mesh=mesh,
        in_specs=(
            P("frag", "basis", None),
            P("frag", None, "basis"),
            P(("frag", "basis"), None),
            P(),
            P(("frag", "basis")),
        ),
        out_specs=(P("frag", "basis", None), P("frag", "basis")),
        check_vma=False,
    )
```

```python
import jax
import jax.numpy as jnp
from jax import lax
from jax.experimental import pallas as pl
from jax.experimental.pallas import tpu as pltpu
from jax.sharding import PartitionSpec as P


COUPLE = 0.015625
BIG = 1 << 30
BF16 = jnp.bfloat16
F32 = jnp.float32
KX, KZ = 6, 2
NX, NZ = 3 * KX, 8 * KZ
SENT, RELAY, POS, BACK, HOME, LATE, STEPS, MODE, TABLE = 0, 32, 64, 96, 128, 160, 192, 224, 256
OUT, BASE, STEP1, RANKED = 0, 32, 64, 96

VMEM = pl.BlockSpec(memory_space=pltpu.VMEM)
SMEM = pl.BlockSpec(memory_space=pltpu.SMEM)


def loop(count, body):
    def step(n, unused):
        body(n)
        return unused

    lax.fori_loop(0, count, step, 0)


def ranked_at(device, place):
    return place * 8 + jnp.where(place % 2 == 0, device, 7 - device)


def pack(tables, me, find, outs, rows, home, items):
    sizes = ([32] if home else []) + [item.shape[0] for item in items]

    def kernel(*refs):
        table_refs, me_ref, refs = refs[: len(tables)], refs[len(tables)], refs[len(tables) + 1 :]
        sources, out_refs = refs[: len(refs) - outs], refs[len(refs) - outs :]
        for n, out_ref in enumerate(out_refs):

            def body(row, n=n, out_ref=out_ref):
                at = jnp.maximum(find(table_refs, me_ref[0], n, row), 0)
                base, left = 0, list(sources)
                for which, size in enumerate(sizes):
                    here = (at >= base) & (at < base + size)
                    if home and which == 0:
                        aux_ref, den_ref = left.pop(0), left.pop(0)

                        @pl.when(here)
                        def _(aux_ref=aux_ref, den_ref=den_ref):
                            out_ref[row, 0:256, :] = aux_ref[at]
                            block = den_ref[at]
                            out_ref[row, 256:288, :] = block[:, 0:128]
                            out_ref[row, 288:320, :] = block[:, 128:256]
                    else:
                        item_ref = left.pop(0)

                        @pl.when(here)
                        def _(item_ref=item_ref, base=base):
                            out_ref[row] = item_ref[at - base]

                    base += size

            loop(rows, body)

    sources = list(home) + list(items)
    return pl.pallas_call(
        kernel,
        out_shape=[jax.ShapeDtypeStruct((rows, 320, 128), BF16)] * outs,
        in_specs=[SMEM] * (len(tables) + 1) + [VMEM] * len(sources),
        out_specs=[VMEM] * outs,
        name="pack",
    )(*tables, me, *sources)


def place(tables, me, parts, finds, out_rows):
    def kernel(*refs):
        table_refs, me_ref, refs = refs[: len(tables)], refs[len(tables)], refs[len(tables) + 1 :]
        for part_ref, find in zip(refs[: len(parts)], finds, strict=True):

            def body(row, part_ref=part_ref, find=find):
                at = find(table_refs, me_ref[0], row)
                base = 0
                for out_ref, size in zip(refs[len(parts) :], out_rows, strict=True):

                    @pl.when((at >= base) & (at < base + size))
                    def _(out_ref=out_ref, base=base):
                        out_ref[at - base] = part_ref[row]

                    base += size

            loop(part_ref.shape[0], body)

    return pl.pallas_call(
        kernel,
        out_shape=[jax.ShapeDtypeStruct((size, 72, 128), BF16) for size in out_rows],
        in_specs=[SMEM] * (len(tables) + 1) + [VMEM] * len(parts),
        out_specs=[VMEM] * len(out_rows),
        name="place",
    )(*tables, me, *parts)


def add_up(tables, me, parts, finds, dens, emb):
    def kernel(*refs):
        table_refs, me_ref, refs = refs[: len(tables)], refs[len(tables)], refs[len(tables) + 1 :]
        dens_in, emb_in, dens_ref, emb_ref = refs[len(parts) :]
        dens_ref[...] = dens_in[...]
        emb_ref[...] = emb_in[...]
        for part_ref, find in zip(refs[: len(parts)], finds, strict=True):

            def body(row, part_ref=part_ref, find=find):
                slot = find(table_refs, me_ref[0], row)

                @pl.when((slot >= 0) & (slot < 32))
                def _():
                    dens_ref[slot, :, 0:128] += part_ref[row, 0:32, :].astype(F32)
                    dens_ref[slot, :, 128:256] += part_ref[row, 32:64, :].astype(F32)
                    emb_ref[pl.ds(slot, 1), :] += part_ref[row, 64:72, :].astype(F32)[0:1, :]

            loop(part_ref.shape[0], body)

    first = len(tables) + 1 + len(parts)
    return pl.pallas_call(
        kernel,
        out_shape=[jax.ShapeDtypeStruct(dens.shape, F32), jax.ShapeDtypeStruct(emb.shape, F32)],
        in_specs=[SMEM] * (len(tables) + 1) + [VMEM] * (len(parts) + 2),
        out_specs=[VMEM, VMEM],
        input_output_aliases={first: 0, first + 1: 1},
        name="add_up",
    )(*tables, me, *parts, dens, emb)


def take(half, me, parts, row, stacked, dens):
    for n in range(8):
        lanes = slice(n * 128, n * 128 + 128)
        at = pl.multiple_of(lax.bitwise_xor(me, n) * 32, 32)
        stacked[half : half + 256, lanes] = parts[n][row, 0:256, :]
        dens[pl.ds(half + at, 32), 0:128] = parts[n][row, 256:288, :]
        dens[pl.ds(half + at, 32), 128:256] = parts[n][row, 288:320, :]


def one_dimer(steps, me, load, out, scratch):
    stacked, weighted, dens, current = scratch

    @pl.when(steps > 0)
    def _():
        load()
        fits = []
        for half in (0, 256):
            block = dens[half : half + 256, :]
            sums = []
            for n in range(4):
                lanes = slice(n * 256, n * 256 + 256)
                factor = stacked[half : half + 256, lanes]
                projected = jnp.dot(block, factor, preferred_element_type=F32)
                sums.append(jnp.sum(factor.astype(F32) * projected, axis=0, keepdims=True))
            fits.append(jnp.concatenate(sums, axis=1).astype(BF16).astype(F32))
        coeff = fits[0] + fits[1]

        def weigh(n):
            rows = pl.ds(pl.multiple_of(n * 64, 64), 64)
            weighted[rows, :] = (stacked[rows, :].astype(F32) * coeff).astype(BF16)

        loop(8, weigh)
        coulomb = lax.dot_general(
            weighted[...], stacked[...], (((1,), (1,)), ((), ())), preferred_element_type=F32
        )
        row_at = lax.broadcasted_iota(jnp.int32, (256, 512), 0)
        col_at = lax.broadcasted_iota(jnp.int32, (256, 512), 1)
        blank = jnp.zeros((256, 256), F32)
        for half in (0, 256):
            own = dens[half : half + 256, :].astype(F32)
            wide = jnp.concatenate([own, blank] if half == 0 else [blank, own], axis=1)
            eye = jnp.where(row_at + half == col_at, 0.5, 0.0)
            current[half : half + 256, :] = (eye + wide + COUPLE * coulomb[half : half + 256, :]).astype(BF16)

        def purify(index, unused):
            whole = current[...]
            square = jnp.dot(whole, whole, preferred_element_type=F32)
            cube = jnp.dot(square.astype(BF16), whole, preferred_element_type=F32)
            current[...] = (3.0 * square - 2.0 * cube).astype(BF16)
            return unused

        lax.fori_loop(0, steps, purify, 0)
        row_at = lax.broadcasted_iota(jnp.int32, (256, 256), 0)
        col_at = lax.broadcasted_iota(jnp.int32, (256, 256), 1)
        eye = jnp.where(row_at == col_at, 0.5, 0.0)
        for half in (0, 256):
            own = slice(half, half + 256)
            change = current[own, own].astype(F32) - dens[own, :].astype(F32) - eye
            dens[own, :] = change.astype(BF16)
        for n in range(8):
            to = lax.bitwise_xor(me, n)
            at = pl.multiple_of(to * 32, 32)
            lanes = slice(n * 128, n * 128 + 128)
            for r in range(2):
                change = dens[pl.ds(r * 256 + at, 32), :]
                target = out[0].at[to, r] if len(out) == 1 else out[n].at[r]
                target[0:32, :] = change[:, 0:128]
                target[32:64, :] = change[:, 128:256]
                partner = jnp.broadcast_to(fits[1 - r][:, lanes], (8, 128))
                target[64:72, :] = partner.astype(BF16)


SCRATCH = [
    pltpu.VMEM((512, 1024), BF16),
    pltpu.VMEM((512, 1024), BF16),
    pltpu.VMEM((512, 256), BF16),
    pltpu.VMEM((512, 512), BF16),
]


def run_dimers(kernel, count, tables, blocks, maps, parts, apart=False):
    rows = 2 * count
    shapes = [(rows, 72, 128)] * 8 if apart else [(8, rows, 72, 128)]
    out_block = pl.BlockSpec((2, 72, 128), lambda i, *_: (i, 0, 0))
    if not apart:
        out_block = pl.BlockSpec((8, 2, 72, 128), lambda i, *_: (0, i, 0, 0))
    specs = []
    for block, index_map in zip(blocks, maps, strict=True):
        specs += [pl.BlockSpec((block, 320, 128), index_map)] * 8
    return pl.pallas_call(
        kernel,
        out_shape=[jax.ShapeDtypeStruct(shape, BF16) for shape in shapes],
        grid_spec=pltpu.PrefetchScalarGridSpec(
            num_scalar_prefetch=2,
            grid=(count,),
            in_specs=specs,
            out_specs=[out_block] * len(shapes),
            scratch_shapes=SCRATCH,
        ),
        name="dimers",
        cost_estimate=pl.CostEstimate(
            flops=count * 4_000_000_000, bytes_accessed=count * 1_500_000, transcendentals=0
        ),
    )(*tables, *parts)


def kernel_1(table_ref, me_ref, *refs):
    me, i = me_ref[0], pl.program_id(0)
    first, second, out, scratch = refs[0:8], refs[8:16], refs[16:17], refs[17:]
    stacked, dens = scratch[0], scratch[2]

    def load():
        take(0, me, first, 0, stacked, dens)
        take(256, me, second, 0, stacked, dens)

    other = table_ref[RANKED + ranked_at(me, i)]
    one_dimer(table_ref[STEP1 + other], me, load, out, scratch)


def kernel_2(table_ref, me_ref, *refs):
    me, i = me_ref[0], pl.program_id(0)
    home, late, out, scratch = refs[0:8], refs[8:16], refs[16:24], refs[24:]
    stacked, dens = scratch[0], scratch[2]
    split = table_ref[MODE + me] > 0

    def load():
        both_late = split & (i == 0)
        both_home = split & (i == 1)

        @pl.when(both_late)
        def _():
            take(0, me, late, 0, stacked, dens)

        @pl.when(jnp.logical_not(both_late))
        def _():
            take(0, me, home, jnp.where(split, 0, i), stacked, dens)

        @pl.when(both_home)
        def _():
            take(256, me, home, 1, stacked, dens)

        @pl.when(jnp.logical_not(both_home))
        def _():
            take(256, me, late, jnp.where(split, 1, i), stacked, dens)

    one_dimer(table_ref[STEPS + 2 * me + i], me, load, out, scratch)


def plan_kernel(me_ref, inside_ref, count_ref, list_ref, table_ref, left_ref, to_x, to_z, n_direct, n_third, n_self, n_split, room, taken, mine):
    me = me_ref[0]
    me_x, me_z = me >> 3, me & 7

    def clear(n):
        for i in range(8):
            to_z[n * 8 + i] = 0
            table_ref[n * 8 + i] = jnp.where(n < STEPS // 8, -1, 0)

    def clear_x(n):
        for i in range(8):
            to_x[n * 8 + i] = 0

    def clear_c(n):
        n_direct[n] = 0
        n_third[n] = 0
        n_self[n] = 0
        n_split[n] = inside_ref[n]
        room[n] = 1 + inside_ref[n]
        taken[n] = 0

    loop(TABLE // 8, clear)
    loop(16, clear_x)
    loop(32, clear_c)

    def put(at, good, spare, value):
        table_ref[jnp.where(good, at, spare)] = value

    def can(o, c, extra):
        zo, xc, zc = o & 7, c >> 3, c & 7
        free = ((taken[c] >> o) & 1) == 0
        return free & (to_x[o * 4 + xc] < KX) & ((zo == zc) | (to_z[xc * 64 + zo * 8 + zc] + extra < KZ))

    def send(o, slot, c, at_x, at_z, n_x, n_z):
        xo, zo, xc, zc = o >> 3, o & 7, c >> 3, c & 7
        move_x, move_z = xo != xc, zo != zc
        taken[c] = taken[c] | lax.shift_left(jnp.int32(1), o)
        to_x[at_x] = n_x + jnp.where(move_x, 1, 0)
        to_z[at_z] = n_z + jnp.where(move_z, 1, 0)
        in_x = (lax.bitwise_xor(xo, xc) - 1) * KX + n_x

        @pl.when(zo == me_z)
        def _():
            put(SENT + in_x, move_x & (o == me), SENT + 31, slot)
            put(BACK + c, o == me, SENT + 31, slot)
            put(RELAY + zc * KZ + n_z, move_z & (xc == me_x), RELAY + 31, jnp.where(move_x, 32 + in_x, slot))

        return jnp.where(move_z, 32 + NX + zo * KZ + n_z, 32 + in_x)

    def visit(d):
        word = list_ref[d]
        cost = word >> 20
        la, oa, lb, ob = word & 31, (word >> 5) & 31, (word >> 10) & 31, (word >> 15) & 31
        left_ref[d] = 0
        za, xa, zb, xb = oa & 7, oa >> 3, ob & 7, ob >> 3
        x_at_a, z_at_a = ob * 4 + xa, xa * 64 + zb * 8 + za
        x_at_b, z_at_b = oa * 4 + xb, xb * 64 + za * 8 + zb
        x_a, z_a, x_b, z_b = to_x[x_at_a], to_z[z_at_a], to_x[x_at_b], to_z[z_at_b]
        room_a, room_b = room[oa], room[ob]
        free_a, free_b = ((taken[oa] >> ob) & 1) == 0, ((taken[ob] >> oa) & 1) == 0
        can_a = free_a & (x_a < KX) & (z_a < KZ) & (room_a <= 8)
        can_b = free_b & (x_b < KX) & (z_b < KZ) & (room_b <= 8)
        use_a = can_a & (jnp.logical_not(can_b) | (z_a * 4 + room_a <= z_b * 4 + room_b))
        apart = oa != ob
        direct = apart & (can_a | can_b)

        @pl.when(direct)
        def _():
            c, o = jnp.where(use_a, oa, ob), jnp.where(use_a, ob, oa)
            stay, move = jnp.where(use_a, la, lb), jnp.where(use_a, lb, la)
            at = n_direct[c]
            n_direct[c] = at + 1
            room[c] = ((at + 3) >> 1) + n_split[c]
            late = send(
                o,
                move,
                c,
                jnp.where(use_a, x_at_a, x_at_b),
                jnp.where(use_a, z_at_a, z_at_b),
                jnp.where(use_a, x_a, x_b),
                jnp.where(use_a, z_a, z_b),
            )

            @pl.when(c == me)
            def _():
                mine[at * 4] = stay
                mine[at * 4 + 1] = 32 + o
                mine[at * 4 + 2] = late
                mine[at * 4 + 3] = cost

        @pl.when(jnp.logical_not(direct))
        def _():
            @pl.when(jnp.logical_not(apart))
            def _():
                q = n_self[oa]

                @pl.when(q < 8)
                def _():
                    n_self[oa] = q + 1

                    @pl.when(oa == me)
                    def _():
                        at = 2 * (7 - q)
                        table_ref[POS + 2 * at + 2] = la
                        table_ref[POS + 2 * at + 3] = lb
                        table_ref[HOME + at] = la
                        table_ref[HOME + at + 1] = lb
                        table_ref[STEPS + at + 1] = cost
                        table_ref[MODE + 7 - q] = 1

                @pl.when(q >= 8)
                def _():
                    left_ref[d] = 1

            @pl.when(apart)
            def _():
                same_z = jnp.where(za == zb, 1, 0)

                def look(carry):
                    n, _ = carry
                    turn = ((d + n) & 3) * 8
                    c = jnp.where(n < 4, turn + za, jnp.where(n < 8, turn + zb, (d + n) & 31))
                    fit = ((n_direct[c] + 1) >> 1) + jnp.maximum(n_third[c] + 1, inside_ref[c]) <= 8
                    good = fit & can(oa, c, same_z) & can(ob, c, same_z) & (c != oa) & (c != ob)
                    return n + 1, jnp.where(good, c, -1)

                _, c = lax.while_loop(
                    lambda carry: (carry[0] < 40) & (carry[1] < 0), look, (jnp.int32(0), jnp.int32(-1))
                )

                @pl.when(c < 0)
                def _():
                    left_ref[d] = 1

                @pl.when(c >= 0)
                def _():
                    t = n_third[c]
                    n_third[c] = t + 1
                    split = jnp.maximum(t + 1, inside_ref[c])
                    n_split[c] = split
                    room[c] = ((n_direct[c] + 2) >> 1) + split
                    xc, zc = c >> 3, c & 7
                    x_at, z_at = oa * 4 + xc, xc * 64 + za * 8 + zc
                    late_a = send(oa, la, c, x_at, z_at, to_x[x_at], to_z[z_at])
                    x_at, z_at = ob * 4 + xc, xc * 64 + zb * 8 + zc
                    late_b = send(ob, lb, c, x_at, z_at, to_x[x_at], to_z[z_at])

                    @pl.when(c == me)
                    def _():
                        at = 2 * (7 - t)
                        table_ref[POS + 2 * at] = 32 + oa
                        table_ref[POS + 2 * at + 1] = 32 + ob
                        table_ref[LATE + at] = late_a
                        table_ref[LATE + at + 1] = late_b
                        table_ref[STEPS + at] = cost
                        table_ref[MODE + 7 - t] = 1

    loop(count_ref[0], visit)
    devices = 8 - jnp.maximum(n_third[me], n_self[me])

    def settle(n):
        second = n >= devices
        at = 2 * jnp.where(second, n - devices, n) + jnp.where(second, 1, 0)
        table_ref[POS + 2 * at] = mine[n * 4]
        table_ref[POS + 2 * at + 1] = mine[n * 4 + 1]
        table_ref[HOME + at] = mine[n * 4]
        table_ref[LATE + at] = mine[n * 4 + 2]
        table_ref[STEPS + at] = mine[n * 4 + 3]

    loop(n_direct[me], settle)


def plan_rest(me, inside_count, count, words):
    s32 = jnp.int32
    return pl.pallas_call(
        plan_kernel,
        out_shape=[jax.ShapeDtypeStruct((TABLE,), s32), jax.ShapeDtypeStruct(words.shape, s32)],
        in_specs=[SMEM] * 4,
        out_specs=[SMEM] * 2,
        scratch_shapes=[pltpu.SMEM((128,), s32), pltpu.SMEM((256,), s32)] + [pltpu.SMEM((32,), s32)] * 6 + [pltpu.SMEM((64,), s32)],
        name="plan",
        cost_estimate=pl.CostEstimate(flops=1000, bytes_accessed=30_000_000, transcendentals=0),
    )(me, inside_count, count, words)


def exchange(parts):
    got = [parts[0]]
    for k in range(1, 8):
        got.append(lax.ppermute(parts[k], "basis", [(i, i ^ k) for i in range(8)]))
    return got


def give_back(done):
    return lax.all_to_all(done, "basis", split_axis=0, concat_axis=0, tiled=True).reshape(-1, 72, 128)


def along_x(parts):
    return [lax.ppermute(parts[k - 1], "frag", [(i, i ^ (8 * k)) for i in range(32)]) for k in (1, 2, 3)]


def along_z(part):
    groups = [[8 * x + z for z in range(8)] for x in range(4)]
    return lax.all_to_all(part, "frag", 0, 0, tiled=True, axis_index_groups=groups)


def across(part):
    return lax.all_to_all(part, "frag", split_axis=0, concat_axis=0, tiled=True)


def after(value, *others):
    return lax.optimization_barrier((value, others))[0]


def shards(density, aux_factor, pairs, slot_of, costs):
    n_frag = lax.axis_size("frag")
    n_basis = lax.axis_size("basis")
    me_frag = lax.axis_index("frag").astype(jnp.int32)
    me_basis = lax.axis_index("basis").astype(jnp.int32)
    dimers = pairs.shape[0] * n_frag * n_basis

    lookup = pairs[:, :, None] == jnp.arange(slot_of.shape[0], dtype=jnp.int32)
    slots = jnp.sum(jnp.where(lookup, slot_of, 0), axis=2)
    mine = jnp.concatenate([slots[:, 0], slots[:, 1], costs, jnp.zeros(116, jnp.int32)])
    column = lax.all_to_all(
        jnp.broadcast_to(mine, (n_basis, 1, 128)), "basis", split_axis=0, concat_axis=0, tiled=True
    )
    column = column[:, 0, 0:12].reshape(n_basis, 3, 4).transpose(1, 0, 2).reshape(96)
    column = jnp.concatenate([column, jnp.zeros(32, jnp.int32)])
    every = across(jnp.broadcast_to(column, (n_frag, 1, 128)))
    a = every[:, 0, 0:32].reshape(dimers)
    b = every[:, 0, 32:64].reshape(dimers)
    cost = every[:, 0, 64:96].reshape(dimers)

    order = jnp.arange(dimers, dtype=jnp.int32)
    columns = jnp.arange(n_frag, dtype=jnp.int32)
    own_a, own_b = a // 32, b // 32
    low, high = jnp.minimum(own_a, own_b), jnp.maximum(own_a, own_b)
    pair_id = low * 32 + high
    inside = own_a == own_b
    mine_a = (own_a == me_frag) & jnp.logical_not(inside)
    mine_b = (own_b == me_frag) & jnp.logical_not(inside)
    other = jnp.where(mine_a, own_b, jnp.where(mine_b, own_a, -1))
    local = jnp.where(mine_a, a, b) & 31
    key = order * 256 + local * 8 + cost
    word = a + b * 1024 + cost * 1048576
    me_f, me_b = me_frag.reshape(1), me_basis.reshape(1)
    keep_first = (me_frag < columns) == ((me_frag + columns) % 2 == 0)
    home = (aux_factor, density)

    def one_round(carry):
        return body_round(carry)

    def body_round(carry):
        _, rest, dens, emb = carry
        open_dimer = rest > 0
        match = (other[None, :] == columns[:, None]) & open_dimer[None, :]
        keyed = jnp.where(match, key[None, :], BIG)
        key_0 = jnp.min(keyed, axis=1)
        key_1 = jnp.min(jnp.where(keyed > key_0[:, None], keyed, BIG), axis=1)
        here = jnp.where(keep_first, key_0, key_1)
        there = jnp.where(keep_first, key_1, key_0)
        send_1 = jnp.where(there < BIG, (there >> 3) & 31, -1)
        base_1 = jnp.where(here < BIG, (here >> 3) & 31, -1)
        steps_1 = jnp.where(here < BIG, here & 7, 0)

        (out_1,) = pack((send_1,), me_b, lambda t, me, n, row: t[0][row], 1, 32, home, [])
        in_1 = across(out_1)

        weight = steps_1 * 64 - columns
        rank = jnp.sum((weight[None, :] > weight[:, None]).astype(jnp.int32), axis=1)
        ranked = jnp.sum(jnp.where(rank[None, :] == columns[:, None], columns[None, :], 0), axis=1)
        table_1 = jnp.concatenate([send_1, base_1, steps_1, ranked])

        earlier = (pair_id[:, None] == pair_id[None, :]) & (order[None, :] < order[:, None])
        earlier = jnp.sum(jnp.where(earlier & open_dimer[None, :], 1, 0), axis=1)
        flagged = open_dimer & ((earlier >= 2) | inside)
        ahead = jnp.sum(jnp.where((order[None, :] < order[:, None]) & flagged[None, :], 1, 0), axis=1)
        ahead = jnp.where(flagged, ahead, -1)
        words = jnp.sum(jnp.where(ahead[None, :] == order[:, None], word[None, :], 0), axis=1)
        count = jnp.sum(jnp.where(flagged, 1, 0)).reshape(1)
        inside_here = (own_a[None, :] == columns[:, None]) & (inside & open_dimer)[None, :]
        inside_count = jnp.sum(jnp.where(inside_here, 1, 0), axis=1)
        table_2, listed = plan_rest(me_f, inside_count, count, words)
        listed = jnp.where(order < count, listed, 0)
        left = jnp.sum(jnp.where(ahead[:, None] == order[None, :], listed[None, :], 0), axis=1)
        tables = (table_1, table_2)

        def served(t, me, n, row):
            return t[0][RANKED + ranked_at(lax.bitwise_xor(me, n), row)]

        home_1 = exchange(
            pack(tables[:1], me_b, lambda t, me, n, row: t[0][BASE + served(t, me, n, row)], 8, 4, home, [])
        )
        in_x = along_x(pack(tables, me_b, lambda t, me, n, row: t[1][SENT + n * KX + row], 3, KX, home, []))

        def home_at(t, me, n, row):
            return t[1][HOME + 2 * lax.bitwise_xor(me, n) + row]

        home_2 = exchange(pack(tables, me_b, home_at, 8, 2, home, []))
        parts_1 = pack(tables, me_b, served, 8, 4, (), [in_1])
        away_1 = exchange(parts_1)
        (out_2,) = pack(
            tables, me_b, lambda t, me, n, row: t[1][RELAY + row], 1, NZ, home, after(in_x, parts_1)
        )
        in_z = along_z(out_2)

        one = lambda i, *_: (i, 0, 0)
        (ready_1,) = run_dimers(kernel_1, 4, (table_1, me_b), (1, 1), (one, one), [*home_1, *away_1])
        done_1 = give_back(after(ready_1, in_z))

        def late_at(t, me, n, row):
            return t[1][LATE + 2 * lax.bitwise_xor(me, n) + row] - 32

        late_parts = pack(tables, me_b, late_at, 8, 2, (), [*in_x, after(in_z, away_1)])
        late_2 = exchange(late_parts)
        whole = lambda i, *_: (0, 0, 0)
        ready_2 = run_dimers(kernel_2, 2, (table_2, me_b), (2, 2), (whole, whole), [*home_2, *late_2], True)

        def place_1(t, row):
            return t[0][RANKED + ranked_at(row // 8, row % 8 // 2)]

        def place_2(k):
            def find(t, me, row):
                at = 2 * lax.bitwise_xor(me, k) + row // 2
                return jnp.where(t[1][STEPS + at] > 0, t[1][POS + 2 * at + row % 2], -1)

            return find

        def owner_2(k):
            return lambda t, me, row: place_2(k)(t, me, row) - 32

        (ret_1,) = place(
            tables, me_b, [done_1], [lambda t, me, row: jnp.where(row % 2 == 1, place_1(t, row), -1)], [32]
        )
        back_1 = across(ret_1)
        done_2 = exchange(ready_2)
        (ret_2,) = place(tables, me_b, done_2, [owner_2(k) for k in range(8)], [32])
        back_2 = across(after(ret_2, back_1))
        finds = [
            lambda t, me, row: jnp.where(row % 2 == 0, t[0][BASE + place_1(t, row)], -1),
            *[place_2(k) for k in range(8)],
            lambda t, me, row: t[0][OUT + row],
        ]
        dens, emb = add_up(tables, me_b, [done_1, *done_2, back_1], finds, dens, emb)
        dens, emb = add_up(tables, me_b, [back_2], [lambda t, me, row: t[1][BACK + row]], dens, emb)
        return jnp.sum(left), left, dens, emb

    start = (
        jnp.int32(dimers),
        jnp.ones(dimers, jnp.int32),
        jnp.zeros(density.shape, F32),
        jnp.zeros((density.shape[0], aux_factor.shape[2]), F32),
    )
    _, _, dens, emb = lax.while_loop(lambda carry: carry[0] > 0, one_round, start)
    return dens, emb


def solution(mesh):
    return jax.shard_map(
        shards,
        mesh=mesh,
        in_specs=(
            P("frag", "basis", None),
            P("frag", None, "basis"),
            P(("frag", "basis"), None),
            P(),
            P(("frag", "basis")),
        ),
        out_specs=(P("frag", "basis", None), P("frag", "basis")),
        check_vma=False,
    )
```

```python
import jax
import jax.numpy as jnp
from jax import lax
from jax.experimental import pallas as pl
from jax.experimental.pallas import tpu as pltpu
from jax.sharding import PartitionSpec as P


COUPLE = 0.015625
BIG = 1 << 30
BF16 = jnp.bfloat16
F32 = jnp.float32
KX, KZ = 6, 2
NX, NZ = 3 * KX, 8 * KZ
SENT, RELAY, POS, BACK, HOME, LATE, STEPS, MODE, TABLE = 0, 32, 64, 96, 128, 160, 192, 224, 256
OUT, BASE, STEP1, RANKED = 0, 32, 64, 96

VMEM = pl.BlockSpec(memory_space=pltpu.VMEM)
SMEM = pl.BlockSpec(memory_space=pltpu.SMEM)


def loop(count, body):
    def step(n, unused):
        body(n)
        return unused

    lax.fori_loop(0, count, step, 0)


def ranked_at(device, place):
    return place * 8 + jnp.where(place % 2 == 0, device, 7 - device)


def pack(tables, me, find, outs, rows, home, items):
    sizes = ([32] if home else []) + [item.shape[0] for item in items]

    def kernel(*refs):
        table_refs, me_ref, refs = refs[: len(tables)], refs[len(tables)], refs[len(tables) + 1 :]
        sources, out_refs = refs[: len(refs) - outs], refs[len(refs) - outs :]
        for n, out_ref in enumerate(out_refs):

            def body(row, n=n, out_ref=out_ref):
                at = jnp.maximum(find(table_refs, me_ref[0], n, row), 0)
                base, left = 0, list(sources)
                for which, size in enumerate(sizes):
                    here = (at >= base) & (at < base + size)
                    if home and which == 0:
                        aux_ref, den_ref = left.pop(0), left.pop(0)

                        @pl.when(here)
                        def _(aux_ref=aux_ref, den_ref=den_ref):
                            out_ref[row, 0:256, :] = aux_ref[at]
                            block = den_ref[at]
                            out_ref[row, 256:288, :] = block[:, 0:128]
                            out_ref[row, 288:320, :] = block[:, 128:256]
                    else:
                        item_ref = left.pop(0)

                        @pl.when(here)
                        def _(item_ref=item_ref, base=base):
                            out_ref[row] = item_ref[at - base]

                    base += size

            loop(rows, body)

    sources = list(home) + list(items)
    return pl.pallas_call(
        kernel,
        out_shape=[jax.ShapeDtypeStruct((rows, 320, 128), BF16)] * outs,
        in_specs=[SMEM] * (len(tables) + 1) + [VMEM] * len(sources),
        out_specs=[VMEM] * outs,
        name="pack",
    )(*tables, me, *sources)


def place(tables, me, parts, finds, out_rows):
    def kernel(*refs):
        table_refs, me_ref, refs = refs[: len(tables)], refs[len(tables)], refs[len(tables) + 1 :]
        for part_ref, find in zip(refs[: len(parts)], finds, strict=True):

            def body(row, part_ref=part_ref, find=find):
                at = find(table_refs, me_ref[0], row)
                base = 0
                for out_ref, size in zip(refs[len(parts) :], out_rows, strict=True):

                    @pl.when((at >= base) & (at < base + size))
                    def _(out_ref=out_ref, base=base):
                        out_ref[at - base] = part_ref[row]

                    base += size

            loop(part_ref.shape[0], body)

    return pl.pallas_call(
        kernel,
        out_shape=[jax.ShapeDtypeStruct((size, 72, 128), BF16) for size in out_rows],
        in_specs=[SMEM] * (len(tables) + 1) + [VMEM] * len(parts),
        out_specs=[VMEM] * len(out_rows),
        name="place",
    )(*tables, me, *parts)


def add_up(tables, me, parts, finds, dens, emb):
    def kernel(*refs):
        table_refs, me_ref, refs = refs[: len(tables)], refs[len(tables)], refs[len(tables) + 1 :]
        dens_in, emb_in, dens_ref, emb_ref = refs[len(parts) :]
        dens_ref[...] = dens_in[...]
        emb_ref[...] = emb_in[...]
        for part_ref, find in zip(refs[: len(parts)], finds, strict=True):

            def body(row, part_ref=part_ref, find=find):
                slot = find(table_refs, me_ref[0], row)

                @pl.when((slot >= 0) & (slot < 32))
                def _():
                    dens_ref[slot, :, 0:128] += part_ref[row, 0:32, :].astype(F32)
                    dens_ref[slot, :, 128:256] += part_ref[row, 32:64, :].astype(F32)
                    emb_ref[pl.ds(slot, 1), :] += part_ref[row, 64:72, :].astype(F32)[0:1, :]

            loop(part_ref.shape[0], body)

    first = len(tables) + 1 + len(parts)
    return pl.pallas_call(
        kernel,
        out_shape=[jax.ShapeDtypeStruct(dens.shape, F32), jax.ShapeDtypeStruct(emb.shape, F32)],
        in_specs=[SMEM] * (len(tables) + 1) + [VMEM] * (len(parts) + 2),
        out_specs=[VMEM, VMEM],
        input_output_aliases={first: 0, first + 1: 1},
        name="add_up",
    )(*tables, me, *parts, dens, emb)


def take(half, me, parts, row, stacked, dens):
    for n in range(8):
        lanes = slice(n * 128, n * 128 + 128)
        at = pl.multiple_of(lax.bitwise_xor(me, n) * 32, 32)
        stacked[half : half + 256, lanes] = parts[n][row, 0:256, :]
        dens[pl.ds(half + at, 32), 0:128] = parts[n][row, 256:288, :]
        dens[pl.ds(half + at, 32), 128:256] = parts[n][row, 288:320, :]


def one_dimer(steps, me, load, out, scratch):
    stacked, weighted, dens, current = scratch

    @pl.when(steps > 0)
    def _():
        load()
        fits = []
        for half in (0, 256):
            block = dens[half : half + 256, :]
            sums = []
            for n in range(4):
                lanes = slice(n * 256, n * 256 + 256)
                factor = stacked[half : half + 256, lanes]
                projected = jnp.dot(block, factor, preferred_element_type=F32)
                sums.append(jnp.sum(factor.astype(F32) * projected, axis=0, keepdims=True))
            fits.append(jnp.concatenate(sums, axis=1).astype(BF16).astype(F32))
        coeff = fits[0] + fits[1]

        def weigh(n):
            rows = pl.ds(pl.multiple_of(n * 64, 64), 64)
            weighted[rows, :] = (stacked[rows, :].astype(F32) * coeff).astype(BF16)

        loop(8, weigh)
        coulomb = lax.dot_general(
            weighted[...], stacked[...], (((1,), (1,)), ((), ())), preferred_element_type=F32
        )
        row_at = lax.broadcasted_iota(jnp.int32, (256, 512), 0)
        col_at = lax.broadcasted_iota(jnp.int32, (256, 512), 1)
        blank = jnp.zeros((256, 256), F32)
        for half in (0, 256):
            own = dens[half : half + 256, :].astype(F32)
            wide = jnp.concatenate([own, blank] if half == 0 else [blank, own], axis=1)
            eye = jnp.where(row_at + half == col_at, 0.5, 0.0)
            current[half : half + 256, :] = (eye + wide + COUPLE * coulomb[half : half + 256, :]).astype(BF16)

        def purify(index, unused):
            whole = current[...]
            square = jnp.dot(whole, whole, preferred_element_type=F32)
            cube = jnp.dot(square.astype(BF16), whole, preferred_element_type=F32)
            current[...] = (3.0 * square - 2.0 * cube).astype(BF16)
            return unused

        lax.fori_loop(0, steps, purify, 0)
        row_at = lax.broadcasted_iota(jnp.int32, (256, 256), 0)
        col_at = lax.broadcasted_iota(jnp.int32, (256, 256), 1)
        eye = jnp.where(row_at == col_at, 0.5, 0.0)
        for half in (0, 256):
            own = slice(half, half + 256)
            change = current[own, own].astype(F32) - dens[own, :].astype(F32) - eye
            dens[own, :] = change.astype(BF16)
        for n in range(8):
            to = lax.bitwise_xor(me, n)
            at = pl.multiple_of(to * 32, 32)
            lanes = slice(n * 128, n * 128 + 128)
            for r in range(2):
                change = dens[pl.ds(r * 256 + at, 32), :]
                target = out[0].at[to, r] if len(out) == 1 else out[n].at[r]
                target[0:32, :] = change[:, 0:128]
                target[32:64, :] = change[:, 128:256]
                partner = jnp.broadcast_to(fits[1 - r][:, lanes], (8, 128))
                target[64:72, :] = partner.astype(BF16)


SCRATCH = [
    pltpu.VMEM((512, 1024), BF16),
    pltpu.VMEM((512, 1024), BF16),
    pltpu.VMEM((512, 256), BF16),
    pltpu.VMEM((512, 512), BF16),
]


def run_dimers(kernel, count, tables, blocks, maps, parts, apart=False):
    rows = 2 * count
    shapes = [(rows, 72, 128)] * 8 if apart else [(8, rows, 72, 128)]
    out_block = pl.BlockSpec((2, 72, 128), lambda i, *_: (i, 0, 0))
    if not apart:
        out_block = pl.BlockSpec((8, 2, 72, 128), lambda i, *_: (0, i, 0, 0))
    specs = []
    for block, index_map in zip(blocks, maps, strict=True):
        specs += [pl.BlockSpec((block, 320, 128), index_map)] * 8
    return pl.pallas_call(
        kernel,
        out_shape=[jax.ShapeDtypeStruct(shape, BF16) for shape in shapes],
        grid_spec=pltpu.PrefetchScalarGridSpec(
            num_scalar_prefetch=2,
            grid=(count,),
            in_specs=specs,
            out_specs=[out_block] * len(shapes),
            scratch_shapes=SCRATCH,
        ),
        name="dimers",
        cost_estimate=pl.CostEstimate(
            flops=count * 4_000_000_000, bytes_accessed=count * 1_500_000, transcendentals=0
        ),
    )(*tables, *parts)


def kernel_1(table_ref, me_ref, *refs):
    me, i = me_ref[0], pl.program_id(0)
    first, second, out, scratch = refs[0:8], refs[8:16], refs[16:17], refs[17:]
    stacked, dens = scratch[0], scratch[2]

    def load():
        take(0, me, first, 0, stacked, dens)
        take(256, me, second, 0, stacked, dens)

    other = table_ref[RANKED + ranked_at(me, i)]
    one_dimer(table_ref[STEP1 + other], me, load, out, scratch)


def kernel_2(table_ref, me_ref, *refs):
    me, i = me_ref[0], pl.program_id(0)
    home, late, out, scratch = refs[0:8], refs[8:16], refs[16:24], refs[24:]
    stacked, dens = scratch[0], scratch[2]
    split = table_ref[MODE + me] > 0

    def load():
        both_late = split & (i == 0)
        both_home = split & (i == 1)

        @pl.when(both_late)
        def _():
            take(0, me, late, 0, stacked, dens)

        @pl.when(jnp.logical_not(both_late))
        def _():
            take(0, me, home, jnp.where(split, 0, i), stacked, dens)

        @pl.when(both_home)
        def _():
            take(256, me, home, 1, stacked, dens)

        @pl.when(jnp.logical_not(both_home))
        def _():
            take(256, me, late, jnp.where(split, 1, i), stacked, dens)

    one_dimer(table_ref[STEPS + 2 * me + i], me, load, out, scratch)


def plan_kernel(me_ref, inside_ref, count_ref, list_ref, table_ref, left_ref, to_x, to_z, n_direct, n_third, n_self, n_split, n_next, room, taken, mine):
    me = me_ref[0]
    me_x, me_z = me >> 3, me & 7

    def clear(n):
        for i in range(8):
            to_z[n * 8 + i] = 0
            table_ref[n * 8 + i] = jnp.where(n < STEPS // 8, -1, 0)

    def clear_x(n):
        for i in range(8):
            to_x[n * 8 + i] = 0

    def clear_c(n):
        n_direct[n] = 0
        n_third[n] = 0
        n_self[n] = 0
        n_split[n] = inside_ref[n]
        n_next[n] = jnp.maximum(1, inside_ref[n])
        room[n] = 1 + inside_ref[n]
        taken[n] = 0

    loop(TABLE // 8, clear)
    loop(16, clear_x)
    loop(32, clear_c)

    def put(at, good, spare, value):
        table_ref[jnp.where(good, at, spare)] = value

    def can(o, c, extra):
        zo, xc, zc = o & 7, c >> 3, c & 7
        free = ((taken[c] >> o) & 1) == 0
        return free & (to_x[o * 4 + xc] < KX) & ((zo == zc) | (to_z[xc * 64 + zo * 8 + zc] + extra < KZ))

    def send(o, slot, c, at_x, at_z, n_x, n_z):
        xo, zo, xc, zc = o >> 3, o & 7, c >> 3, c & 7
        move_x, move_z = xo != xc, zo != zc
        taken[c] = taken[c] | lax.shift_left(jnp.int32(1), o)
        to_x[at_x] = n_x + jnp.where(move_x, 1, 0)
        to_z[at_z] = n_z + jnp.where(move_z, 1, 0)
        in_x = (lax.bitwise_xor(xo, xc) - 1) * KX + n_x

        @pl.when(zo == me_z)
        def _():
            put(SENT + in_x, move_x & (o == me), SENT + 31, slot)
            put(BACK + c, o == me, SENT + 31, slot)
            put(RELAY + zc * KZ + n_z, move_z & (xc == me_x), RELAY + 31, jnp.where(move_x, 32 + in_x, slot))

        return jnp.where(move_z, 32 + NX + zo * KZ + n_z, 32 + in_x)

    def visit(d):
        word = list_ref[d]
        cost = word >> 20
        la, oa, lb, ob = word & 31, (word >> 5) & 31, (word >> 10) & 31, (word >> 15) & 31
        left_ref[d] = 0
        za, xa, zb, xb = oa & 7, oa >> 3, ob & 7, ob >> 3
        x_at_a, z_at_a = ob * 4 + xa, xa * 64 + zb * 8 + za
        x_at_b, z_at_b = oa * 4 + xb, xb * 64 + za * 8 + zb
        x_a, z_a, x_b, z_b = to_x[x_at_a], to_z[z_at_a], to_x[x_at_b], to_z[z_at_b]
        room_a, room_b = room[oa], room[ob]
        free_a, free_b = ((taken[oa] >> ob) & 1) == 0, ((taken[ob] >> oa) & 1) == 0
        can_a = free_a & (x_a < KX) & (z_a < KZ) & (room_a <= 8)
        can_b = free_b & (x_b < KX) & (z_b < KZ) & (room_b <= 8)
        use_a = can_a & (jnp.logical_not(can_b) | (z_a * 4 + room_a <= z_b * 4 + room_b))
        apart = oa != ob
        direct = apart & (can_a | can_b)

        @pl.when(direct)
        def _():
            c, o = jnp.where(use_a, oa, ob), jnp.where(use_a, ob, oa)
            stay, move = jnp.where(use_a, la, lb), jnp.where(use_a, lb, la)
            at = n_direct[c]
            n_direct[c] = at + 1
            room[c] = ((at + 3) >> 1) + n_split[c]
            late = send(
                o,
                move,
                c,
                jnp.where(use_a, x_at_a, x_at_b),
                jnp.where(use_a, z_at_a, z_at_b),
                jnp.where(use_a, x_a, x_b),
                jnp.where(use_a, z_a, z_b),
            )

            @pl.when(c == me)
            def _():
                mine[at * 4] = stay
                mine[at * 4 + 1] = 32 + o
                mine[at * 4 + 2] = late
                mine[at * 4 + 3] = cost

        @pl.when(jnp.logical_not(direct))
        def _():
            @pl.when(jnp.logical_not(apart))
            def _():
                q = n_self[oa]

                @pl.when(q < 8)
                def _():
                    n_self[oa] = q + 1

                    @pl.when(oa == me)
                    def _():
                        at = 2 * (7 - q)
                        table_ref[POS + 2 * at + 2] = la
                        table_ref[POS + 2 * at + 3] = lb
                        table_ref[HOME + at] = la
                        table_ref[HOME + at + 1] = lb
                        table_ref[STEPS + at + 1] = cost
                        table_ref[MODE + 7 - q] = 1

                @pl.when(q >= 8)
                def _():
                    left_ref[d] = 1

            @pl.when(apart)
            def _():
                same_z = jnp.where(za == zb, 1, 0)

                def look(carry):
                    n, found = carry
                    for i in (3, 2, 1, 0):
                        turn = ((d + i) & 3) * 8
                        c = jnp.where(n == 0, turn + za, jnp.where(n == 1, turn + zb, (d + 4 * n + i) & 31))
                        fit = ((n_direct[c] + 1) >> 1) + n_next[c] <= 8
                        good = fit & can(oa, c, same_z) & can(ob, c, same_z) & (c != oa) & (c != ob)
                        found = jnp.where(good, c, found)
                    return n + 1, found

                _, c = lax.while_loop(
                    lambda carry: (carry[0] < 10) & (carry[1] < 0), look, (jnp.int32(0), jnp.int32(-1))
                )

                @pl.when(c < 0)
                def _():
                    left_ref[d] = 1

                @pl.when(c >= 0)
                def _():
                    t = n_third[c]
                    n_third[c] = t + 1
                    split = jnp.maximum(t + 1, inside_ref[c])
                    n_split[c] = split
                    n_next[c] = jnp.maximum(t + 2, inside_ref[c])
                    room[c] = ((n_direct[c] + 2) >> 1) + split
                    xc, zc = c >> 3, c & 7
                    x_at, z_at = oa * 4 + xc, xc * 64 + za * 8 + zc
                    late_a = send(oa, la, c, x_at, z_at, to_x[x_at], to_z[z_at])
                    x_at, z_at = ob * 4 + xc, xc * 64 + zb * 8 + zc
                    late_b = send(ob, lb, c, x_at, z_at, to_x[x_at], to_z[z_at])

                    @pl.when(c == me)
                    def _():
                        at = 2 * (7 - t)
                        table_ref[POS + 2 * at] = 32 + oa
                        table_ref[POS + 2 * at + 1] = 32 + ob
                        table_ref[LATE + at] = late_a
                        table_ref[LATE + at + 1] = late_b
                        table_ref[STEPS + at] = cost
                        table_ref[MODE + 7 - t] = 1

    loop(count_ref[0], visit)
    devices = 8 - jnp.maximum(n_third[me], n_self[me])

    def settle(n):
        second = n >= devices
        at = 2 * jnp.where(second, n - devices, n) + jnp.where(second, 1, 0)
        table_ref[POS + 2 * at] = mine[n * 4]
        table_ref[POS + 2 * at + 1] = mine[n * 4 + 1]
        table_ref[HOME + at] = mine[n * 4]
        table_ref[LATE + at] = mine[n * 4 + 2]
        table_ref[STEPS + at] = mine[n * 4 + 3]

    loop(n_direct[me], settle)


def plan_rest(me, inside_count, count, words):
    s32 = jnp.int32
    return pl.pallas_call(
        plan_kernel,
        out_shape=[jax.ShapeDtypeStruct((TABLE,), s32), jax.ShapeDtypeStruct(words.shape, s32)],
        in_specs=[SMEM] * 4,
        out_specs=[SMEM] * 2,
        scratch_shapes=[pltpu.SMEM((128,), s32), pltpu.SMEM((256,), s32)] + [pltpu.SMEM((32,), s32)] * 7 + [pltpu.SMEM((64,), s32)],
        name="plan",
        cost_estimate=pl.CostEstimate(flops=1000, bytes_accessed=30_000_000, transcendentals=0),
    )(me, inside_count, count, words)


def exchange(parts):
    got = [parts[0]]
    for k in range(1, 8):
        got.append(lax.ppermute(parts[k], "basis", [(i, i ^ k) for i in range(8)]))
    return got


def give_back(done):
    return lax.all_to_all(done, "basis", split_axis=0, concat_axis=0, tiled=True).reshape(-1, 72, 128)


def along_x(parts):
    return [lax.ppermute(parts[k - 1], "frag", [(i, i ^ (8 * k)) for i in range(32)]) for k in (1, 2, 3)]


def along_z(part):
    groups = [[8 * x + z for z in range(8)] for x in range(4)]
    return lax.all_to_all(part, "frag", 0, 0, tiled=True, axis_index_groups=groups)


def across(part):
    return lax.all_to_all(part, "frag", split_axis=0, concat_axis=0, tiled=True)


def after(value, *others):
    return lax.optimization_barrier((value, others))[0]


def shards(density, aux_factor, pairs, slot_of, costs):
    n_frag = lax.axis_size("frag")
    n_basis = lax.axis_size("basis")
    me_frag = lax.axis_index("frag").astype(jnp.int32)
    me_basis = lax.axis_index("basis").astype(jnp.int32)
    dimers = pairs.shape[0] * n_frag * n_basis

    lookup = pairs[:, :, None] == jnp.arange(slot_of.shape[0], dtype=jnp.int32)
    slots = jnp.sum(jnp.where(lookup, slot_of, 0), axis=2)
    mine = jnp.concatenate([slots[:, 0], slots[:, 1], costs, jnp.zeros(116, jnp.int32)])
    column = lax.all_to_all(
        jnp.broadcast_to(mine, (n_basis, 1, 128)), "basis", split_axis=0, concat_axis=0, tiled=True
    )
    column = column[:, 0, 0:12].reshape(n_basis, 3, 4).transpose(1, 0, 2).reshape(96)
    column = jnp.concatenate([column, jnp.zeros(32, jnp.int32)])
    every = across(jnp.broadcast_to(column, (n_frag, 1, 128)))
    a = every[:, 0, 0:32].reshape(dimers)
    b = every[:, 0, 32:64].reshape(dimers)
    cost = every[:, 0, 64:96].reshape(dimers)

    order = jnp.arange(dimers, dtype=jnp.int32)
    columns = jnp.arange(n_frag, dtype=jnp.int32)
    own_a, own_b = a // 32, b // 32
    low, high = jnp.minimum(own_a, own_b), jnp.maximum(own_a, own_b)
    pair_id = low * 32 + high
    inside = own_a == own_b
    mine_a = (own_a == me_frag) & jnp.logical_not(inside)
    mine_b = (own_b == me_frag) & jnp.logical_not(inside)
    other = jnp.where(mine_a, own_b, jnp.where(mine_b, own_a, -1))
    local = jnp.where(mine_a, a, b) & 31
    key = order * 256 + local * 8 + cost
    word = a + b * 1024 + cost * 1048576
    me_f, me_b = me_frag.reshape(1), me_basis.reshape(1)
    keep_first = (me_frag < columns) == ((me_frag + columns) % 2 == 0)
    home = (aux_factor, density)

    def one_round(carry):
        return body_round(carry)

    def body_round(carry):
        _, rest, dens, emb = carry
        open_dimer = rest > 0
        match = (other[None, :] == columns[:, None]) & open_dimer[None, :]
        keyed = jnp.where(match, key[None, :], BIG)
        key_0 = jnp.min(keyed, axis=1)
        key_1 = jnp.min(jnp.where(keyed > key_0[:, None], keyed, BIG), axis=1)
        here = jnp.where(keep_first, key_0, key_1)
        there = jnp.where(keep_first, key_1, key_0)
        send_1 = jnp.where(there < BIG, (there >> 3) & 31, -1)
        base_1 = jnp.where(here < BIG, (here >> 3) & 31, -1)
        steps_1 = jnp.where(here < BIG, here & 7, 0)

        (out_1,) = pack((send_1,), me_b, lambda t, me, n, row: t[0][row], 1, 32, home, [])
        in_1 = across(out_1)

        weight = steps_1 * 64 - columns
        rank = jnp.sum((weight[None, :] > weight[:, None]).astype(jnp.int32), axis=1)
        ranked = jnp.sum(jnp.where(rank[None, :] == columns[:, None], columns[None, :], 0), axis=1)
        table_1 = jnp.concatenate([send_1, base_1, steps_1, ranked])

        earlier = (pair_id[:, None] == pair_id[None, :]) & (order[None, :] < order[:, None])
        earlier = jnp.sum(jnp.where(earlier & open_dimer[None, :], 1, 0), axis=1)
        flagged = open_dimer & ((earlier >= 2) | inside)
        late_turn = jnp.where(inside | (earlier == 2), 2, jnp.where(earlier == 3, 0, 1))
        turn = order + dimers * late_turn
        ahead = jnp.sum(jnp.where((turn[None, :] < turn[:, None]) & flagged[None, :], 1, 0), axis=1)
        ahead = jnp.where(flagged, ahead, -1)
        words = jnp.sum(jnp.where(ahead[None, :] == order[:, None], word[None, :], 0), axis=1)
        count = jnp.sum(jnp.where(flagged, 1, 0)).reshape(1)
        inside_here = (own_a[None, :] == columns[:, None]) & (inside & open_dimer)[None, :]
        inside_count = jnp.sum(jnp.where(inside_here, 1, 0), axis=1)
        table_2, listed = plan_rest(me_f, inside_count, count, words)
        listed = jnp.where(order < count, listed, 0)
        left = jnp.sum(jnp.where(ahead[:, None] == order[None, :], listed[None, :], 0), axis=1)
        tables = (table_1, table_2)

        def served(t, me, n, row):
            return t[0][RANKED + ranked_at(lax.bitwise_xor(me, n), row)]

        home_1 = exchange(
            pack(tables[:1], me_b, lambda t, me, n, row: t[0][BASE + served(t, me, n, row)], 8, 4, home, [])
        )
        in_x = along_x(pack(tables, me_b, lambda t, me, n, row: t[1][SENT + n * KX + row], 3, KX, home, []))

        def home_at(t, me, n, row):
            return t[1][HOME + 2 * lax.bitwise_xor(me, n) + row]

        home_2 = exchange(pack(tables, me_b, home_at, 8, 2, home, []))
        parts_1 = pack(tables, me_b, served, 8, 4, (), [in_1])
        away_1 = exchange(parts_1)
        (out_2,) = pack(
            tables, me_b, lambda t, me, n, row: t[1][RELAY + row], 1, NZ, home, after(in_x, parts_1)
        )
        in_z = along_z(out_2)

        one = lambda i, *_: (i, 0, 0)
        (ready_1,) = run_dimers(kernel_1, 4, (table_1, me_b), (1, 1), (one, one), [*home_1, *away_1])
        done_1 = give_back(after(ready_1, in_z))

        def late_at(t, me, n, row):
            return t[1][LATE + 2 * lax.bitwise_xor(me, n) + row] - 32

        late_parts = pack(tables, me_b, late_at, 8, 2, (), [*in_x, after(in_z, away_1)])
        late_2 = exchange(late_parts)
        whole = lambda i, *_: (0, 0, 0)
        ready_2 = run_dimers(kernel_2, 2, (table_2, me_b), (2, 2), (whole, whole), [*home_2, *late_2], True)

        def place_1(t, row):
            return t[0][RANKED + ranked_at(row // 8, row % 8 // 2)]

        def place_2(k):
            def find(t, me, row):
                at = 2 * lax.bitwise_xor(me, k) + row // 2
                return jnp.where(t[1][STEPS + at] > 0, t[1][POS + 2 * at + row % 2], -1)

            return find

        def owner_2(k):
            return lambda t, me, row: place_2(k)(t, me, row) - 32

        (ret_1,) = place(
            tables, me_b, [done_1], [lambda t, me, row: jnp.where(row % 2 == 1, place_1(t, row), -1)], [32]
        )
        back_1 = across(ret_1)
        done_2 = exchange(ready_2)
        (ret_2,) = place(tables, me_b, done_2, [owner_2(k) for k in range(8)], [32])
        back_2 = across(after(ret_2, back_1))
        finds = [
            lambda t, me, row: jnp.where(row % 2 == 0, t[0][BASE + place_1(t, row)], -1),
            *[place_2(k) for k in range(8)],
            lambda t, me, row: t[0][OUT + row],
        ]
        dens, emb = add_up(tables, me_b, [done_1, *done_2, back_1], finds, dens, emb)
        dens, emb = add_up(tables, me_b, [back_2], [lambda t, me, row: t[1][BACK + row]], dens, emb)
        return jnp.sum(left), left, dens, emb

    start = (
        jnp.int32(dimers),
        jnp.ones(dimers, jnp.int32),
        jnp.zeros(density.shape, F32),
        jnp.zeros((density.shape[0], aux_factor.shape[2]), F32),
    )
    _, _, dens, emb = lax.while_loop(lambda carry: carry[0] > 0, one_round, start)
    return dens, emb


def solution(mesh):
    return jax.shard_map(
        shards,
        mesh=mesh,
        in_specs=(
            P("frag", "basis", None),
            P("frag", None, "basis"),
            P(("frag", "basis"), None),
            P(),
            P(("frag", "basis")),
        ),
        out_specs=(P("frag", "basis", None), P("frag", "basis")),
        check_vma=False,
    )
```
